32 devices in a mesh: dp: 8 (over z, y), mp: 4 (over x, core).
Axes of the slice: x: 2, y: 2, z: 4, core: 2. Of those that a mesh axis runs over, the one named last changes fastest.
Arguments:
- block_input: bfloat16 [8, 2048, 1024], P('dp'), may hold values from -6 to 6
- segment_ids: int32 [8, 2048], P('dp'), may hold values from 0 to 7, never falling along the last dimension, each value on 1 to 1024 neighbouring positions
- cotangent: bfloat16 [8, 2048, 1024], P('dp'), may hold values from -6 to 6
- weight_qkv: bfloat16 [1024, 3072], P(None, 'mp')
- bias_qkv: bfloat16 [3072], P('mp'), may hold values from -1.75 to 1.75
- weight_out: bfloat16 [1024, 1024], P('mp'), may hold values from -3 to 3
- bias_out: bfloat16 [1024], replicated, may hold values from -1.75 to 1.75
- weight_up: bfloat16 [1024, 4096], P(None, 'mp')
- bias_up: bfloat16 [4096], P('mp'), may hold values from -3 to 3
- weight_down: bfloat16 [4096, 1024], P('mp'), may hold values from -0.09375 to 0.09375
- bias_down: bfloat16 [1024], replicated, may hold values from -1.75 to 1.75
- gain_first: bfloat16 [1024], replicated, may hold values from 0.25 to 1.75
- shift_first: bfloat16 [1024], replicated, may hold values from -0.05 to 0.05
- gain_second: bfloat16 [1024], replicated, may hold values from 0.25 to 1.75
- shift_second: bfloat16 [1024], replicated, may hold values from -0.05 to 0.05
Outputs:
- block_output: bfloat16 [8, 2048, 1024], P('dp', 'mp')
- grad_input: float32 [8, 2048, 1024], P('dp', 'mp')
- grad_weight_qkv: float32 [1024, 3072], P('dp', 'mp')
- grad_bias_qkv: float32 [3072], P('mp')
- grad_weight_out: float32 [1024, 1024], P('mp', 'dp')
- grad_bias_out: float32 [1024], replicated
- grad_weight_up: float32 [1024, 4096], P('dp', 'mp')
- grad_bias_up: float32 [4096], P('mp')
- grad_weight_down: float32 [4096, 1024], P('mp', 'dp')
- grad_bias_down: float32 [1024], replicated
- grad_gain_first: float32 [1024], replicated
- grad_shift_first: float32 [1024], replicated
- grad_gain_second: float32 [1024], replicated
- grad_shift_second: float32 [1024], replicated
- doc_norms: float32 [8, 8], P('dp')
The draws below stay inside these ranges and needn't reach their ends.
Inputs may be any that keep to these rules, and one draw needn't show every extreme that they name: `segment_ids`: in each row the numbers 0 to 7 appear in order, each on 1 to 1024 consecutive tokens, and one document has exactly 1024 tokens.
All inputs are finite; a program needn't handle non-finite values.
Results may differ from the reference program's by a relative error of at most 0.005.
The reference program's roundings to bfloat16 on the way count: a program that leaves them out, or rounds other values in their place, can miss the bound.
Values may be sent and summed in bfloat16 or wider, within the bound.
A program may use at most 256 MiB of HBM per device.

```python
import math
import jax
import jax.numpy as jnp
import numpy as np
from jax import lax

D = 1024
HEADS = 16
HD = 64
FF = 4096
ROT = 16
SEQ = 2048
DOCS = 8
DOC_MOST = 1024
ROWS = 8


def ramp_weight(key, salt, rows_in, cols_out):
    noise_key = jax.random.fold_in(key, salt + 11)
    scale_key = jax.random.fold_in(key, salt + 23)
    base_noise = jax.random.truncated_normal(noise_key, -4.0, 4.0, (rows_in, cols_out), jnp.float32)
    column_pos = lax.broadcasted_iota(jnp.float32, (1, cols_out), 1) / max(cols_out - 1, 1)
    jitter_scale = jnp.exp(jax.random.uniform(scale_key, (1, cols_out), jnp.float32, -0.35, 0.35))
    column_scale = 0.6 * jnp.exp(column_pos * math.log(3.0)) * jitter_scale
    return (base_noise * column_scale / math.sqrt(rows_in)).astype(jnp.bfloat16)


def small_shift(key, salt):
    shift_key = jax.random.fold_in(key, salt)
    values_out = 0.02 * jax.random.truncated_normal(shift_key, -2.5, 2.5, (D,), jnp.float32)
    return values_out.astype(jnp.bfloat16)


def draw_weight_qkv(key, part):
    return ramp_weight(key, 100, D, 3 * D)


def draw_weight_up(key, part):
    return ramp_weight(key, 200, D, FF)


def draw_shift_first(key, part):
    return small_shift(key, 331)


def draw_shift_second(key, part):
    return small_shift(key, 337)


def strengthened(drawn, stream_key, source, target, blocks, factor):
    def block_of(dim):
        return (jnp.arange(drawn.shape[dim]) // (drawn.shape[dim] // blocks)).reshape((-1,) + (1,) * (drawn.ndim - 1 - dim))

    one_side = jax.random.permutation(stream_key, blocks)[block_of(target)]
    second = (block_of(target) + blocks // 2) % blocks
    return jnp.where((block_of(source) == one_side) | (block_of(source) == second), factor * drawn, drawn)


def level_of(key, shape, shards, least, high):
    def one(axis_at, shards_of):
        heights = jax.random.uniform(jax.random.fold_in(jax.random.fold_in(key, 6), axis_at), (shards_of,), jnp.float32, least / len(shards), high / len(shards))
        return jnp.repeat(jnp.exp(heights), shape[axis_at] // shards_of).reshape((-1,) + (1,) * (len(shape) - axis_at - 1))

    level = one(*shards[0])
    for cut in shards[1:]:
        level = level * one(*cut)
    return level


def length_profile(amount, total, reach, slope):
    portions = [(1 << 20) // math.isqrt(standing ** slope) + 1 for standing in range(2, amount + 1)]
    surplus, given = total - reach - (amount - 1), [1] * (amount - 1)
    while surplus > 0:
        free = [i for i in range(amount - 1) if given[i] < reach]
        pool, remaining = sum([portions[i] for i in free]), surplus
        for i in free:
            more = min(reach - given[i], max(1, remaining * portions[i] // pool), surplus)
            given[i] = given[i] + more
            surplus = surplus - more
    return np.array([reach] + given)


def uneven(key, count, total, limit, skew):
    if count == 2:
        one = jax.random.randint(key, (), max(1, total - limit), min(limit, total - 1) + 1)
        return jnp.stack([one, total - one])
    sizes = jnp.asarray(length_profile(count, total, limit, skew), jnp.int32)
    pairs = (count - 1) // 2
    source_of, receiver = sizes[1:1 + 2 * pairs:2], sizes[2:2 + 2 * pairs:2]
    margin = jnp.minimum(source_of - 1, limit - receiver)
    moved = jax.random.randint(jax.random.fold_in(key, 1), (pairs,), 0, 1 << 20) % (margin + 1)
    sizes = sizes.at[1:1 + 2 * pairs:2].set(source_of - moved).at[2:2 + 2 * pairs:2].set(receiver + moved)
    return sizes[jax.random.permutation(jax.random.fold_in(key, 2), count)]


def scatter_about(own_key, shape, width, bound, cuts=(), held_as=jnp.bfloat16):
    loudness = level_of(own_key, shape, cuts, -0.22, 0.18) if cuts else 1.0
    array = jax.random.normal(own_key, shape, jnp.float32) * width * loudness
    return jnp.minimum(jnp.maximum(array, -bound), bound).astype(held_as)


def heavy_noise(stream_key, shape, scale, limit, cuts, heavy, held_as=jnp.bfloat16):
    array = scale * jax.random.normal(stream_key, shape, jnp.float32)
    if cuts:
        array = array * level_of(stream_key, shape, cuts, -0.22, 0.18)
    return jnp.clip(strengthened(array, jax.random.fold_in(stream_key, 3), *heavy), -limit, limit).astype(held_as)


def setup_inputs(seed: int = 0) -> dict:
    key_list = jax.random.split(jax.random.key(seed), 16)
    return {
        "block_input": heavy_noise(key_list[0], (ROWS, SEQ, D), 1.0, 6.0, ((0, 8),), (0, 2, 8, 2.0)),
        "segment_ids": jax.vmap(lambda own: jnp.searchsorted(jnp.cumsum(uneven(own, DOCS, SEQ, DOC_MOST, 2)), jnp.arange(SEQ), side="right"))(jax.random.split(key_list[1], ROWS)).reshape((ROWS, SEQ)).astype(jnp.int32),
        "cotangent": heavy_noise(key_list[2], (ROWS, SEQ, D), 1.0, 6.0, ((0, 8),), (0, 2, 8, 2.0)),
        "weight_qkv": draw_weight_qkv(jax.random.fold_in(key_list[15], 71), 0),
        "bias_qkv": scatter_about(key_list[4], (3 * D,), 0.3, 1.75, ((0, 4),)),
        "weight_out": scatter_about(key_list[5], (D, D), (max(D // 256, 1)) ** -0.5, 3.0, ((0, 4),)),
        "bias_out": scatter_about(key_list[6], (D,), 0.3, 1.75),
        "weight_up": draw_weight_up(jax.random.fold_in(key_list[15], 71), 0),
        "bias_up": scatter_about(key_list[8], (FF,), 0.5, 3.0, ((0, 4),)),
        "weight_down": scatter_about(key_list[9], (FF, D), FF ** -0.5, 0.09375, ((0, 4),)),
        "bias_down": scatter_about(key_list[10], (D,), 0.3, 1.75),
        "gain_first": jnp.clip(1.0 + 0.15 * jax.random.normal(key_list[11], (D,), jnp.float32), 0.25, 1.75).astype(jnp.bfloat16),
        "shift_first": draw_shift_first(jax.random.fold_in(key_list[15], 71), 0),
        "gain_second": jnp.clip(1.0 + 0.15 * jax.random.normal(key_list[13], (D,), jnp.float32), 0.25, 1.75).astype(jnp.bfloat16),
        "shift_second": draw_shift_second(jax.random.fold_in(key_list[15], 71), 0),
    }


ln_eps = 1e-05
norm_eps = 1e-06
masked_score = -1e+30
highest = lax.Precision.HIGHEST

@jax.custom_vjp
def low(v):
    return lax.optimization_barrier(v.astype(jnp.bfloat16)).astype(jnp.float32)

@jax.custom_vjp
def low_back(v):
    return v

def low_keep(v):
    return (low(v), None)

def low_pass(kept, grad):
    return (grad,)

def back_keep(v):
    return (v, None)

def back_low(kept, grad):
    return (low(grad),)
low.defvjp(low_keep, low_pass)
low_back.defvjp(back_keep, back_low)

def layer_stats(flat_input):
    mean_value = lax.optimization_barrier(jnp.mean(flat_input, axis=-1, keepdims=True))
    centred = flat_input - mean_value
    variance = lax.optimization_barrier(jnp.mean(centred * centred, axis=-1, keepdims=True))
    inv_std = lax.rsqrt(variance + ln_eps)
    return (centred * inv_std, inv_std)

def doc_positions(segment_rows):
    token_index = lax.broadcasted_iota(jnp.int32, segment_rows.shape, 1)
    earlier = jnp.concatenate([segment_rows[:, :1] - 1, segment_rows[:, :-1]], axis=1)
    starts = jnp.where(segment_rows != earlier, token_index, 0)
    return token_index - lax.cummax(starts, axis=1)

def rotary_tables(position, rot_dims):
    half_dims = rot_dims // 2
    exponent = jnp.arange(half_dims, dtype=jnp.float32) * (2.0 / rot_dims)
    inv_freq = jnp.exp(exponent * -math.log(10000.0))
    angles = position.astype(jnp.float32)[..., None] * inv_freq
    return (jnp.cos(angles), jnp.sin(angles))

def rotate(tensor, cosine_table, sine_table, rot_dims):
    half_dims = rot_dims // 2
    first_half = tensor[..., :half_dims]
    second_half = tensor[..., half_dims:rot_dims]
    cos_part = cosine_table[..., None, :]
    sin_part = sine_table[..., None, :]
    return jnp.concatenate([first_half * cos_part - second_half * sin_part, second_half * cos_part + first_half * sin_part, tensor[..., rot_dims:]], axis=-1)

def head_attention(query, key_rows, value, allowed, score_scale):
    scores = jnp.dot(query, key_rows.T, precision=highest) * score_scale
    scores = low_back(jnp.where(allowed, scores, masked_score))
    probs = jax.nn.softmax(scores, axis=-1)
    return low_back(jnp.dot(low(probs), value, precision=highest))

def linear_grad(inputs_mat, weight, scaled):
    unused_value, pull_weight = jax.vjp(lambda matrix_in: jnp.dot(inputs_mat, matrix_in, precision=highest), weight)
    return pull_weight(low(scaled))[0]

def shift_grad(shift, scaled):
    unused_value, pull_shift = jax.vjp(lambda shift_in: jnp.broadcast_to(shift_in, scaled.shape), shift)
    return pull_shift(scaled)[0]

def reference(block_input, segment_ids, cotangent, weight_qkv, bias_qkv, weight_out, bias_out, weight_up, bias_up, weight_down, bias_down, gain_first, shift_first, gain_second, shift_second):
    qkv_matrix = weight_qkv.astype(jnp.float32)
    qkv_shift = bias_qkv.astype(jnp.float32)
    out_matrix = weight_out.astype(jnp.float32)
    out_shift = bias_out.astype(jnp.float32)
    up_matrix = weight_up.astype(jnp.float32)
    up_shift = bias_up.astype(jnp.float32)
    down_matrix = weight_down.astype(jnp.float32)
    down_shift = bias_down.astype(jnp.float32)
    gain_one = gain_first.astype(jnp.float32)
    shift_one = shift_first.astype(jnp.float32)
    gain_two = gain_second.astype(jnp.float32)
    shift_two = shift_second.astype(jnp.float32)
    score_scale = 1.0 / math.sqrt(HD)
    seq_index = jnp.arange(SEQ)
    causal = seq_index[None, :] <= seq_index[:, None]
    doc_index = jnp.arange(DOCS, dtype=jnp.int32)

    def row_step(carry, row_data):
        row_input, row_segments, row_cot = row_data
        flat_input = row_input.astype(jnp.float32)
        cot_value = row_cot.astype(jnp.float32)
        position = doc_positions(row_segments[None])[0]
        cosine_table, sine_table = rotary_tables(position, ROT)
        allowed = causal & (row_segments[:, None] == row_segments[None, :])

        def attend_head(head_triple):
            return head_attention(head_triple[0], head_triple[1], head_triple[2], allowed, score_scale)

        def forward(input_value, probe_first, probe_second, probe_qkv, probe_up):
            normed, inv_std = layer_stats(input_value)
            first_input = low(normed * gain_one + shift_one + probe_first)
            projected = low_back(jnp.dot(first_input, qkv_matrix, precision=highest) + qkv_shift + probe_qkv)
            projected = projected.reshape(SEQ, HEADS, 3, HD)
            queries = low(rotate(projected[:, :, 0], cosine_table, sine_table, ROT))
            keys_rot = low(rotate(projected[:, :, 1], cosine_table, sine_table, ROT))
            values = low(projected[:, :, 2])
            per_head = lax.map(jax.checkpoint(attend_head), (jnp.swapaxes(queries, 0, 1), jnp.swapaxes(keys_rot, 0, 1), jnp.swapaxes(values, 0, 1)))
            attended = low(jnp.swapaxes(per_head, 0, 1).reshape(SEQ, D))
            branch_attn = low_back(jnp.dot(attended, out_matrix, precision=highest) + out_shift)
            second_input = low(normed * gain_two + shift_two + probe_second)
            up_pre = low_back(jnp.dot(second_input, up_matrix, precision=highest) + up_shift + probe_up)
            activated = low(jax.nn.gelu(up_pre, approximate=False))
            branch_mlp = low_back(jnp.dot(activated, down_matrix, precision=highest) + down_shift)
            return (input_value + branch_attn + branch_mlp, (normed, first_input, attended, second_input, activated))
        zero_model = jnp.zeros((SEQ, D), jnp.float32)
        zero_qkv = jnp.zeros((SEQ, 3 * D), jnp.float32)
        zero_up = jnp.zeros((SEQ, FF), jnp.float32)
        row_output, pull_back, saved = jax.vjp(forward, flat_input, zero_model, zero_model, zero_qkv, zero_up, has_aux=True)
        grad_input, grad_first, grad_second, grad_proj, grad_up = pull_back(cot_value)
        normed, first_input, attended, second_input, activated = saved
        unused_norm, pull_first = jax.vjp(lambda gain_in, shift_in: normed * gain_in + shift_in, gain_one, shift_one)
        unused_second, pull_second = jax.vjp(lambda gain_in, shift_in: normed * gain_in + shift_in, gain_two, shift_two)

        def all_grads(weights_col, first_grad, proj_grad, dy_grad, up_grad, second_grad):
            proj_part = weights_col * proj_grad
            dy_part = weights_col * dy_grad
            up_part = weights_col * up_grad
            first_pair = pull_first(weights_col * first_grad)
            second_pair = pull_second(weights_col * second_grad)
            return (linear_grad(first_input, qkv_matrix, proj_part), shift_grad(qkv_shift, proj_part), linear_grad(attended, out_matrix, dy_part), shift_grad(out_shift, dy_part), linear_grad(second_input, up_matrix, up_part), shift_grad(up_shift, up_part), linear_grad(activated, down_matrix, dy_part), shift_grad(down_shift, dy_part), first_pair[0], first_pair[1], second_pair[0], second_pair[1])

        def doc_square(doc):
            mask_col = (row_segments == doc).astype(jnp.float32)[:, None]
            pieces = all_grads(mask_col, grad_first, grad_proj, cot_value, grad_up, grad_second)
            total = jnp.zeros((), jnp.float32)
            for piece in pieces:
                total = total + jnp.sum(piece * piece)
            return total
        norm_values = jnp.sqrt(lax.map(doc_square, doc_index) + norm_eps)
        clip_factor = jnp.minimum(1.0, jnp.mean(norm_values) / norm_values)
        token_clip = jnp.take(clip_factor, row_segments)[:, None]
        terms = all_grads(token_clip, grad_first, grad_proj, cot_value, grad_up, grad_second)
        new_carry = tuple((total + term for total, term in zip(carry, terms)))
        return (new_carry, (row_output.astype(jnp.bfloat16), grad_input, norm_values))
    start_carry = (jnp.zeros((D, 3 * D), jnp.float32), jnp.zeros((3 * D,), jnp.float32), jnp.zeros((D, D), jnp.float32), jnp.zeros((D,), jnp.float32), jnp.zeros((D, FF), jnp.float32), jnp.zeros((FF,), jnp.float32), jnp.zeros((FF, D), jnp.float32), jnp.zeros((D,), jnp.float32), jnp.zeros((D,), jnp.float32), jnp.zeros((D,), jnp.float32), jnp.zeros((D,), jnp.float32), jnp.zeros((D,), jnp.float32))
    sums, stacked_rows = lax.scan(row_step, start_carry, (block_input, segment_ids, cotangent))
    block_output, grad_input, doc_norms = stacked_rows
    return (block_output, grad_input, sums[0], sums[1], sums[2], sums[3], sums[4], sums[5], sums[6], sums[7], sums[8], sums[9], sums[10], sums[11], doc_norms)
```

```python
import functools
import math

import jax
import jax.numpy as jnp
from jax import lax
from jax.experimental import pallas as pl
from jax.experimental.pallas import tpu as pltpu
from jax.sharding import PartitionSpec as P

HD = 64
ROT = 16
DOCS = 8
BLK = 256
LN_EPS = 1e-05
NORM_EPS = 1e-06
NEG = -1e30
F32 = jnp.float32
BF16 = jnp.bfloat16
VMEM_LIMIT = 60 * 1024 * 1024

TAIL = (0.099163489, 0.109273513, 0.0348237317, 0.263242867, -0.249259412, 0.332377466, -0.089621649)


def dot_nn(a, b):
    return lax.dot_general(a, b, (((1,), (0,)), ((), ())), preferred_element_type=F32)


def dot_nt(a, b):
    return lax.dot_general(a, b, (((1,), (1,)), ((), ())), preferred_element_type=F32)


def stats_of(x):
    mean = jnp.mean(x, axis=-1, keepdims=True)
    centred = x - mean
    var = jnp.mean(centred * centred, axis=-1, keepdims=True)
    inv = lax.rsqrt(var + LN_EPS)
    return centred * inv, inv


def gelu_parts(u):
    e = jnp.exp(u * u * -0.5)
    t = 1.0 / (1.0 + 0.25 * jnp.abs(u))
    r = jnp.full_like(t, TAIL[-1])
    for c in TAIL[-2::-1]:
        r = r * t + c
    tail = r * t * e
    cdf = jnp.where(u >= 0.0, 1.0 - tail, tail)
    return u * cdf, cdf + u * (e * (1.0 / math.sqrt(2.0 * math.pi)))


def wide(table, width):
    return jnp.concatenate([table] * (width // table.shape[1]), axis=1) if table.shape[1] != width else table


def proj_kernel(x_ref, dy_ref, wqkv_ref, bqkv_ref, wup_ref, bup_ref, wdown_ref, wout_ref, g1_ref, s1_ref, g2_ref, s2_ref, tc_ref, ts_ref, tr_ref,
                first_ref, second_ref, q_ref, k_ref, v_ref, act_ref, gu_ref, ga_ref):
    heads = q_ref.shape[1]
    normed, _ = stats_of(x_ref[...].astype(F32))
    first = (normed * g1_ref[...].astype(F32) + s1_ref[...].astype(F32)).astype(BF16)
    second = (normed * g2_ref[...].astype(F32) + s2_ref[...].astype(F32)).astype(BF16)
    first_ref[...] = first
    second_ref[...] = second
    proj = dot_nn(first, wqkv_ref[...]) + bqkv_ref[...].astype(F32)
    tc, ts, tr = (wide(r[...], heads) for r in (tc_ref, ts_ref, tr_ref))

    def rotate(v):
        return v * tc + pltpu.roll(v, heads - ROT // 2, 1) * ts + pltpu.roll(v, ROT // 2, 1) * tr

    q_ref[...] = (rotate(proj[:, :heads]).astype(BF16).astype(F32) * (1.0 / math.sqrt(HD))).astype(BF16)
    k_ref[...] = rotate(proj[:, heads:2 * heads]).astype(BF16)
    v_ref[...] = proj[:, 2 * heads:].astype(BF16)
    dy = dy_ref[...]
    ga_ref[...] = dot_nt(dy, wout_ref[...]).astype(BF16)
    up = dot_nn(second, wup_ref[...]) + bup_ref[...].astype(F32)
    act, slope = gelu_parts(up)
    act_ref[...] = act.astype(BF16)
    gu_ref[...] = (dot_nt(dy, wdown_ref[...]) * slope).astype(BF16)


def full(shape):
    return pl.BlockSpec(shape, lambda *_: (0,) * len(shape))


def rows(width):
    return pl.BlockSpec((BLK, width), lambda i, *_: (i, 0))


def project(x, dy, wqkv, bqkv, wup, bup, wdown, wout, g1, s1, g2, s2, tables):
    tokens, width = x.shape
    heads, units = wqkv.shape[1] // 3, wup.shape[1]
    lanes = tables[0].shape[1]
    outs = [width, width, heads, heads, heads, units, units, heads]
    return pl.pallas_call(
        proj_kernel,
        grid=(tokens // BLK,),
        in_specs=[rows(width), rows(width), full(wqkv.shape), full(bqkv.shape), full(wup.shape), full(bup.shape), full(wdown.shape), full(wout.shape)]
        + [full(g1.shape)] * 4 + [rows(lanes)] * 3,
        out_specs=[rows(w) for w in outs],
        out_shape=[jax.ShapeDtypeStruct((tokens, w), BF16) for w in outs],
        compiler_params=pltpu.CompilerParams(vmem_limit_bytes=VMEM_LIMIT),
        name="project",
    )(x, dy, wqkv, bqkv, wup, bup, wdown, wout, g1, s1, g2, s2, *tables)


MOST = 5


def attend_kernel(lo_ref, q_ref, k_ref, v_ref, ga_ref, st_ref, tc_ref, ts_ref, tr_ref, att_ref, gp_ref,
                  kt_ref, vt_ref, dk_ref, dv_ref, s_ref, d_ref):
    i = pl.program_id(0)
    steps = pl.num_programs(0)
    tokens, width = k_ref.shape
    heads = width // HD

    @pl.when(i == 0)
    def _():
        kt_ref[...] = k_ref[...].T
        vt_ref[...] = v_ref[...].T
        dk_ref[...] = jnp.zeros_like(dk_ref)
        dv_ref[...] = jnp.zeros_like(dv_ref)

    lane_head = lax.broadcasted_iota(jnp.int32, (BLK, width), 1) // HD
    q, ga = q_ref[...], ga_ref[...]
    qm = [jnp.where(lane_head == h, q, jnp.zeros_like(q)) for h in range(heads)]
    gm = [jnp.where(lane_head == h, ga, jnp.zeros_like(ga)) for h in range(heads)]
    lo = lo_ref[i]
    count = i - lo + 1
    start_q = st_ref[...]
    q_at = i * BLK + lax.broadcasted_iota(jnp.int32, (BLK, BLK), 1)
    k_off = lax.broadcasted_iota(jnp.int32, (BLK, BLK), 0)

    def block(n):
        return pl.ds(pl.multiple_of((lo + n) * BLK, BLK), BLK)

    def scores(n, best):
        k_at = k_off + (lo + n) * BLK
        allowed = (k_at <= q_at) & (k_at >= start_q)
        keys = k_ref[block(n), :]
        new = []
        for h in range(heads):
            s = jnp.where(allowed, dot_nt(keys, qm[h]), NEG)
            s_ref[n, h] = s
            new.append(jnp.maximum(best[h], jnp.max(s, axis=0, keepdims=True)))
        return tuple(new)

    best = lax.fori_loop(0, count, scores, tuple(jnp.full((1, BLK), NEG, F32) for _ in range(heads)))

    def exps(n, total):
        new = []
        for h in range(heads):
            e = jnp.exp(s_ref[n, h] - best[h])
            s_ref[n, h] = e
            new.append(total[h] + jnp.sum(e, axis=0, keepdims=True))
        return tuple(new)

    total = lax.fori_loop(0, count, exps, tuple(jnp.zeros((1, BLK), F32) for _ in range(heads)))
    share = [1.0 / t for t in total]

    def values(n, carry):
        att, delta = carry
        vals = v_ref[block(n), :]
        new_att, new_delta, dv = [], [], None
        for h in range(heads):
            p = s_ref[n, h] * share[h]
            low = p.astype(BF16)
            new_att.append(att[h] + dot_nn(vt_ref[h * HD:(h + 1) * HD, block(n)], low))
            gp = dot_nt(vals, gm[h])
            s_ref[n, h] = p
            d_ref[n, h] = gp
            new_delta.append(delta[h] + jnp.sum(p * gp, axis=0, keepdims=True))
            part = dot_nn(low, gm[h])
            dv = part if dv is None else dv + part
        dv_ref[block(n), :] += dv
        return tuple(new_att), tuple(new_delta)

    zero_t = tuple(jnp.zeros((HD, BLK), F32) for _ in range(heads))
    att, delta = lax.fori_loop(0, count, values, (zero_t, tuple(jnp.zeros((1, BLK), F32) for _ in range(heads))))
    att_ref[...] = jnp.concatenate(att, axis=0).T.astype(BF16)

    def grads(n, dq):
        new, dk = [], None
        for h in range(heads):
            ds = (s_ref[n, h] * (d_ref[n, h] - delta[h])).astype(BF16)
            new.append(dq[h] + dot_nn(kt_ref[h * HD:(h + 1) * HD, block(n)], ds))
            part = dot_nn(ds, qm[h])
            dk = part if dk is None else dk + part
        dk_ref[block(n), :] += dk
        return tuple(new)

    dq = lax.fori_loop(0, count, grads, zero_t)

    def rotate_back(g, at):
        tc, ts, tr = (wide(r[at, :], width) for r in (tc_ref, ts_ref, tr_ref))
        return g * tc - pltpu.roll(g, width - ROT // 2, 1) * ts - pltpu.roll(g, ROT // 2, 1) * tr

    here = pl.ds(pl.multiple_of(i * BLK, BLK), BLK)
    dq = jnp.concatenate(dq, axis=0).T * (1.0 / math.sqrt(HD))
    gp_ref[here, :width] = rotate_back(dq, here).astype(BF16)

    @pl.when(i == steps - 1)
    def _():
        @pl.loop(0, tokens // BLK)
        def _(j):
            at = pl.ds(pl.multiple_of(j * BLK, BLK), BLK)
            gp_ref[at, width:2 * width] = rotate_back(dk_ref[at, :], at).astype(BF16)
            gp_ref[at, 2 * width:] = dv_ref[at, :].astype(BF16)


def attend(lo, q, k, v, ga, start_row, tables):
    tokens, width = q.shape
    lanes = tables[0].shape[1]
    heads = width // HD
    return pl.pallas_call(
        attend_kernel,
        grid_spec=pltpu.PrefetchScalarGridSpec(
            num_scalar_prefetch=1,
            grid=(tokens // BLK,),
            in_specs=[rows(width), full(k.shape), full(v.shape), rows(width), pl.BlockSpec((1, BLK), lambda i, *_: (0, i))] + [full((tokens, lanes))] * 3,
            out_specs=[rows(width), full((tokens, 3 * width))],
            scratch_shapes=[pltpu.VMEM((width, tokens), BF16)] * 2 + [pltpu.VMEM((tokens, width), F32)] * 2
            + [pltpu.VMEM((MOST, heads, BLK, BLK), F32)] * 2,
        ),
        out_shape=[jax.ShapeDtypeStruct((tokens, width), BF16), jax.ShapeDtypeStruct((tokens, 3 * width), BF16)],
        compiler_params=pltpu.CompilerParams(vmem_limit_bytes=VMEM_LIMIT),
        name="attend",
    )(lo, q, k, v, ga, start_row, *tables)


def back_kernel(bounds_ref, span_ref, x_ref, gp_ref, gu_ref, wqkv_ref, wup_ref, g1_ref, g2_ref, h_ref, vec_ref):
    i = pl.program_id(0)

    @pl.when(i == 0)
    def _():
        vec_ref[...] = jnp.zeros_like(vec_ref)

    width = x_ref.shape[1]
    normed, _ = stats_of(x_ref[...].astype(F32))
    gf = dot_nt(gp_ref[...], wqkv_ref[...])
    gs = dot_nt(gu_ref[...], wup_ref[...])
    h_ref[...] = (gf * g1_ref[...].astype(F32) + gs * g2_ref[...].astype(F32)).astype(BF16)
    at = i * BLK + lax.broadcasted_iota(jnp.int32, (BLK, 1), 0)
    parts = (gf * normed, gf, gs * normed, gs)

    def doc(d, _):
        inside = (at >= bounds_ref[d]) & (at < bounds_ref[d + 1])
        for n, part in enumerate(parts):
            vec_ref[n, d] += jnp.sum(jnp.where(inside, part, 0.0).reshape(BLK // 8, 8, width), axis=0)
        return 0

    lax.fori_loop(span_ref[i, 0], span_ref[i, 1] + 1, doc, 0)


def back(bounds, span, x, gp, gu, wqkv, wup, g1, g2):
    tokens, width = x.shape
    return pl.pallas_call(
        back_kernel,
        grid_spec=pltpu.PrefetchScalarGridSpec(
            num_scalar_prefetch=2,
            grid=(tokens // BLK,),
            in_specs=[rows(width), rows(gp.shape[1]), rows(gu.shape[1]), full(wqkv.shape), full(wup.shape), full(g1.shape), full(g2.shape)],
            out_specs=[rows(width), full((4, DOCS, 8, width))],
        ),
        out_shape=[jax.ShapeDtypeStruct((tokens, width), BF16), jax.ShapeDtypeStruct((4, DOCS, 8, width), F32)],
        compiler_params=pltpu.CompilerParams(vmem_limit_bytes=VMEM_LIMIT),
        name="back",
    )(bounds, span, x, gp, gu, wqkv, wup, g1, g2)


def gram_kernel(share, hi_ref, end_ref, *refs):
    mats, out_ref = refs[:7], refs[7]
    first, gp, second, gu, att, act, dy = mats
    j = pl.program_id(0)
    cols = pl.ds(pl.multiple_of(j * BLK, BLK), BLK)
    col_at = j * BLK + lax.broadcasted_iota(jnp.int32, (BLK, BLK), 1)
    off = lax.broadcasted_iota(jnp.int32, (BLK, BLK), 0)
    end = end_ref[...]

    def step(i, total):
        at = pl.ds(pl.multiple_of(i * BLK, BLK), BLK)

        def gram(m):
            return dot_nt(m[at, :], m[cols, :])

        terms = (gram(first) + 1.0) * gram(gp)
        terms = terms + (gram(second) + 1.0) * gram(gu)
        terms = terms + (gram(att) + gram(act) + share) * gram(dy)
        row_at = off + i * BLK
        weight = jnp.where(row_at > col_at, 2.0, jnp.where(row_at == col_at, 1.0, 0.0))
        terms = jnp.where(row_at < end, terms * weight, 0.0)
        return total + jnp.sum(terms.reshape(BLK // 8, 8, BLK), axis=0)

    out_ref[...] = lax.fori_loop(j, hi_ref[j] + 1, step, jnp.zeros((8, BLK), F32))


def gram_sums(hi, end_row, mats, share):
    tokens = mats[0].shape[0]
    return pl.pallas_call(
        functools.partial(gram_kernel, share),
        grid_spec=pltpu.PrefetchScalarGridSpec(
            num_scalar_prefetch=1,
            grid=(tokens // BLK,),
            in_specs=[pl.BlockSpec((1, BLK), lambda i, *_: (0, i))] + [full(m.shape) for m in mats],
            out_specs=pl.BlockSpec((8, BLK), lambda i, *_: (0, i)),
        ),
        out_shape=jax.ShapeDtypeStruct((8, tokens), F32),
        compiler_params=pltpu.CompilerParams(vmem_limit_bytes=VMEM_LIMIT),
        name="gram",
    )(hi, end_row, *mats)


def rotary(position, heads_lanes):
    lane = lax.broadcasted_iota(jnp.int32, (1, heads_lanes), 1) % HD
    half = ROT // 2
    freq = jnp.exp((lane % half).astype(F32) * (2.0 / ROT) * -math.log(10000.0))
    angle = position.astype(F32) * freq
    turn = lane < ROT
    cos, sin = jnp.cos(angle), jnp.sin(angle)
    return (jnp.where(turn, cos, 1.0), jnp.where(lane < half, -sin, 0.0), jnp.where(turn & (lane >= half), sin, 0.0))


def shards(block_input, segment_ids, cotangent, weight_qkv, bias_qkv, weight_out, bias_out, weight_up, bias_up, weight_down, bias_down,
           gain_first, shift_first, gain_second, shift_second):
    _, tokens, width = block_input.shape
    tp = lax.axis_size("mp")
    local = weight_qkv.shape[1] // (3 * HD)
    x, dy = block_input[0], cotangent[0]
    seg = segment_ids
    blocks = tokens // BLK
    doc_ids = lax.broadcasted_iota(jnp.int32, (DOCS + 1, 1), 0)
    bounds = jnp.sum((seg < doc_ids).astype(jnp.int32), axis=1)
    docs_col = lax.broadcasted_iota(jnp.int32, (DOCS, 1), 0)
    hot = seg == docs_col
    start_row = jnp.sum(jnp.where(hot, bounds[:DOCS, None], 0), axis=0, keepdims=True)
    end_row = jnp.sum(jnp.where(hot, bounds[1:, None], 0), axis=0, keepdims=True)
    first_seg, last_seg = seg[0, ::BLK], seg[0, BLK - 1::BLK]
    lo = start_row[0, ::BLK] // BLK
    hi = (end_row[0, BLK - 1::BLK] - 1) // BLK
    span = jnp.stack([first_seg, last_seg], axis=1)
    position = lax.broadcasted_iota(jnp.int32, (1, tokens), 1) - start_row
    tables = rotary(position.reshape(tokens, 1), 2 * HD)

    def part_major(w):
        return jnp.swapaxes(w.reshape(w.shape[:-1] + (local, 3, HD)), -3, -2).reshape(w.shape)

    def head_major(w):
        return jnp.swapaxes(w.reshape(w.shape[:-1] + (3, local, HD)), -3, -2).reshape(w.shape)

    wqkv, bqkv = part_major(weight_qkv), part_major(bias_qkv)
    row = lambda v: v.reshape(1, -1)
    first, second, q, k, v, act, gu, ga = project(
        x, dy, wqkv, row(bqkv), weight_up, row(bias_up), weight_down, weight_out, row(gain_first), row(shift_first), row(gain_second), row(shift_second), tables)
    att, gp = attend(lo, q, k, v, ga, start_row, tables)
    h, vec = back(bounds, span, x, gp, gu, wqkv, weight_up, row(gain_first), row(gain_second))
    h_rows = lax.psum_scatter(h, "mp", scatter_dimension=0, tiled=True)
    branches = (jnp.dot(att, weight_out, preferred_element_type=F32) + jnp.dot(act, weight_down, preferred_element_type=F32)).astype(BF16)
    summed = lax.psum_scatter(branches, "mp", scatter_dimension=0, tiled=True)
    col_sums = gram_sums(hi, end_row, (first, gp, second, gu, att, act, dy), 2.0 / tp)
    gram_part = jnp.sum(jnp.where(hot, jnp.sum(col_sums, axis=0, keepdims=True), 0.0), axis=1)
    vectors, gram_total = lax.psum((jnp.sum(vec, axis=2), gram_part), "mp")
    norm_values = jnp.sqrt(gram_total + jnp.sum(vectors * vectors, axis=(0, 2)) + NORM_EPS)
    clip = jnp.minimum(1.0, jnp.mean(norm_values) / norm_values)
    token_clip = jnp.sum(jnp.where(hot, clip[:, None], 0.0), axis=0).reshape(tokens, 1)
    scaled_proj = token_clip * gp.astype(F32)
    scaled_dy = token_clip * dy.astype(F32)
    scaled_up = token_clip * gu.astype(F32)
    clipped_dy = scaled_dy.astype(BF16)

    def tn(a, b):
        return jnp.einsum("tc,td->cd", a, b, preferred_element_type=F32).astype(BF16)

    g_qkv = lax.psum_scatter(tn(first, scaled_proj.astype(BF16)), "dp", scatter_dimension=0, tiled=True)
    g_up = lax.psum_scatter(tn(second, scaled_up.astype(BF16)), "dp", scatter_dimension=0, tiled=True)
    g_out = lax.psum_scatter(tn(att, clipped_dy), "dp", scatter_dimension=1, tiled=True)
    g_down = lax.psum_scatter(tn(act, clipped_dy), "dp", scatter_dimension=1, tiled=True)
    norm_grads = jnp.sum(vectors * clip[None, :, None], axis=1)
    b_qkv, b_up, b_out, norm_grads = lax.psum(
        (jnp.sum(scaled_proj, axis=0), jnp.sum(scaled_up, axis=0), jnp.sum(scaled_dy, axis=0), norm_grads), "dp")
    share = tokens // tp
    at = lax.axis_index("mp") * share
    x_rows = lax.dynamic_slice_in_dim(x, at, share, 0).astype(F32)
    dy_rows = lax.dynamic_slice_in_dim(dy, at, share, 0).astype(F32)
    block_output = (x_rows + summed.astype(F32) + bias_out.astype(F32) + bias_down.astype(F32)).astype(BF16)
    normed, inv = stats_of(x_rows)
    scaled = h_rows.astype(F32)
    grad_input = dy_rows + inv * (scaled - jnp.mean(scaled, axis=-1, keepdims=True) - normed * jnp.mean(scaled * normed, axis=-1, keepdims=True))
    return (block_output[None], grad_input[None], head_major(g_qkv.astype(F32)), head_major(b_qkv), g_out.astype(F32), b_out, g_up.astype(F32), b_up,
            g_down.astype(F32), b_out, norm_grads[0], norm_grads[1], norm_grads[2], norm_grads[3], norm_values[None])


def solution(mesh):
    placed = (P("dp", None, None), P("dp", None), P("dp", None, None), P(None, "mp"), P("mp"), P("mp", None), P(), P(None, "mp"), P("mp"), P("mp", None),
              P(), P(), P(), P(), P())
    return jax.shard_map(
        shards,
        mesh=mesh,
        in_specs=placed,
        out_specs=(P("dp", "mp", None), P("dp", "mp", None), P("dp", "mp"), P("mp"), P("mp", "dp"), P(), P("dp", "mp"), P("mp"), P("mp", "dp"), P(), P(),
                   P(), P(), P(), P("dp", None)),
        check_vma=False,
    )
```

```python
import functools
import math

import jax
import jax.numpy as jnp
from jax import lax
from jax.experimental import pallas as pl
from jax.experimental.pallas import tpu as pltpu
from jax.sharding import PartitionSpec as P

HD = 64
ROT = 16
DOCS = 8
BLK = 256
LN_EPS = 1e-05
NORM_EPS = 1e-06
NEG = -1e30
F32 = jnp.float32
BF16 = jnp.bfloat16
VMEM_LIMIT = 60 * 1024 * 1024

TAIL = (0.099163489, 0.109273513, 0.0348237317, 0.263242867, -0.249259412, 0.332377466, -0.089621649)


def dot_nn(a, b):
    return lax.dot_general(a, b, (((1,), (0,)), ((), ())), preferred_element_type=F32)


def dot_nt(a, b):
    return lax.dot_general(a, b, (((1,), (1,)), ((), ())), preferred_element_type=F32)


def stats_of(x):
    mean = jnp.mean(x, axis=-1, keepdims=True)
    centred = x - mean
    var = jnp.mean(centred * centred, axis=-1, keepdims=True)
    inv = lax.rsqrt(var + LN_EPS)
    return centred * inv, inv


def gelu_parts(u):
    e = jnp.exp(u * u * -0.5)
    t = 1.0 / (1.0 + 0.25 * jnp.abs(u))
    r = jnp.full_like(t, TAIL[-1])
    for c in TAIL[-2::-1]:
        r = r * t + c
    tail = r * t * e
    cdf = jnp.where(u >= 0.0, 1.0 - tail, tail)
    return u * cdf, cdf + u * (e * (1.0 / math.sqrt(2.0 * math.pi)))


def wide(table, width):
    return jnp.concatenate([table] * (width // table.shape[1]), axis=1) if table.shape[1] != width else table


def proj_kernel(x_ref, dy_ref, wqkv_ref, bqkv_ref, wup_ref, bup_ref, wdown_ref, wout_ref, g1_ref, s1_ref, g2_ref, s2_ref, tc_ref, ts_ref, tr_ref,
                first_ref, second_ref, q_ref, k_ref, v_ref, act_ref, gu_ref, ga_ref, first_t, second_t, dy_t):
    heads = q_ref.shape[1]
    normed, _ = stats_of(x_ref[...].astype(F32))
    first = (normed * g1_ref[...].astype(F32) + s1_ref[...].astype(F32)).astype(BF16)
    second = (normed * g2_ref[...].astype(F32) + s2_ref[...].astype(F32)).astype(BF16)
    first_ref[...] = first
    second_ref[...] = second
    first_t[...] = first.T
    second_t[...] = second.T
    dy_t[...] = dy_ref[...].T
    proj = dot_nn(first, wqkv_ref[...]) + bqkv_ref[...].astype(F32)
    tc, ts, tr = (wide(r[...], heads) for r in (tc_ref, ts_ref, tr_ref))

    def rotate(v):
        return v * tc + pltpu.roll(v, heads - ROT // 2, 1) * ts + pltpu.roll(v, ROT // 2, 1) * tr

    q_ref[...] = (rotate(proj[:, :heads]).astype(BF16).astype(F32) * (1.0 / math.sqrt(HD))).astype(BF16)
    k_ref[...] = rotate(proj[:, heads:2 * heads]).astype(BF16)
    v_ref[...] = proj[:, 2 * heads:].astype(BF16)
    dy = dy_ref[...]
    ga_ref[...] = dot_nt(dy, wout_ref[...]).astype(BF16)
    up = dot_nn(second, wup_ref[...]) + bup_ref[...].astype(F32)
    act, slope = gelu_parts(up)
    act_ref[...] = act.astype(BF16)
    gu_ref[...] = (dot_nt(dy, wdown_ref[...]) * slope).astype(BF16)


def full(shape):
    return pl.BlockSpec(shape, lambda *_: (0,) * len(shape))


def rows(width):
    return pl.BlockSpec((BLK, width), lambda i, *_: (i, 0))


def project(x, dy, wqkv, bqkv, wup, bup, wdown, wout, g1, s1, g2, s2, tables):
    tokens, width = x.shape
    heads, units = wqkv.shape[1] // 3, wup.shape[1]
    lanes = tables[0].shape[1]
    outs = [width, width, heads, heads, heads, units, units, heads]
    return pl.pallas_call(
        proj_kernel,
        grid=(tokens // BLK,),
        in_specs=[rows(width), rows(width), full(wqkv.shape), full(bqkv.shape), full(wup.shape), full(bup.shape), full(wdown.shape), full(wout.shape)]
        + [full(g1.shape)] * 4 + [rows(lanes)] * 3,
        out_specs=[rows(w) for w in outs] + [pl.BlockSpec((width, BLK), lambda i: (0, i))] * 3,
        out_shape=[jax.ShapeDtypeStruct((tokens, w), BF16) for w in outs] + [jax.ShapeDtypeStruct((width, tokens), BF16)] * 3,
        compiler_params=pltpu.CompilerParams(vmem_limit_bytes=VMEM_LIMIT),
        name="project",
    )(x, dy, wqkv, bqkv, wup, bup, wdown, wout, g1, s1, g2, s2, *tables)


MOST = 5


def attend_kernel(lo_ref, q_ref, k_ref, v_ref, ga_ref, st_ref, tc_ref, ts_ref, tr_ref, att_ref, gp_ref,
                  kt_ref, vt_ref, dk_ref, dv_ref, s_ref, d_ref):
    i = pl.program_id(0)
    steps = pl.num_programs(0)
    tokens, width = k_ref.shape
    heads = width // HD

    @pl.when(i == 0)
    def _():
        kt_ref[...] = k_ref[...].T
        vt_ref[...] = v_ref[...].T
        dk_ref[...] = jnp.zeros_like(dk_ref)
        dv_ref[...] = jnp.zeros_like(dv_ref)

    lane_head = lax.broadcasted_iota(jnp.int32, (BLK, width), 1) // HD
    q, ga = q_ref[...], ga_ref[...]
    qm = [jnp.where(lane_head == h, q, jnp.zeros_like(q)) for h in range(heads)]
    gm = [jnp.where(lane_head == h, ga, jnp.zeros_like(ga)) for h in range(heads)]
    lo = lo_ref[i]
    count = i - lo + 1
    start_q = st_ref[...]
    q_at = i * BLK + lax.broadcasted_iota(jnp.int32, (BLK, BLK), 1)
    k_off = lax.broadcasted_iota(jnp.int32, (BLK, BLK), 0)

    def block(n):
        return pl.ds(pl.multiple_of((lo + n) * BLK, BLK), BLK)

    def scores(n, best):
        k_at = k_off + (lo + n) * BLK
        allowed = (k_at <= q_at) & (k_at >= start_q)
        keys = k_ref[block(n), :]
        new = []
        for h in range(heads):
            s = jnp.where(allowed, dot_nt(keys, qm[h]), NEG)
            s_ref[n, h] = s
            new.append(jnp.maximum(best[h], jnp.max(s, axis=0, keepdims=True)))
        return tuple(new)

    best = lax.fori_loop(0, count, scores, tuple(jnp.full((1, BLK), NEG, F32) for _ in range(heads)))

    def exps(n, total):
        new = []
        for h in range(heads):
            e = jnp.exp(s_ref[n, h] - best[h])
            s_ref[n, h] = e
            new.append(total[h] + jnp.sum(e, axis=0, keepdims=True))
        return tuple(new)

    total = lax.fori_loop(0, count, exps, tuple(jnp.zeros((1, BLK), F32) for _ in range(heads)))
    share = [1.0 / t for t in total]

    def values(n, carry):
        att, delta = carry
        vals = v_ref[block(n), :]
        new_att, new_delta, dv = [], [], None
        for h in range(heads):
            p = s_ref[n, h] * share[h]
            low = p.astype(BF16)
            new_att.append(att[h] + dot_nn(vt_ref[h * HD:(h + 1) * HD, block(n)], low))
            gp = dot_nt(vals, gm[h])
            s_ref[n, h] = p
            d_ref[n, h] = gp
            new_delta.append(delta[h] + jnp.sum(p * gp, axis=0, keepdims=True))
            part = dot_nn(low, gm[h])
            dv = part if dv is None else dv + part
        dv_ref[block(n), :] += dv
        return tuple(new_att), tuple(new_delta)

    zero_t = tuple(jnp.zeros((HD, BLK), F32) for _ in range(heads))
    att, delta = lax.fori_loop(0, count, values, (zero_t, tuple(jnp.zeros((1, BLK), F32) for _ in range(heads))))
    att_ref[...] = jnp.concatenate(att, axis=0).T.astype(BF16)

    def grads(n, dq):
        new, dk = [], None
        for h in range(heads):
            ds = (s_ref[n, h] * (d_ref[n, h] - delta[h])).astype(BF16)
            new.append(dq[h] + dot_nn(kt_ref[h * HD:(h + 1) * HD, block(n)], ds))
            part = dot_nn(ds, qm[h])
            dk = part if dk is None else dk + part
        dk_ref[block(n), :] += dk
        return tuple(new)

    dq = lax.fori_loop(0, count, grads, zero_t)

    def rotate_back(g, at):
        tc, ts, tr = (wide(r[at, :], width) for r in (tc_ref, ts_ref, tr_ref))
        return g * tc - pltpu.roll(g, width - ROT // 2, 1) * ts - pltpu.roll(g, ROT // 2, 1) * tr

    here = pl.ds(pl.multiple_of(i * BLK, BLK), BLK)
    dq = jnp.concatenate(dq, axis=0).T * (1.0 / math.sqrt(HD))
    gp_ref[here, :width] = rotate_back(dq, here).astype(BF16)

    @pl.when(i == steps - 1)
    def _():
        @pl.loop(0, tokens // BLK)
        def _(j):
            at = pl.ds(pl.multiple_of(j * BLK, BLK), BLK)
            gp_ref[at, width:2 * width] = rotate_back(dk_ref[at, :], at).astype(BF16)
            gp_ref[at, 2 * width:] = dv_ref[at, :].astype(BF16)


def attend(lo, q, k, v, ga, start_row, tables):
    tokens, width = q.shape
    lanes = tables[0].shape[1]
    heads = width // HD
    return pl.pallas_call(
        attend_kernel,
        grid_spec=pltpu.PrefetchScalarGridSpec(
            num_scalar_prefetch=1,
            grid=(tokens // BLK,),
            in_specs=[rows(width), full(k.shape), full(v.shape), rows(width), pl.BlockSpec((1, BLK), lambda i, *_: (0, i))] + [full((tokens, lanes))] * 3,
            out_specs=[rows(width), full((tokens, 3 * width))],
            scratch_shapes=[pltpu.VMEM((width, tokens), BF16)] * 2 + [pltpu.VMEM((tokens, width), F32)] * 2
            + [pltpu.VMEM((MOST, heads, BLK, BLK), F32)] * 2,
        ),
        out_shape=[jax.ShapeDtypeStruct((tokens, width), BF16), jax.ShapeDtypeStruct((tokens, 3 * width), BF16)],
        compiler_params=pltpu.CompilerParams(vmem_limit_bytes=VMEM_LIMIT),
        name="attend",
    )(lo, q, k, v, ga, start_row, *tables)


def back_kernel(bounds_ref, span_ref, x_ref, gp_ref, gu_ref, wqkv_ref, wup_ref, g1_ref, g2_ref, h_ref, vec_ref):
    i = pl.program_id(0)

    @pl.when(i == 0)
    def _():
        vec_ref[...] = jnp.zeros_like(vec_ref)

    width = x_ref.shape[1]
    normed, _ = stats_of(x_ref[...].astype(F32))
    gf = dot_nt(gp_ref[...], wqkv_ref[...])
    gs = dot_nt(gu_ref[...], wup_ref[...])
    h_ref[...] = (gf * g1_ref[...].astype(F32) + gs * g2_ref[...].astype(F32)).astype(BF16)
    at = i * BLK + lax.broadcasted_iota(jnp.int32, (BLK, 1), 0)
    parts = (gf * normed, gf, gs * normed, gs)

    def doc(d, _):
        inside = (at >= bounds_ref[d]) & (at < bounds_ref[d + 1])
        for n, part in enumerate(parts):
            vec_ref[n, d] += jnp.sum(jnp.where(inside, part, 0.0).reshape(BLK // 8, 8, width), axis=0)
        return 0

    lax.fori_loop(span_ref[i, 0], span_ref[i, 1] + 1, doc, 0)


def back(bounds, span, x, gp, gu, wqkv, wup, g1, g2):
    tokens, width = x.shape
    return pl.pallas_call(
        back_kernel,
        grid_spec=pltpu.PrefetchScalarGridSpec(
            num_scalar_prefetch=2,
            grid=(tokens // BLK,),
            in_specs=[rows(width), rows(gp.shape[1]), rows(gu.shape[1]), full(wqkv.shape), full(wup.shape), full(g1.shape), full(g2.shape)],
            out_specs=[rows(width), full((4, DOCS, 8, width))],
        ),
        out_shape=[jax.ShapeDtypeStruct((tokens, width), BF16), jax.ShapeDtypeStruct((4, DOCS, 8, width), F32)],
        compiler_params=pltpu.CompilerParams(vmem_limit_bytes=VMEM_LIMIT),
        name="back",
    )(bounds, span, x, gp, gu, wqkv, wup, g1, g2)


def gram_kernel(share, hi_ref, end_ref, *refs):
    mats, out_ref = refs[:7], refs[7]
    first, gp, second, gu, att, act, dy = mats
    j = pl.program_id(0)
    cols = pl.ds(pl.multiple_of(j * BLK, BLK), BLK)
    col_at = j * BLK + lax.broadcasted_iota(jnp.int32, (BLK, BLK), 1)
    off = lax.broadcasted_iota(jnp.int32, (BLK, BLK), 0)
    end = end_ref[...]

    def step(i, total):
        at = pl.ds(pl.multiple_of(i * BLK, BLK), BLK)

        def gram(m):
            return dot_nt(m[at, :], m[cols, :])

        terms = (gram(first) + 1.0) * gram(gp)
        terms = terms + (gram(second) + 1.0) * gram(gu)
        terms = terms + (gram(att) + gram(act) + share) * gram(dy)
        row_at = off + i * BLK
        weight = jnp.where(row_at > col_at, 2.0, jnp.where(row_at == col_at, 1.0, 0.0))
        terms = jnp.where(row_at < end, terms * weight, 0.0)
        return total + jnp.sum(terms.reshape(BLK // 8, 8, BLK), axis=0)

    out_ref[...] = lax.fori_loop(j, hi_ref[j] + 1, step, jnp.zeros((8, BLK), F32))


def gram_sums(hi, end_row, mats, share):
    tokens = mats[0].shape[0]
    return pl.pallas_call(
        functools.partial(gram_kernel, share),
        grid_spec=pltpu.PrefetchScalarGridSpec(
            num_scalar_prefetch=1,
            grid=(tokens // BLK,),
            in_specs=[pl.BlockSpec((1, BLK), lambda i, *_: (0, i))] + [full(m.shape) for m in mats],
            out_specs=pl.BlockSpec((8, BLK), lambda i, *_: (0, i)),
        ),
        out_shape=jax.ShapeDtypeStruct((8, tokens), F32),
        compiler_params=pltpu.CompilerParams(vmem_limit_bytes=VMEM_LIMIT),
        name="gram",
    )(hi, end_row, *mats)


LOAD_AHEAD = 3


def bit_of(index, bit):
    return lax.rem(lax.div(index, 2**bit), 2)


def across(index, bit):
    return index + (1 - 2 * bit_of(index, bit)) * 2**bit


def log2(n):
    return n.bit_length() - 1


def remote(src, dst, send, recv, axis, index):
    return pltpu.make_async_remote_copy(src_ref=src, dst_ref=dst, send_sem=send, recv_sem=recv, device_id={axis: index}, device_id_type=pl.DeviceIdType.MESH)


def tail_kernel(n, tp, w, order, vec_ref, col_ref, seg_ref, b1_ref, b2_ref, second_t, first_t, dy_t, gu, gp, act, att, h, x, dy, wdown, wout,
                gup_ref, gq_ref, gdown_ref, gout_ref, bo_ref, gi_ref, small_ref, norm_ref,
                at, b, snd, rcv, keep, oacc, hown, hs, hr, bs, br, wd, xr, dyr, trow, tcol, gsend, grecv, bsum, smine, sall,
                at_sem, b_sem, w_sem, snd_sem, rcv_sem, hs_sem, hr_sem, bs_sem, br_sem, gs_sem, gr_sem, ss_sem, sr_sem, hown_sem, row_sem):
    width, tokens = first_t.shape
    me, m = lax.axis_index("dp"), lax.axis_index("mp")
    nb, mb = log2(n), log2(tp)
    shard, rows_own = width // n, tokens // tp
    nu, nq, na, ne = (r.shape[1] // w for r in (gu, gp, act, att))
    units = nu + nq + na + ne

    barrier = pltpu.get_barrier_semaphore()
    for r in range(1, n):
        pl.semaphore_signal(barrier, inc=1, device_id={"dp": lax.rem(me + r, n)}, device_id_type=pl.DeviceIdType.MESH)
    for r in range(1, tp):
        pl.semaphore_signal(barrier, inc=1, device_id={"mp": lax.rem(m + r, tp)}, device_id_type=pl.DeviceIdType.MESH)
    pl.semaphore_wait(barrier, n - 1 + tp - 1)

    for j in range(tp // 2):
        there = 2 * j + 1 - bit_of(m, 0)
        remote(h.at[pl.ds(there * rows_own, rows_own)], hr[0].at[j], hs_sem.at[0, j], hr_sem.at[0, j], "mp", across(m, 0)).start()

    sources = (second_t, first_t, dy_t)

    def place(p):
        return sum(((p >> (nb - 1 - k)) & 1) << order[k] for k in range(nb))

    def load_at(mat):
        for p in range(n):
            pltpu.make_async_copy(sources[mat].at[pl.ds(place(p) * shard, shard)], at.at[mat, pl.ds(p * shard, shard)], at_sem.at[mat]).start()

    def load_b(base, src):
        for i in range(src.shape[1] // w):
            pltpu.make_async_copy(src.at[:, pl.ds(i * w, w)], b.at[base + i], b_sem.at[base + i]).start()

    load_at(0)
    load_b(0, gu)
    load_at(1)
    load_b(nu, gp)
    load_at(2)
    load_b(nu + nq, act)
    load_b(nu + nq + na, att)
    split = act.shape[1]
    wd_copies = (pltpu.make_async_copy(wdown, wd.at[pl.ds(0, split)], w_sem.at[0]), pltpu.make_async_copy(wout, wd.at[pl.ds(split, wd.shape[0] - split)], w_sem.at[1]))
    own_at = pl.ds(m * rows_own, rows_own)
    row_copies = (pltpu.make_async_copy(x.at[own_at], xr, row_sem.at[0]), pltpu.make_async_copy(dy.at[own_at], dyr, row_sem.at[1]))
    hown_copies = [pltpu.make_async_copy(h.at[pl.ds((2 * j + bit_of(m, 0)) * rows_own, rows_own)], hown.at[j], hown_sem.at[j]) for j in range(tp // 2)]
    for c in (*wd_copies, *row_copies, *hown_copies):
        c.start()

    hot = seg_ref[...] == lax.broadcasted_iota(jnp.int32, (DOCS, tokens), 0)
    mine = jnp.sum(jnp.where(hot, jnp.sum(col_ref[...], axis=0, keepdims=True), 0.0), axis=1, keepdims=True)
    gsend[...] = jnp.broadcast_to(mine, gsend.shape)
    grecv[m] = gsend[...]
    for r in range(1, tp):
        remote(gsend, grecv.at[m], gs_sem.at[r - 1], gr_sem.at[m], "mp", lax.rem(m + r, tp)).start()
    squares = jnp.zeros((DOCS, 1), F32)
    for j in range(4):
        squares = squares + jnp.sum(vec_ref[j] * vec_ref[j], axis=1, keepdims=True)
    for r in range(1, tp):
        src = lax.rem(m + r, tp)
        remote(gsend, grecv.at[src], gs_sem.at[r - 1], gr_sem.at[src], "mp", src).wait_recv()
    gram = grecv[0]
    for r in range(1, tp):
        gram = gram + grecv[r]
    norm = jnp.sqrt(gram[:, :1] + squares + NORM_EPS)
    norm_ref[...] = jnp.broadcast_to(norm, norm_ref.shape)
    clip = jnp.minimum(1.0, jnp.mean(norm, axis=0, keepdims=True) / norm)
    per_token = jnp.sum(jnp.where(hot, clip, 0.0), axis=0, keepdims=True)
    trow[...] = per_token
    tcol[...] = jnp.broadcast_to(per_token, (DOCS, tokens)).T
    smine[...] = jnp.zeros_like(smine)
    for j in range(4):
        smine[3 + j:4 + j, :] = jnp.sum(vec_ref[j] * clip, axis=0, keepdims=True)

    half = width // 2
    bits = [bit_of(me, k) for k in order]
    partners = [across(me, k) for k in order]

    def matrix_of(u):
        return jnp.where(u >= nu, 1, 0) + jnp.where(u >= nu + nq, 1, 0)

    def exchange(k, u):
        return remote(snd[k].at[u], rcv[k].at[u], snd_sem.at[k, u], rcv_sem.at[k, u], "dp", partners[k])

    def other_half(mat, clipped, u):
        pltpu.make_async_copy(gu.at[:, pl.ds(0, w)], b.at[u], b_sem.at[u]).wait()
        if clipped:
            scaled = b[u].astype(F32) * tcol[:, :1]
            b[u] = scaled.astype(BF16)
            bsum[u] = jnp.sum(scaled.reshape(tokens // 8, 8, w), axis=0)
        away = pl.ds(pl.multiple_of((1 - bits[0]) * half, half), half)
        snd[0][u] = dot_nn(at[mat, away, :], b[u]).astype(BF16)

        @pl.when(u < LOAD_AHEAD)
        def _():
            exchange(0, u).start()

    def at_ready(mat):
        pltpu.make_async_copy(sources[mat], at.at[mat], at_sem.at[mat]).wait()

    at_ready(0)
    pl.loop(0, nu)(lambda u: other_half(0, True, u))
    at_ready(1)
    pl.loop(nu, nu + nq)(lambda u: other_half(1, True, u))
    at_ready(2)
    for p in range(n):
        piece = pl.ds(p * shard, shard)
        scaled = at[2, piece, :].astype(F32) * trow[...]
        at[2, piece, :] = scaled.astype(BF16)
        folded = scaled[:, :128]
        for k in range(1, tokens // 128):
            folded = folded + scaled[:, k * 128:(k + 1) * 128]
        smine[2:3, place(p) * shard:(place(p) + 1) * shard] = jnp.sum(folded.T, axis=0, keepdims=True)
    pl.loop(nu + nq, units)(lambda u: other_half(2, False, u))

    for i in range(nq):
        smine[0:1, i * w:(i + 1) * w] = jnp.sum(bsum[nu + i], axis=0, keepdims=True)
    for i in range(nu):
        smine[1:2, i * w:(i + 1) * w] = jnp.sum(bsum[i], axis=0, keepdims=True)
    sall[me] = smine[...]
    for r in range(1, n):
        remote(smine, sall.at[me], ss_sem.at[r - 1], sr_sem.at[me], "dp", lax.rem(me + r, n)).start()

    chunk = min(rows_own, 256)
    for c in wd_copies:
        c.wait()

    def branch(owner, c):
        at_rows = pl.ds(pl.multiple_of(owner * rows_own + c * chunk, chunk), chunk)
        left = jnp.concatenate([b[nu + nq + i, at_rows, :] for i in range(na + ne)], axis=1)
        return dot_nn(left, wd[...])

    def chunks(body):
        pl.loop(0, rows_own // chunk)(lambda c: body(c, pl.ds(pl.multiple_of(c * chunk, chunk), chunk)))

    def slot(owner, k):
        return lax.div(owner, 2 ** (k + 1))

    for j in range(tp // 2):
        there = 2 * j + 1 - bit_of(m, 0)

        def first_send(c, rows_at):
            bs[0][j, rows_at, :] = branch(there, c).astype(BF16)

        chunks(first_send)
        remote(bs[0].at[j], br[0].at[j], bs_sem.at[0, j], br_sem.at[0, j], "mp", across(m, 0)).start()

    for c in hown_copies:
        c.wait()

    def wait_mp(k, buf, recv_sem, send_sem):
        for j in range(tp >> (k + 1)):
            remote(buf[k].at[j], buf[k].at[j], send_sem.at[k, j], recv_sem.at[k, j], "mp", across(m, k)).wait_recv()

    for k in range(1, mb):
        wait_mp(k - 1, hr, hr_sem, hs_sem)
        for j in range(tp >> (k + 1)):
            owner = (2 * j + 1 - bit_of(m, k)) * 2**k + lax.rem(m, 2**k)

            def h_send(c, rows_at):
                val = hown[slot(owner, 0), rows_at, :].astype(F32)
                for r in range(k):
                    val = val + hr[r][slot(owner, r), rows_at, :].astype(F32)
                hs[k - 1][j, rows_at, :] = val.astype(BF16)

            chunks(h_send)
            remote(hs[k - 1].at[j], hr[k].at[j], hs_sem.at[k, j], hr_sem.at[k, j], "mp", across(m, k)).start()
        wait_mp(k - 1, br, br_sem, bs_sem)
        for j in range(tp >> (k + 1)):
            owner = (2 * j + 1 - bit_of(m, k)) * 2**k + lax.rem(m, 2**k)

            def b_send(c, rows_at):
                val = branch(owner, c)
                for r in range(k):
                    val = val + br[r][slot(owner, r), rows_at, :].astype(F32)
                bs[k][j, rows_at, :] = val.astype(BF16)

            chunks(b_send)
            remote(bs[k].at[j], br[k].at[j], bs_sem.at[k, j], br_sem.at[k, j], "mp", across(m, k)).start()

    def split_off(k, u, away, stay):
        snd[k][u] = away.astype(BF16)
        keep[k - 1][...] = stay
        exchange(k, u).start()

    def later(k, u):
        exchange(k, u).wait_recv()
        val = keep[k - 1][...] + rcv[k][u].astype(F32)
        if k == nb - 1:
            oacc[u] = val
            return
        size = val.shape[0] // 2
        upper = bits[k + 1] == 1
        split_off(k + 1, u, jnp.where(upper, val[:size], val[size:]), jnp.where(upper, val[size:], val[:size]))

    def first(u):
        mat = matrix_of(u)
        exchange(0, u).wait_recv()

        @pl.when(u + LOAD_AHEAD < units)
        def _():
            exchange(0, u + LOAD_AHEAD).start()

        size = half // 2
        parts = []
        for take in (1 - bits[1], bits[1]):
            own = pl.ds(pl.multiple_of(bits[0] * half + take * size, size), size)
            got = pl.ds(pl.multiple_of(take * size, size), size)
            parts.append(dot_nn(at[mat, own, :], b[u]) + rcv[0][u, got, :].astype(F32))
        split_off(1, u, *parts)

    def step(t):
        for k in range(nb - 1, 0, -1):
            pl.when((t >= k) & (t < units + k))(functools.partial(later, k, t - k))
        pl.when(t < units)(functools.partial(first, t))

    pl.loop(0, units // 2)(step)

    for c in row_copies:
        c.wait()
    wait_mp(mb - 1, hr, hr_sem, hs_sem)
    wait_mp(mb - 1, br, br_sem, bs_sem)

    def finish(c, rows_at):
        val = hown[slot(m, 0), rows_at, :].astype(F32)
        for r in range(mb):
            val = val + hr[r][slot(m, r), rows_at, :].astype(F32)
        xs = xr[rows_at, :].astype(F32)
        normed, inv = stats_of(xs)
        back_x = inv * (val - jnp.mean(val, axis=-1, keepdims=True) - normed * jnp.mean(val * normed, axis=-1, keepdims=True))
        gi_ref[rows_at, :] = dyr[rows_at, :].astype(F32) + back_x
        out = branch(m, c) + (xs + b1_ref[...].astype(F32) + b2_ref[...].astype(F32))
        for r in range(mb):
            out = out + br[r][slot(m, r), rows_at, :].astype(F32)
        bo_ref[rows_at, :] = out.astype(BF16)

    chunks(finish)
    pl.loop(units // 2, units + nb - 1)(step)

    for i in range(nu):
        gup_ref[:, i * w:(i + 1) * w] = oacc[i]
    for i in range(nq):
        gq_ref[:, i * w:(i + 1) * w] = oacc[nu + i]
    for i in range(na):
        gdown_ref[i * w:(i + 1) * w, :] = oacc[nu + nq + i].T
    for i in range(ne):
        gout_ref[i * w:(i + 1) * w, :] = oacc[nu + nq + na + i].T
    for r in range(1, n):
        src = lax.rem(me + r, n)
        remote(smine, sall.at[src], ss_sem.at[r - 1], sr_sem.at[src], "dp", src).wait_recv()
    total = sall[0]
    for r in range(1, n):
        total = total + sall[r]
    small_ref[...] = total

    @pl.loop(0, units)
    def _(u):
        for k in range(nb):
            exchange(k, u).wait_send()

    for r in range(1, n):
        remote(smine, sall.at[me], ss_sem.at[r - 1], sr_sem.at[me], "dp", lax.rem(me + r, n)).wait_send()
    for r in range(1, tp):
        remote(gsend, grecv.at[m], gs_sem.at[r - 1], gr_sem.at[m], "mp", lax.rem(m + r, tp)).wait_send()
    for k in range(mb):
        for j in range(tp >> (k + 1)):
            src_h = h.at[pl.ds(0, rows_own)] if k == 0 else hs[k - 1].at[j]
            remote(src_h, hr[k].at[j], hs_sem.at[k, j], hr_sem.at[k, j], "mp", across(m, k)).wait_send()
            remote(bs[k].at[j], br[k].at[j], bs_sem.at[k, j], br_sem.at[k, j], "mp", across(m, k)).wait_send()


def tail(n, tp, vec, col, seg, b1, b2, second_t, first_t, dy_t, gu, gp, act, att, h, x, dy, wdown, wout):
    width, tokens = first_t.shape
    widths = [a.shape[1] for a in (gu, gp, act, att)]
    w = BLK if all(v % BLK == 0 for v in widths) else BLK // 2
    units = sum(widths) // w
    nb, mb = log2(n), log2(tp)
    order = tuple(range(nb))
    shard, own = width // n, tokens // tp
    hbm = pl.BlockSpec(memory_space=pl.ANY)
    vmem = pl.BlockSpec(memory_space=pltpu.VMEM)
    V, D = pltpu.VMEM, pltpu.SemaphoreType.DMA
    mp_bufs = lambda lo: [V((tp >> (k + 1), own, width), BF16) for k in range(lo, mb)]
    step_bufs = lambda: [V((units, width >> (k + 1), w), BF16) for k in range(nb)]
    return pl.pallas_call(
        functools.partial(tail_kernel, n, tp, w, order),
        in_specs=[vmem] * 5 + [hbm] * 12,
        out_specs=[vmem] * 8,
        out_shape=[jax.ShapeDtypeStruct(s, t) for s, t in (
            ((shard, widths[0]), F32), ((shard, widths[1]), F32), ((widths[2], shard), F32), ((widths[3], shard), F32),
            ((own, width), BF16), ((own, width), F32), ((8, width), F32), ((DOCS, 128), F32))],
        scratch_shapes=[
            V((3, width, tokens), BF16), V((units, tokens, w), BF16), step_bufs(), step_bufs(), [V((width >> (k + 1), w), F32) for k in range(1, nb)],
            V((units, shard, w), F32), V((tp // 2, own, width), BF16), mp_bufs(1), mp_bufs(0), mp_bufs(0), mp_bufs(0),
            V((wdown.shape[0] + wout.shape[0], width), BF16), V((own, width), BF16), V((own, width), BF16), V((1, tokens), F32), V((tokens, DOCS), F32),
            V((DOCS, 128), F32), V((tp, DOCS, 128), F32), V((units, 8, w), F32), V((8, width), F32), V((n, 8, width), F32),
            D((3,)), D((units,)), D((2,)), D((nb, units)), D((nb, units)), D((mb, tp // 2)), D((mb, tp // 2)), D((mb, tp // 2)), D((mb, tp // 2)),
            D((tp - 1,)), D((tp,)), D((n - 1,)), D((n,)), D((tp // 2,)), D((2,))],
        compiler_params=pltpu.CompilerParams(collective_id=1, has_side_effects=True, vmem_limit_bytes=64 * 1024 * 1024 - 1024 * 1024),
        name="tail",
    )(vec, col, seg, b1, b2, second_t, first_t, dy_t, gu, gp, act, att, h, x, dy, wdown, wout)


def rotary(position, heads_lanes):
    lane = lax.broadcasted_iota(jnp.int32, (1, heads_lanes), 1) % HD
    half = ROT // 2
    freq = jnp.exp((lane % half).astype(F32) * (2.0 / ROT) * -math.log(10000.0))
    angle = position.astype(F32) * freq
    turn = lane < ROT
    cos, sin = jnp.cos(angle), jnp.sin(angle)
    return (jnp.where(turn, cos, 1.0), jnp.where(lane < half, -sin, 0.0), jnp.where(turn & (lane >= half), sin, 0.0))


def shards(block_input, segment_ids, cotangent, weight_qkv, bias_qkv, weight_out, bias_out, weight_up, bias_up, weight_down, bias_down,
           gain_first, shift_first, gain_second, shift_second):
    _, tokens, width = block_input.shape
    tp = lax.axis_size("mp")
    local = weight_qkv.shape[1] // (3 * HD)
    x, dy = block_input[0], cotangent[0]
    seg = segment_ids
    blocks = tokens // BLK
    doc_ids = lax.broadcasted_iota(jnp.int32, (DOCS + 1, 1), 0)
    bounds = jnp.sum((seg < doc_ids).astype(jnp.int32), axis=1)
    docs_col = lax.broadcasted_iota(jnp.int32, (DOCS, 1), 0)
    hot = seg == docs_col
    start_row = jnp.sum(jnp.where(hot, bounds[:DOCS, None], 0), axis=0, keepdims=True)
    end_row = jnp.sum(jnp.where(hot, bounds[1:, None], 0), axis=0, keepdims=True)
    first_seg, last_seg = seg[0, ::BLK], seg[0, BLK - 1::BLK]
    lo = start_row[0, ::BLK] // BLK
    hi = (end_row[0, BLK - 1::BLK] - 1) // BLK
    span = jnp.stack([first_seg, last_seg], axis=1)
    position = lax.broadcasted_iota(jnp.int32, (1, tokens), 1) - start_row
    tables = rotary(position.reshape(tokens, 1), 2 * HD)

    def part_major(w):
        return jnp.swapaxes(w.reshape(w.shape[:-1] + (local, 3, HD)), -3, -2).reshape(w.shape)

    def head_major(w):
        return jnp.swapaxes(w.reshape(w.shape[:-1] + (3, local, HD)), -3, -2).reshape(w.shape)

    wqkv, bqkv = part_major(weight_qkv), part_major(bias_qkv)
    row = lambda v: v.reshape(1, -1)
    first, second, q, k, v, act, gu, ga, first_t, second_t, dy_t = project(
        x, dy, wqkv, row(bqkv), weight_up, row(bias_up), weight_down, weight_out, row(gain_first), row(shift_first), row(gain_second), row(shift_second), tables)
    att, gp = attend(lo, q, k, v, ga, start_row, tables)
    h, vec = back(bounds, span, x, gp, gu, wqkv, weight_up, row(gain_first), row(gain_second))
    vectors = lax.psum(jnp.sum(vec, axis=2), "mp")
    col_sums = gram_sums(hi, end_row, (first, gp, second, gu, att, act, dy), 2.0 / tp)
    g_up, g_qkv, g_down, g_out, block_output, grad_input, small, norms = tail(
        lax.axis_size("dp"), tp, vectors, col_sums, seg, row(bias_out), row(bias_down), second_t, first_t, dy_t, gu, gp, act, att, h, x, dy, weight_down, weight_out)
    b_out = small[2]
    return (block_output[None], grad_input[None], head_major(g_qkv), head_major(small[0, :g_qkv.shape[1]]), g_out, b_out, g_up, small[1, :g_up.shape[1]],
            g_down, b_out, small[3], small[4], small[5], small[6], norms[:, 0][None])


def solution(mesh):
    placed = (P("dp", None, None), P("dp", None), P("dp", None, None), P(None, "mp"), P("mp"), P("mp", None), P(), P(None, "mp"), P("mp"), P("mp", None),
              P(), P(), P(), P(), P())
    return jax.shard_map(
        shards,
        mesh=mesh,
        in_specs=placed,
        out_specs=(P("dp", "mp", None), P("dp", "mp", None), P("dp", "mp"), P("mp"), P("mp", "dp"), P(), P("dp", "mp"), P("mp"), P("mp", "dp"), P(), P(),
                   P(), P(), P(), P("dp", None)),
        check_vma=False,
    )
```

```python
import functools
import math

import jax
import jax.numpy as jnp
from jax import lax
from jax.experimental import pallas as pl
from jax.experimental.pallas import tpu as pltpu
from jax.sharding import PartitionSpec as P

HD = 64
ROT = 16
DOCS = 8
BLK = 256
LN_EPS = 1e-05
NORM_EPS = 1e-06
NEG = -1e30
F32 = jnp.float32
BF16 = jnp.bfloat16
VMEM_LIMIT = 60 * 1024 * 1024

TAIL = (0.099163489, 0.109273513, 0.0348237317, 0.263242867, -0.249259412, 0.332377466, -0.089621649)


def dot_nn(a, b):
    return lax.dot_general(a, b, (((1,), (0,)), ((), ())), preferred_element_type=F32)


def dot_nt(a, b):
    return lax.dot_general(a, b, (((1,), (1,)), ((), ())), preferred_element_type=F32)


def stats_of(x):
    mean = jnp.mean(x, axis=-1, keepdims=True)
    centred = x - mean
    var = jnp.mean(centred * centred, axis=-1, keepdims=True)
    inv = lax.rsqrt(var + LN_EPS)
    return centred * inv, inv


def gelu_parts(u):
    e = jnp.exp(u * u * -0.5)
    t = 1.0 / (1.0 + 0.25 * jnp.abs(u))
    r = jnp.full_like(t, TAIL[-1])
    for c in TAIL[-2::-1]:
        r = r * t + c
    tail = r * t * e
    cdf = jnp.where(u >= 0.0, 1.0 - tail, tail)
    return u * cdf, cdf + u * (e * (1.0 / math.sqrt(2.0 * math.pi)))


MOST = 5


def pre_kernel(share, seg_ref, par_ref, x, dy, wqkv, wup, wdown, wout,
               first_o, second_o, dy_o, gp_o, gu_o, act_o, att_o, h_o, col_ref, vec_ref,
               xv, dyv, first, second, act, gu, gp, att, qt, kt, vt, gat, kf, vf, dkt, dvt, wqt, wu, wd, wo, tst, hst, start, end, cosr, sinr, bq, sgp, sgu, bounds,
               x_sem, dy_sem, w_sem, t_sem, h_sem, o_sem):
    tokens, width = xv.shape
    units, heads3 = act.shape[1], gp.shape[1]
    heads = att.shape[1]
    count = heads // HD
    blocks = tokens // BLK

    def block(i, n=1):
        return pl.ds(pl.multiple_of(i * BLK, BLK), n * BLK)

    def x_copy(i):
        return pltpu.make_async_copy(x.at[block(i)], xv.at[block(i)], x_sem.at[i])

    def dy_copy(i):
        return pltpu.make_async_copy(dy.at[block(i)], dyv.at[block(i)], dy_sem.at[i])

    raw = gp.at[pl.ds(0, width)]
    w_copies = [pltpu.make_async_copy(a, b, w_sem.at[n]) for n, (a, b) in enumerate(((wqkv, raw), (wout, wo), (wup, wu), (wdown, wd)))]
    w_copies[0].start()
    x_copy(0).start()
    dy_copy(0).start()
    for c in w_copies[1:]:
        c.start()
    for i in range(1, blocks):
        x_copy(i).start()
        dy_copy(i).start()

    seg = seg_ref[...]
    edges = [jnp.sum((seg < d).astype(jnp.int32)) for d in range(1, DOCS)]
    bounds[0] = 0
    bounds[DOCS] = tokens
    begin, finish = jnp.zeros_like(seg), jnp.full_like(seg, tokens)
    for d in range(1, DOCS):
        bounds[d] = edges[d - 1]
        begin = jnp.where(seg >= d, edges[d - 1], begin)
    for d in range(DOCS - 1, 0, -1):
        finish = jnp.where(seg < d, edges[d - 1], finish)
    start[...] = begin
    end[...] = finish
    half = ROT // 2
    at_token = lax.broadcasted_iota(jnp.int32, (half, tokens), 1)
    freq = jnp.exp(lax.broadcasted_iota(jnp.int32, (half, tokens), 0).astype(F32) * (2.0 / ROT) * -math.log(10000.0))
    angle = (at_token - begin).astype(F32) * freq
    cosr[...] = jnp.cos(angle)
    sinr[...] = jnp.sin(angle)
    o = 0
    parts = []
    for size in (heads3, units, width, width, width, width):
        parts.append(par_ref[:, o:o + size].astype(F32))
        o += size
    bqkv, bup, g1, s1, g2, s2 = parts
    bq[...] = jnp.broadcast_to(bqkv, (8, heads3)).T
    w_copies[0].wait()
    wqt[...] = raw[...].T
    for c in w_copies[1:]:
        c.wait()

    def t_copies(i):
        slot = lax.rem(i, 2)
        return [pltpu.make_async_copy(tst.at[slot, n], out.at[:, block(i)], t_sem.at[slot, n]) for n, out in enumerate((first_o, second_o, dy_o))]

    def out_copy(n, src, out, i):
        return pltpu.make_async_copy(src.at[block(i)], out.at[block(i)], o_sem.at[n, i])

    outs = ((act, act_o), (gu, gu_o), (att, att_o), (gp, gp_o))

    def turn(v, c, s):
        a, b = v[:half], v[half:ROT]
        return jnp.concatenate([a * c - b * s, b * c + a * s, v[ROT:]], axis=0)

    @pl.loop(0, blocks)
    def _(i):
        at = block(i)
        x_copy(i).wait()
        dy_copy(i).wait()
        normed, _ = stats_of(xv[at, :].astype(F32))
        fi = (normed * g1 + s1).astype(BF16)
        se = (normed * g2 + s2).astype(BF16)
        dyb = dyv[at, :]
        first[at, :] = fi
        second[at, :] = se
        chunk = min(256, units)
        ups = [(dot_nn(se, wu[:, c:c + chunk]), dot_nt(dyb, wd[c:c + chunk, :])) for c in range(0, units, chunk)]
        pt = dot_nt(wqt[...], fi) + bq[:, :1]
        gat[:, at] = dot_nt(wo[...], dyb).astype(BF16)
        for n, c in enumerate(range(0, units, chunk)):
            value, slope = gelu_parts(ups[n][0] + bup[:, c:c + chunk])
            act[at, c:c + chunk] = value.astype(BF16)
            gu[at, c:c + chunk] = (ups[n][1] * slope).astype(BF16)

        @pl.when(i >= 2)
        def _():
            for c in t_copies(i - 2):
                c.wait()

        slot = lax.rem(i, 2)
        tst[slot, 0] = fi.T
        tst[slot, 1] = se.T
        tst[slot, 2] = dyb.T
        c, s = cosr[:, at], sinr[:, at]
        qs, ks, vs = [], [], []
        for h in range(count):
            o = h * 3 * HD
            qs.append((turn(pt[o:o + HD], c, s).astype(BF16).astype(F32) * (1.0 / math.sqrt(HD))).astype(BF16))
            ks.append(turn(pt[o + HD:o + 2 * HD], c, s).astype(BF16))
            vs.append(pt[o + 2 * HD:o + 3 * HD].astype(BF16))
        kb, vb = jnp.concatenate(ks, axis=0), jnp.concatenate(vs, axis=0)
        qt[:, at] = jnp.concatenate(qs, axis=0)
        kt[:, at] = kb
        vt[:, at] = vb
        kf[at, :] = kb.T
        vf[at, :] = vb.T
        for copy in (*t_copies(i), out_copy(0, act, act_o, i), out_copy(1, gu, gu_o, i)):
            copy.start()

    dkt[...] = jnp.zeros_like(dkt)
    dvt[...] = jnp.zeros_like(dvt)

    def low_block(i):
        lowest = 0
        for d in range(1, DOCS):
            lowest = jnp.maximum(lowest, jnp.where(bounds[d] <= i * BLK, bounds[d], 0))
        return lax.div(lowest, BLK)

    def high_block(j):
        last = j * BLK + BLK - 1
        highest = tokens
        for d in range(1, DOCS):
            highest = jnp.minimum(highest, jnp.where(bounds[d] > last, bounds[d], tokens))
        return lax.div(highest - 1, BLK)

    def attend(i, lo, n):
        at, keys, size = block(i), block(lo, n), n * BLK
        k_at = lo * BLK + lax.broadcasted_iota(jnp.int32, (size, BLK), 0)
        q_at = i * BLK + lax.broadcasted_iota(jnp.int32, (size, BLK), 1)
        bias = jnp.where((k_at <= q_at) & (k_at >= start[:, at]), 0.0, NEG)
        blank = jnp.zeros((HD, BLK), BF16)
        span = min(2 * HD, heads)

        def spread(v, h):
            return jnp.concatenate([v if g == h % (span // HD) else blank for g in range(span // HD)], axis=0)

        def lanes(h):
            return slice(h * HD // span * span, h * HD // span * span + span)

        def rows_of(h):
            return slice(h * HD, (h + 1) * HD)

        s, p, low, gprob, ds, atts, dqs = {}, {}, {}, {}, {}, {}, {}

        def stage_a(h):
            s[h] = dot_nn(kf[keys, lanes(h)], spread(qt[rows_of(h), at], h)) + bias

        def stage_b(h):
            e = jnp.exp(s[h] - jnp.max(s[h], axis=0, keepdims=True))
            p[h] = e * (1.0 / jnp.sum(e, axis=0, keepdims=True))
            low[h] = p[h].astype(BF16)

        def stage_c(h):
            atts[h] = dot_nn(vt[rows_of(h), keys], low[h])
            gprob[h] = dot_nn(vf[keys, lanes(h)], spread(gat[rows_of(h), at], h))
            dvt[rows_of(h), keys] += dot_nt(gat[rows_of(h), at], low[h])

        def stage_d(h):
            delta = jnp.sum(p[h] * gprob[h], axis=0, keepdims=True)
            ds[h] = (p[h] * (gprob[h] - delta)).astype(BF16)

        def stage_e(h):
            dqs[h] = dot_nn(kt[rows_of(h), keys], ds[h])
            dkt[rows_of(h), keys] += dot_nt(qt[rows_of(h), at], ds[h])

        stages = (stage_a, stage_b, stage_c, stage_d, stage_e)
        for t in range(count + len(stages) - 1):
            for k, stage in enumerate(stages):
                if 0 <= t - k < count:
                    stage(t - k)
        att[at, :] = jnp.concatenate([atts[h] for h in range(count)], axis=0).T.astype(BF16)
        c, sn = cosr[:, at], -sinr[:, at]
        qt[:, at] = jnp.concatenate([turn(dqs[h] * (1.0 / math.sqrt(HD)), c, sn) for h in range(count)], axis=0).astype(BF16)

    @pl.loop(0, blocks)
    def _(i):
        lo = low_block(i)
        for n in range(1, MOST + 1):
            pl.when(i - lo + 1 == n)(functools.partial(attend, i, lo, n))
        out_copy(2, att, att_o, i).start()

    vec_ref[...] = jnp.zeros_like(vec_ref)
    sgp[...] = jnp.zeros_like(sgp)
    sgu[...] = jnp.zeros_like(sgu)

    def pair(v):
        high = v.astype(BF16)
        return high, (v - high.astype(F32)).astype(BF16)

    def h_copy(i):
        slot = lax.rem(i, 2)
        return pltpu.make_async_copy(hst.at[slot], h_o.at[block(i)], h_sem.at[slot])

    @pl.loop(0, blocks)
    def _(i):
        at = block(i)
        c, sn = cosr[:, at], -sinr[:, at]
        pieces = []
        for h in range(count):
            r = slice(h * HD, (h + 1) * HD)
            pieces += [qt[r, at], turn(dkt[r, at], c, sn).astype(BF16), dvt[r, at].astype(BF16)]
        gpb = jnp.concatenate(pieces, axis=0).T
        gp[at, :] = gpb
        out_copy(3, gp, gp_o, i).start()
        gub = gu[at, :]
        gs = dot_nt(gub, wu[...])
        gf = dot_nn(gpb, wqt[...])
        normed, _ = stats_of(xv[at, :].astype(F32))

        @pl.when(i >= 2)
        def _():
            h_copy(i - 2).wait()

        hot = jnp.where(seg_ref[:, at] == lax.broadcasted_iota(jnp.int32, (DOCS, BLK), 0), 1.0, 0.0).astype(BF16)
        sgu[...] += dot_nn(hot, gub)
        sgp[...] += dot_nn(hot, gpb)
        for n, g in ((2, gs), (0, gf)):
            high, low = pair(g * normed)
            vec_ref[n] += dot_nn(hot, high) + dot_nn(hot, low)
        hst[lax.rem(i, 2)] = (gf * g1 + gs * g2).astype(BF16)
        h_copy(i).start()

    for n, sums, mul in ((1, sgp, lambda v: dot_nn(v, wqt[...])), (3, sgu, lambda v: dot_nt(v, wu[...]))):
        high, low = pair(sums[...])
        vec_ref[n] = mul(high) + mul(low)

    pairs_of = ((first, gp, 1.0), (second, gu, 1.0))

    def gram_block(j, i, n):
        at, cols, size = block(i, n), block(j), n * BLK

        def gram(m):
            return dot_nt(m[at, :], m[cols, :])

        terms = None
        for a, b, plus in pairs_of:
            term = (gram(a) + plus) * gram(b)
            terms = term if terms is None else terms + term
        terms = terms + (gram(att) + gram(act) + share) * gram(dyv)
        row_at = lax.broadcasted_iota(jnp.int32, (size, BLK), 0) + i * BLK
        col_at = lax.broadcasted_iota(jnp.int32, (size, BLK), 1) + j * BLK
        weight = jnp.where(row_at > col_at, 2.0, jnp.where(row_at == col_at, 1.0, 0.0))
        terms = jnp.where(row_at < end[:, cols], terms * weight, 0.0)
        col_ref[:, cols] += jnp.sum(terms.reshape(size // 8, 8, BLK), axis=0)

    col_ref[...] = jnp.zeros_like(col_ref)

    @pl.loop(0, blocks)
    def _(j):
        total = high_block(j) - j + 1
        pl.loop(0, lax.div(total, 2))(lambda s: gram_block(j, j + 2 * s, 2))
        pl.when(lax.rem(total, 2) == 1)(lambda: gram_block(j, j + total - 1, 1))

    for i in (blocks - 2, blocks - 1):
        for c in (*t_copies(i), h_copy(i)):
            c.wait()

    @pl.loop(0, blocks)
    def _(i):
        for n, (src, out) in enumerate(outs):
            out_copy(n, src, out, i).wait()


def pre(share, seg, params, x, dy, wqkv, wup, wdown, wout):
    tokens, width = x.shape
    heads3, units, heads = wqkv.shape[1], wup.shape[1], wout.shape[0]
    blocks = tokens // BLK
    hbm, vmem = pl.BlockSpec(memory_space=pl.ANY), pl.BlockSpec(memory_space=pltpu.VMEM)
    V, D = pltpu.VMEM, pltpu.SemaphoreType.DMA
    t_shape, S = (width, tokens), jax.ShapeDtypeStruct
    return pl.pallas_call(
        functools.partial(pre_kernel, share),
        in_specs=[vmem] * 2 + [hbm] * 6,
        out_specs=[hbm] * 8 + [vmem] * 2,
        out_shape=[S(t_shape, BF16)] * 3 + [S((tokens, n), BF16) for n in (heads3, units, units, heads, width)] + [S((8, tokens), F32), S((4, DOCS, width), F32)],
        scratch_shapes=[V((tokens, width), BF16)] * 4 + [V((tokens, units), BF16)] * 2 + [V((tokens, heads3), BF16), V((tokens, heads), BF16)]
        + [V((heads, tokens), BF16)] * 4 + [V((tokens, heads), BF16)] * 2 + [V((heads, tokens), F32)] * 2
        + [V((heads3, width), BF16), V((width, units), BF16), V((units, width), BF16), V((heads, width), BF16), V((2, 3, width, BLK), BF16), V((2, BLK, width), BF16)]
        + [V((1, tokens), jnp.int32)] * 2 + [V((ROT // 2, tokens), F32)] * 2 + [V((heads3, 8), F32), V((DOCS, heads3), F32), V((DOCS, units), F32)]
        + [pltpu.SMEM((DOCS + 1,), jnp.int32)]
        + [D((blocks,)), D((blocks,)), D((4,)), D((2, 3)), D((2,)), D((4, blocks))],
        compiler_params=pltpu.CompilerParams(vmem_limit_bytes=63 * 1024 * 1024),
        name="pre",
    )(seg, params, x, dy, wqkv, wup, wdown, wout)


LOAD_AHEAD = 4
LAG = 3


def bit_of(index, bit):
    return lax.rem(lax.div(index, 2**bit), 2)


def across(index, bit):
    return index + (1 - 2 * bit_of(index, bit)) * 2**bit


def log2(n):
    return n.bit_length() - 1


def remote(src, dst, send, recv, axis, index):
    return pltpu.make_async_remote_copy(src_ref=src, dst_ref=dst, send_sem=send, recv_sem=recv, device_id={axis: index}, device_id_type=pl.DeviceIdType.MESH)


def tail_kernel(n, tp, w, vec_ref, col_ref, seg_ref, b1_ref, b2_ref, second_t, first_t, dy_t, gu, gp, act, att, h, x, dy, wdown, wout,
                gup_ref, gq_ref, gdown_ref, gout_ref, bo_ref, gi_ref, small_ref, norm_ref,
                at, b, snd, rcv, keep, oacc, hown, hs, hr, bs, br, wd, xr, dyr, trow, tcol, vsend, vrecv, bsum, smine, sall,
                at_sem, b_sem, w_sem, snd_sem, rcv_sem, hs_sem, hr_sem, bs_sem, br_sem, gs_sem, gr_sem, ss_sem, sr_sem, hown_sem, row_sem, gi_stage, bo_stage, out_sem):
    width, tokens = first_t.shape
    me, m = lax.axis_index("dp"), lax.axis_index("mp")
    nb, mb = log2(n), log2(tp)
    shard, rows_own = width // n, tokens // tp
    nu, nq, na, ne = (r.shape[1] // w for r in (gu, gp, act, att))
    units = nu + nq + na + ne

    barrier = pltpu.get_barrier_semaphore()
    for r in range(1, n):
        pl.semaphore_signal(barrier, inc=1, device_id={"dp": lax.rem(me + r, n)}, device_id_type=pl.DeviceIdType.MESH)
    for r in range(1, tp):
        pl.semaphore_signal(barrier, inc=1, device_id={"mp": lax.rem(m + r, tp)}, device_id_type=pl.DeviceIdType.MESH)
    pl.semaphore_wait(barrier, n - 1 + tp - 1)

    def vec_exchange(k):
        return remote(vsend.at[k], vrecv.at[k], gs_sem.at[k], gr_sem.at[k], "mp", across(m, k))

    hot = seg_ref[...] == lax.broadcasted_iota(jnp.int32, (DOCS, tokens), 0)
    mine = jnp.sum(jnp.where(hot, jnp.sum(col_ref[...], axis=0, keepdims=True), 0.0), axis=1, keepdims=True)
    vsend[0, :4] = vec_ref[...]
    vsend[0, 4] = jnp.broadcast_to(mine, (DOCS, width))
    vec_exchange(0).start()

    for j in range(tp // 2):
        there = 2 * j + 1 - bit_of(m, 0)
        remote(h.at[pl.ds(there * rows_own, rows_own)], hr[0].at[j], hs_sem.at[0, j], hr_sem.at[0, j], "mp", across(m, 0)).start()

    sources = (second_t, first_t, dy_t)

    def place(p):
        return sum(((p >> (nb - 1 - k)) & 1) << k for k in range(nb))

    def load_at(mat):
        for p in range(n):
            pltpu.make_async_copy(sources[mat].at[pl.ds(place(p) * shard, shard)], at.at[mat, pl.ds(p * shard, shard)], at_sem.at[mat]).start()

    def load_b(base, src):
        for i in range(src.shape[1] // w):
            pltpu.make_async_copy(src.at[:, pl.ds(i * w, w)], b.at[base + i], b_sem.at[base + i]).start()

    load_at(0)
    load_b(0, gu)
    load_at(1)
    load_b(nu, gp)
    load_at(2)
    load_b(nu + nq, act)
    load_b(nu + nq + na, att)
    split = act.shape[1]
    wd_copies = (pltpu.make_async_copy(wdown, wd.at[pl.ds(0, split)], w_sem.at[0]), pltpu.make_async_copy(wout, wd.at[pl.ds(split, wd.shape[0] - split)], w_sem.at[1]))
    own_at = pl.ds(m * rows_own, rows_own)
    row_copies = (pltpu.make_async_copy(x.at[own_at], xr, row_sem.at[0]), pltpu.make_async_copy(dy.at[own_at], dyr, row_sem.at[1]))
    hown_copies = [pltpu.make_async_copy(h.at[pl.ds((2 * j + bit_of(m, 0)) * rows_own, rows_own)], hown.at[j], hown_sem.at[j]) for j in range(tp // 2)]
    for c in (*wd_copies, *row_copies, *hown_copies):
        c.start()

    for k in range(mb):
        vec_exchange(k).wait_recv()
        vsend[k + 1] = vsend[k] + vrecv[k]
        if k + 1 < mb:
            vec_exchange(k + 1).start()
    squares = vsend[mb, 4, :, :1]
    for j in range(4):
        squares = squares + jnp.sum(vsend[mb, j] * vsend[mb, j], axis=1, keepdims=True)
    norm = jnp.sqrt(squares + NORM_EPS)
    norm_ref[...] = jnp.broadcast_to(norm, norm_ref.shape)
    clip = jnp.minimum(1.0, jnp.mean(norm, axis=0, keepdims=True) / norm)
    per_token = jnp.sum(jnp.where(hot, clip, 0.0), axis=0, keepdims=True)
    trow[...] = per_token
    tcol[...] = jnp.broadcast_to(per_token, (DOCS, tokens)).T
    smine[...] = jnp.zeros_like(smine)
    for j in range(4):
        smine[3 + j:4 + j, :] = jnp.sum(vsend[mb, j] * clip, axis=0, keepdims=True)

    orders = (tuple(range(nb)), tuple(range(1, nb)) + (0,))

    def z_first(u):
        return (u == 1) | (u == units - 3)

    def by_order(u, body):
        pl.when(jnp.logical_not(z_first(u)))(functools.partial(body, orders[0]))
        pl.when(z_first(u))(functools.partial(body, orders[1]))

    def matrix_of(u):
        return jnp.where(u >= nu, 1, 0) + jnp.where(u >= nu + nq, 1, 0)

    def exchange(order, k, u):
        return remote(snd[k].at[u], rcv[k].at[u], snd_sem.at[k, u], rcv_sem.at[k, u], "dp", across(me, order[k]))

    def pieces(bit, side):
        size = width >> (bit + 1)
        return [pl.ds(pl.multiple_of((2 * g + side) * size, size), size) for g in range(2**bit)], size

    def other_half(mat, clipped, u):
        pltpu.make_async_copy(gu.at[:, pl.ds(0, w)], b.at[u], b_sem.at[u]).wait()
        if clipped:
            scaled = b[u].astype(F32) * tcol[:, :1]
            b[u] = scaled.astype(BF16)
            bsum[u] = jnp.sum(scaled.reshape(tokens // 8, 8, w), axis=0)

        def send(order):
            away, size = pieces(order[0], 1 - bit_of(me, order[0]))
            for g, piece in enumerate(away):
                snd[0][u, g * size:(g + 1) * size, :] = dot_nn(at[mat, piece, :], b[u]).astype(BF16)

            @pl.when(u < LOAD_AHEAD)
            def _():
                exchange(order, 0, u).start()

        by_order(u, send)

    def at_ready(mat):
        pltpu.make_async_copy(sources[mat], at.at[mat], at_sem.at[mat]).wait()

    at_ready(0)
    pl.loop(0, nu)(lambda u: other_half(0, True, u))
    at_ready(1)
    pl.loop(nu, nu + nq)(lambda u: other_half(1, True, u))
    at_ready(2)
    for p in range(n):
        piece = pl.ds(p * shard, shard)
        scaled = at[2, piece, :].astype(F32) * trow[...]
        at[2, piece, :] = scaled.astype(BF16)
        folded = scaled[:, :128]
        for k in range(1, tokens // 128):
            folded = folded + scaled[:, k * 128:(k + 1) * 128]
        smine[2:3, place(p) * shard:(place(p) + 1) * shard] = jnp.sum(folded.T, axis=0, keepdims=True)
    pl.loop(nu + nq, units)(lambda u: other_half(2, False, u))

    for i in range(nq):
        smine[0:1, i * w:(i + 1) * w] = jnp.sum(bsum[nu + i], axis=0, keepdims=True)
    for i in range(nu):
        smine[1:2, i * w:(i + 1) * w] = jnp.sum(bsum[i], axis=0, keepdims=True)
    sall[me] = smine[...]
    for r in range(1, n):
        remote(smine, sall.at[me], ss_sem.at[r - 1], sr_sem.at[me], "dp", lax.rem(me + r, n)).start()

    chunk = min(rows_own, 256)
    for c in wd_copies:
        c.wait()

    def branch(owner, c, chunk=chunk):
        at_rows = pl.ds(pl.multiple_of(owner * rows_own + c * chunk, chunk), chunk)
        left = jnp.concatenate([b[nu + nq + i, at_rows, :] for i in range(na + ne)], axis=1)
        return dot_nn(left, wd[...])

    def chunks(body):
        pl.loop(0, rows_own // chunk)(lambda c: body(c, pl.ds(pl.multiple_of(c * chunk, chunk), chunk)))

    def slot(owner, k):
        return lax.div(owner, 2 ** (k + 1))

    for j in range(tp // 2):
        there = 2 * j + 1 - bit_of(m, 0)

        def first_send(c, rows_at):
            bs[0][j, rows_at, :] = branch(there, c).astype(BF16)

        chunks(first_send)
        remote(bs[0].at[j], br[0].at[j], bs_sem.at[0, j], br_sem.at[0, j], "mp", across(m, 0)).start()

    for c in hown_copies:
        c.wait()

    def wait_mp(k, buf, recv_sem, send_sem):
        for j in range(tp >> (k + 1)):
            remote(buf[k].at[j], buf[k].at[j], send_sem.at[k, j], recv_sem.at[k, j], "mp", across(m, k)).wait_recv()

    for k in range(1, mb):
        wait_mp(k - 1, hr, hr_sem, hs_sem)
        for j in range(tp >> (k + 1)):
            owner = (2 * j + 1 - bit_of(m, k)) * 2**k + lax.rem(m, 2**k)

            def h_send(c, rows_at):
                val = hown[slot(owner, 0), rows_at, :].astype(F32)
                for r in range(k):
                    val = val + hr[r][slot(owner, r), rows_at, :].astype(F32)
                hs[k - 1][j, rows_at, :] = val.astype(BF16)

            chunks(h_send)
            remote(hs[k - 1].at[j], hr[k].at[j], hs_sem.at[k, j], hr_sem.at[k, j], "mp", across(m, k)).start()
        wait_mp(k - 1, br, br_sem, bs_sem)
        for j in range(tp >> (k + 1)):
            owner = (2 * j + 1 - bit_of(m, k)) * 2**k + lax.rem(m, 2**k)

            def b_send(c, rows_at):
                val = branch(owner, c)
                for r in range(k):
                    val = val + br[r][slot(owner, r), rows_at, :].astype(F32)
                bs[k][j, rows_at, :] = val.astype(BF16)

            chunks(b_send)
            remote(bs[k].at[j], br[k].at[j], bs_sem.at[k, j], br_sem.at[k, j], "mp", across(m, k)).start()

    def split(val, pos, bit):
        size = val.shape[0] >> (pos + 1)
        low = [val[2 * g * size:(2 * g + 1) * size] for g in range(2**pos)]
        high = [val[(2 * g + 1) * size:(2 * g + 2) * size] for g in range(2**pos)]
        low, high = (v[0] if len(v) == 1 else jnp.concatenate(v, axis=0) for v in (low, high))
        return jnp.where(bit == 1, low, high), jnp.where(bit == 1, high, low)

    def later(k, u):
        def body(order):
            exchange(order, k, u).wait_recv()
            val = keep[k - 1][lax.rem(u, LAG + 1)] + rcv[k][u].astype(F32)
            if k == nb - 1:
                oacc[u] = val
                return
            pos = 1 if order[0] != 0 and k + 1 < nb - 1 else 0
            away, stay = split(val, pos, bit_of(me, order[k + 1]))
            snd[k + 1][u] = away.astype(BF16)
            keep[k][lax.rem(u, LAG + 1)] = stay
            exchange(order, k + 1, u).start()

        by_order(u, body)

    def first(u):
        mat = matrix_of(u)

        def body(order):
            exchange(order, 0, u).wait_recv()
            near, size = pieces(order[0], bit_of(me, order[0]))
            for g, piece in enumerate(near):
                val = dot_nn(at[mat, piece, :], b[u]) + rcv[0][u, g * size:(g + 1) * size, :].astype(F32)
                away, stay = split(val, 0, bit_of(me, order[1]))
                part = size // 2
                snd[1][u, g * part:(g + 1) * part, :] = away.astype(BF16)
                keep[0][lax.rem(u, LAG + 1), g * part:(g + 1) * part, :] = stay
            exchange(order, 1, u).start()

        by_order(u, body)

        @pl.when(u + LOAD_AHEAD < units)
        def _():
            by_order(u + LOAD_AHEAD, lambda order: exchange(order, 0, u + LOAD_AHEAD).start())

    def step(t):
        for k in range(nb - 1, 0, -1):
            pl.when((t >= k * LAG) & (t < units + k * LAG))(functools.partial(later, k, t - k * LAG))
        pl.when(t < units)(functools.partial(first, t))

    pl.loop(0, units)(step)

    for c in row_copies:
        c.wait()
    wait_mp(mb - 1, hr, hr_sem, hs_sem)
    wait_mp(mb - 1, br, br_sem, bs_sem)

    fine = min(rows_own, 128)

    def out_copies(c):
        spot = lax.rem(c, 2)
        to = pl.ds(pl.multiple_of(c * fine, fine), fine)
        return (pltpu.make_async_copy(gi_stage.at[spot], gi_ref.at[to], out_sem.at[0, spot]),
                pltpu.make_async_copy(bo_stage.at[spot], bo_ref.at[to], out_sem.at[1, spot]))

    def finish(c):
        spot = lax.rem(c, 2)
        rows_at = pl.ds(pl.multiple_of(c * fine, fine), fine)

        @pl.when(c >= 2)
        def _():
            for copy in out_copies(c - 2):
                copy.wait()

        val = hown[slot(m, 0), rows_at, :].astype(F32)
        for r in range(mb):
            val = val + hr[r][slot(m, r), rows_at, :].astype(F32)
        xs = xr[rows_at, :].astype(F32)
        normed, inv = stats_of(xs)
        back_x = inv * (val - jnp.mean(val, axis=-1, keepdims=True) - normed * jnp.mean(val * normed, axis=-1, keepdims=True))
        gi_stage[spot] = dyr[rows_at, :].astype(F32) + back_x
        out = branch(m, c, fine) + (xs + b1_ref[...].astype(F32) + b2_ref[...].astype(F32))
        for r in range(mb):
            out = out + br[r][slot(m, r), rows_at, :].astype(F32)
        bo_stage[spot] = out.astype(BF16)
        for copy in out_copies(c):
            copy.start()

    pl.loop(0, rows_own // fine)(finish)
    pl.loop(units, units + (nb - 1) * LAG)(step)

    for i in range(nu):
        gup_ref[:, i * w:(i + 1) * w] = oacc[i]
    for i in range(nq):
        gq_ref[:, i * w:(i + 1) * w] = oacc[nu + i]
    for i in range(na):
        gdown_ref[i * w:(i + 1) * w, :] = oacc[nu + nq + i].T
    for i in range(ne):
        gout_ref[i * w:(i + 1) * w, :] = oacc[nu + nq + na + i].T
    for r in range(1, n):
        src = lax.rem(me + r, n)
        remote(smine, sall.at[src], ss_sem.at[r - 1], sr_sem.at[src], "dp", src).wait_recv()
    total = sall[0]
    for r in range(1, n):
        total = total + sall[r]
    small_ref[...] = total

    for c in range(max(rows_own // fine - 2, 0), rows_own // fine):
        for copy in out_copies(c):
            copy.wait()

    @pl.loop(0, units)
    def _(u):
        for k in range(nb):
            exchange(orders[0], k, u).wait_send()

    for r in range(1, n):
        remote(smine, sall.at[me], ss_sem.at[r - 1], sr_sem.at[me], "dp", lax.rem(me + r, n)).wait_send()
    for k in range(mb):
        vec_exchange(k).wait_send()
    for k in range(mb):
        for j in range(tp >> (k + 1)):
            src_h = h.at[pl.ds(0, rows_own)] if k == 0 else hs[k - 1].at[j]
            remote(src_h, hr[k].at[j], hs_sem.at[k, j], hr_sem.at[k, j], "mp", across(m, k)).wait_send()
            remote(bs[k].at[j], br[k].at[j], bs_sem.at[k, j], br_sem.at[k, j], "mp", across(m, k)).wait_send()


def tail(n, tp, vec, col, seg, b1, b2, second_t, first_t, dy_t, gu, gp, act, att, h, x, dy, wdown, wout):
    width, tokens = first_t.shape
    widths = [a.shape[1] for a in (gu, gp, act, att)]
    w = BLK if all(v % BLK == 0 for v in widths) else BLK // 2
    units = sum(widths) // w
    nb, mb = log2(n), log2(tp)
    shard, own = width // n, tokens // tp
    hbm = pl.BlockSpec(memory_space=pl.ANY)
    vmem = pl.BlockSpec(memory_space=pltpu.VMEM)
    V, D = pltpu.VMEM, pltpu.SemaphoreType.DMA
    mp_bufs = lambda lo: [V((tp >> (k + 1), own, width), BF16) for k in range(lo, mb)]
    step_bufs = lambda: [V((units, width >> (k + 1), w), BF16) for k in range(nb)]
    return pl.pallas_call(
        functools.partial(tail_kernel, n, tp, w),
        in_specs=[vmem] * 5 + [hbm] * 12,
        out_specs=[vmem] * 4 + [hbm] * 2 + [vmem] * 2,
        out_shape=[jax.ShapeDtypeStruct(s, t) for s, t in (
            ((shard, widths[0]), F32), ((shard, widths[1]), F32), ((widths[2], shard), F32), ((widths[3], shard), F32),
            ((own, width), BF16), ((own, width), F32), ((8, width), F32), ((DOCS, 128), F32))],
        scratch_shapes=[
            V((3, width, tokens), BF16), V((units, tokens, w), BF16), step_bufs(), step_bufs(), [V((LAG + 1, width >> (k + 1), w), F32) for k in range(1, nb)],
            V((units, shard, w), F32), V((tp // 2, own, width), BF16), mp_bufs(1), mp_bufs(0), mp_bufs(0), mp_bufs(0),
            V((wdown.shape[0] + wout.shape[0], width), BF16), V((own, width), BF16), V((own, width), BF16), V((1, tokens), F32), V((tokens, DOCS), F32),
            V((mb + 1, 5, DOCS, width), F32), V((mb, 5, DOCS, width), F32), V((units, 8, w), F32), V((8, width), F32), V((n, 8, width), F32),
            D((3,)), D((units,)), D((2,)), D((nb, units)), D((nb, units)), D((mb, tp // 2)), D((mb, tp // 2)), D((mb, tp // 2)), D((mb, tp // 2)),
            D((mb,)), D((mb,)), D((n - 1,)), D((n,)), D((tp // 2,)), D((2,)), V((2, min(own, 128), width), F32), V((2, min(own, 128), width), BF16), D((2, 2))],
        compiler_params=pltpu.CompilerParams(collective_id=1, has_side_effects=True, vmem_limit_bytes=64 * 1024 * 1024 - 1024 * 1024),
        name="tail",
    )(vec, col, seg, b1, b2, second_t, first_t, dy_t, gu, gp, act, att, h, x, dy, wdown, wout)


def shards(block_input, segment_ids, cotangent, weight_qkv, bias_qkv, weight_out, bias_out, weight_up, bias_up, weight_down, bias_down,
           gain_first, shift_first, gain_second, shift_second):
    tp = lax.axis_size("mp")
    x, dy = block_input[0], cotangent[0]
    row = lambda v: v.reshape(1, -1)
    params = row(jnp.concatenate([bias_qkv, bias_up, gain_first, shift_first, gain_second, shift_second]))
    first_t, second_t, dy_t, gp, gu, act, att, h, col_sums, vec = pre(2.0 / tp, segment_ids, params, x, dy, weight_qkv, weight_up, weight_down, weight_out)
    g_up, g_qkv, g_down, g_out, block_output, grad_input, small, norms = tail(
        lax.axis_size("dp"), tp, vec, col_sums, segment_ids, row(bias_out), row(bias_down), second_t, first_t, dy_t, gu, gp, act, att, h, x, dy, weight_down, weight_out)
    b_out = small[2]
    return (block_output[None], grad_input[None], g_qkv, small[0, :g_qkv.shape[1]], g_out, b_out, g_up, small[1, :g_up.shape[1]],
            g_down, b_out, small[3], small[4], small[5], small[6], norms[:, 0][None])


def solution(mesh):
    placed = (P("dp", None, None), P("dp", None), P("dp", None, None), P(None, "mp"), P("mp"), P("mp", None), P(), P(None, "mp"), P("mp"), P("mp", None),
              P(), P(), P(), P(), P())
    return jax.shard_map(
        shards,
        mesh=mesh,
        in_specs=placed,
        out_specs=(P("dp", "mp", None), P("dp", "mp", None), P("dp", "mp"), P("mp"), P("mp", "dp"), P(), P("dp", "mp"), P("mp"), P("mp", "dp"), P(), P(),
                   P(), P(), P(), P("dp", None)),
        check_vma=False,
    )
```

```python
import functools
import math

import jax
import jax.numpy as jnp
from jax import lax
from jax.experimental import pallas as pl
from jax.experimental.pallas import tpu as pltpu
from jax.sharding import PartitionSpec as P

HD = 64
ROT = 16
DOCS = 8
BLK = 256
LN_EPS = 1e-05
NORM_EPS = 1e-06
NEG = -1e30
F32 = jnp.float32
BF16 = jnp.bfloat16
VMEM_LIMIT = 60 * 1024 * 1024

TAIL = (0.099163489, 0.109273513, 0.0348237317, 0.263242867, -0.249259412, 0.332377466, -0.089621649)


def dot_nn(a, b):
    return lax.dot_general(a, b, (((1,), (0,)), ((), ())), preferred_element_type=F32)


def dot_nt(a, b):
    return lax.dot_general(a, b, (((1,), (1,)), ((), ())), preferred_element_type=F32)


def stats_of(x):
    mean = jnp.mean(x, axis=-1, keepdims=True)
    centred = x - mean
    var = jnp.mean(centred * centred, axis=-1, keepdims=True)
    inv = lax.rsqrt(var + LN_EPS)
    return centred * inv, inv


def gelu_parts(u):
    e = jnp.exp(u * u * -0.5)
    t = 1.0 / (1.0 + 0.25 * jnp.abs(u))
    r = jnp.full_like(t, TAIL[-1])
    for c in TAIL[-2::-1]:
        r = r * t + c
    tail = r * t * e
    cdf = jnp.where(u >= 0.0, 1.0 - tail, tail)
    return u * cdf, cdf + u * (e * (1.0 / math.sqrt(2.0 * math.pi)))


def full(shape):
    return pl.BlockSpec(shape, lambda *_: (0,) * len(shape))


MOST = 5


STRIP = 16
HALF = BLK // 2


def pre_kernel(share, seg_ref, bqkv_ref, bup_ref, g1_ref, s1_ref, g2_ref, s2_ref, x, dy, wqkv, wup, wdown, wout,
               first_o, second_o, dy_o, gp_o, gu_o, act_o, att_o, h_o, col_ref, vec_ref,
               xv, dyv, first, second, act, gu, gp, att, qt, kt, vt, gat, kf, vf, dkt, dvt, wqt, wu, wd, wo, hst, start, end, cosr, sinr, bq, vec8, bias, ex, low, gprob, bounds,
               x_sem, dy_sem, w_sem, t_sem, h_sem, o_sem):
    tokens, width = xv.shape
    units, heads3 = act.shape[1], gp.shape[1]
    heads = att.shape[1]
    count = heads // HD
    blocks = tokens // BLK

    def block(i, n=1):
        return pl.ds(pl.multiple_of(i * BLK, BLK), n * BLK)

    def x_copy(i):
        return pltpu.make_async_copy(x.at[block(i)], xv.at[block(i)], x_sem.at[i])

    def dy_copy(i):
        return pltpu.make_async_copy(dy.at[block(i)], dyv.at[block(i)], dy_sem.at[i])

    raw = gp.at[pl.ds(0, width)]
    w_copies = [pltpu.make_async_copy(a, b, w_sem.at[n]) for n, (a, b) in enumerate(((wqkv, raw), (wout, wo), (wup, wu), (wdown, wd)))]
    w_copies[0].start()
    x_copy(0).start()
    dy_copy(0).start()
    for c in w_copies[1:]:
        c.start()
    for i in range(1, blocks):
        x_copy(i).start()
        dy_copy(i).start()

    seg = seg_ref[...]
    edges = [jnp.sum((seg < d).astype(jnp.int32)) for d in range(1, DOCS)]
    bounds[0] = 0
    bounds[DOCS] = tokens
    begin, finish = jnp.zeros_like(seg), jnp.full_like(seg, tokens)
    for d in range(1, DOCS):
        bounds[d] = edges[d - 1]
        begin = jnp.where(seg >= d, edges[d - 1], begin)
    for d in range(DOCS - 1, 0, -1):
        finish = jnp.where(seg < d, edges[d - 1], finish)
    start[...] = begin
    end[...] = finish
    half = ROT // 2
    at_token = lax.broadcasted_iota(jnp.int32, (half, tokens), 1)
    freq = jnp.exp(lax.broadcasted_iota(jnp.int32, (half, tokens), 0).astype(F32) * (2.0 / ROT) * -math.log(10000.0))
    angle = (at_token - begin).astype(F32) * freq
    cosr[...] = jnp.cos(angle)
    sinr[...] = jnp.sin(angle)
    bqkv, bup, g1, s1, g2, s2 = (r[...].astype(F32).reshape(1, -1) for r in (bqkv_ref, bup_ref, g1_ref, s1_ref, g2_ref, s2_ref))
    bq[...] = jnp.broadcast_to(bqkv, (8, heads3)).T
    w_copies[0].wait()
    wqt[...] = raw[...].T
    for c in w_copies[1:]:
        c.wait()

    def t_copies(i):
        return [pltpu.make_async_copy(low.at[n, pl.ds(0, width)], out.at[:, block(i)], t_sem.at[n]) for n, out in enumerate((first_o, second_o, dy_o))]

    def out_copy(n, src, out, i):
        return pltpu.make_async_copy(src.at[block(i)], out.at[block(i)], o_sem.at[n, i])

    outs = ((act, act_o), (gu, gu_o), (att, att_o), (gp, gp_o))

    def turn(v, c, s):
        a, b = v[:half], v[half:ROT]
        return jnp.concatenate([a * c - b * s, b * c + a * s, v[ROT:]], axis=0)

    def norm_block(i):
        for q in range(0, BLK, STRIP):
            at = pl.ds(pl.multiple_of(i * BLK + q, STRIP), STRIP)
            normed, _ = stats_of(xv[at, :].astype(F32))
            first[at, :] = (normed * g1 + s1).astype(BF16)
            second[at, :] = (normed * g2 + s2).astype(BF16)

    x_copy(0).wait()
    norm_block(0)

    @pl.loop(0, blocks)
    def _(i):
        at = block(i)
        after = jnp.minimum(i + 1, blocks - 1)
        dy_copy(i).wait()

        @pl.when(i + 1 < blocks)
        def _():
            x_copy(i + 1).wait()

        chunk = min(256, units)

        def ups(c):
            return dot_nn(second[at, :], wu[:, c:c + chunk]), dot_nt(dyv[at, :], wd[c:c + chunk, :])

        def gelu(c, made):
            for q in range(0, BLK, STRIP):
                strip = pl.ds(pl.multiple_of(i * BLK + q, STRIP), STRIP)
                value, slope = gelu_parts(made[0][q:q + STRIP] + bup[:, c:c + chunk])
                act[strip, c:c + chunk] = value.astype(BF16)
                gu[strip, c:c + chunk] = (made[1][q:q + STRIP] * slope).astype(BF16)

        pt = dot_nt(wqt[...], first[at, :])
        made = ups(0)
        norm_block(after)
        for c in range(chunk, units, chunk):
            later = ups(c)
            gelu(c - chunk, made)
            made = later
        gat[:, at] = dot_nt(wo[...], dyv[at, :]).astype(BF16)
        gelu(units - chunk, made)

        @pl.when(i >= 1)
        def _():
            for copy in t_copies(i - 1):
                copy.wait()

        for n, rows_in in enumerate((first, second, dyv)):
            low[n, :width] = rows_in[at, :].T
        c, s = cosr[:, at], sinr[:, at]
        ks, vs = [], []
        for h in range(count):
            o = h * 3 * HD
            part = [pt[o + n * HD:o + (n + 1) * HD] + bq[o + n * HD:o + (n + 1) * HD, :1] for n in range(3)]
            qt[h * HD:(h + 1) * HD, at] = (turn(part[0], c, s).astype(BF16).astype(F32) * (1.0 / math.sqrt(HD))).astype(BF16)
            ks.append(turn(part[1], c, s).astype(BF16))
            vs.append(part[2].astype(BF16))
            kt[h * HD:(h + 1) * HD, at] = ks[h]
            vt[h * HD:(h + 1) * HD, at] = vs[h]
        kb, vb = jnp.concatenate(ks, axis=0), jnp.concatenate(vs, axis=0)
        kf[at, :] = kb.T
        vf[at, :] = vb.T
        for copy in (*t_copies(i), out_copy(0, act, act_o, i), out_copy(1, gu, gu_o, i)):
            copy.start()

    for copy in t_copies(blocks - 1):
        copy.wait()

    dkt[...] = jnp.zeros_like(dkt)
    dvt[...] = jnp.zeros_like(dvt)

    def low_block(i):
        lowest = 0
        for d in range(1, DOCS):
            lowest = jnp.maximum(lowest, jnp.where(bounds[d] <= i * BLK, bounds[d], 0))
        return lax.div(lowest, BLK)

    def end_of(j):
        last = j * BLK + BLK - 1
        highest = tokens
        for d in range(1, DOCS):
            highest = jnp.minimum(highest, jnp.where(bounds[d] > last, bounds[d], tokens))
        return highest

    def attend(i, lo, n):
        at, keys, size = block(i), block(lo, n), n * BLK
        strips = [slice(r, r + STRIP) for r in range(0, size, STRIP)]
        k_off = lax.broadcasted_iota(jnp.int32, (STRIP, BLK), 0)
        last = i * BLK - lo * BLK + lax.broadcasted_iota(jnp.int32, (1, BLK), 1)
        lead = start[:, at] - lo * BLK
        for r in strips:
            k_at = k_off + r.start
            bias[r] = jnp.where((k_at <= last) & (k_at >= lead), 0.0, NEG)
        blank = jnp.zeros((HD, BLK), BF16)
        span = min(2 * HD, heads)

        def spread(v, h):
            return jnp.concatenate([v if g == h % (span // HD) else blank for g in range(span // HD)], axis=0)

        def lanes(h):
            return slice(h * HD // span * span, h * HD // span * span + span)

        def rows_of(h):
            return slice(h * HD, (h + 1) * HD)

        atts, dqs, share_of = {}, {}, {}

        def stage_a(h):
            ex[h, :size] = dot_nn(kf[keys, lanes(h)], spread(qt[rows_of(h), at], h))

        def stage_b(h):
            best = jnp.full((STRIP, BLK), NEG, F32)
            for r in strips:
                s = ex[h, r] + bias[r]
                ex[h, r] = s
                best = jnp.maximum(best, s)
            best = jnp.max(best, axis=0, keepdims=True)
            total = jnp.zeros((STRIP, BLK), F32)
            for r in strips:
                e = jnp.exp(ex[h, r] - best)
                ex[h, r] = e
                total = total + e
            share_of[h] = 1.0 / jnp.sum(total, axis=0, keepdims=True)
            for r in strips:
                low[h, r] = (ex[h, r] * share_of[h]).astype(BF16)

        def stage_c(h):
            atts[h] = dot_nn(vt[rows_of(h), keys], low[h, :size])
            gprob[h % 2, :size] = dot_nn(vf[keys, lanes(h)], spread(gat[rows_of(h), at], h))
            dvt[rows_of(h), keys] += dot_nt(gat[rows_of(h), at], low[h, :size])

        def stage_d(h):
            delta = jnp.sum(atts[h] * gat[rows_of(h), at].astype(F32), axis=0, keepdims=True)
            for r in strips:
                low[h, r] = (ex[h, r] * share_of[h] * (gprob[h % 2, r] - delta)).astype(BF16)

        def stage_e(h):
            dqs[h] = dot_nn(kt[rows_of(h), keys], low[h, :size])
            dkt[rows_of(h), keys] += dot_nt(qt[rows_of(h), at], low[h, :size])

        stages = (stage_a, stage_b, stage_c, stage_d, stage_e)
        for t in range(count + len(stages) - 1):
            for k, stage in enumerate(stages):
                if 0 <= t - k < count:
                    stage(t - k)
        att[at, :] = jnp.concatenate([atts[h] for h in range(count)], axis=0).T.astype(BF16)
        c, sn = cosr[:, at], -sinr[:, at]
        qt[:, at] = jnp.concatenate([turn(dqs[h] * (1.0 / math.sqrt(HD)), c, sn) for h in range(count)], axis=0).astype(BF16)

    @pl.loop(0, blocks)
    def _(i):
        lo = low_block(i)
        for n in range(1, MOST + 1):
            pl.when(i - lo + 1 == n)(functools.partial(attend, i, lo, n))
        out_copy(2, att, att_o, i).start()

    vec8[...] = jnp.zeros_like(vec8)
    chunk = min(256, width)

    def spare(what, c, strip):
        k = c // chunk * 3 + what
        return ex.at[k % count, pl.ds(k // count * BLK + strip.start, strip.stop - strip.start)]

    def h_copy(i):
        slot = lax.rem(i, 2)
        return pltpu.make_async_copy(hst.at[slot], h_o.at[block(i)], h_sem.at[slot])

    def doc_of(t):
        return sum(jnp.where(bounds[d] <= t, 1, 0) for d in range(1, DOCS))

    @pl.loop(0, blocks)
    def _(i):
        at = block(i)
        c, sn = cosr[:, at], -sinr[:, at]
        pieces = []
        for h in range(count):
            r = slice(h * HD, (h + 1) * HD)
            pieces += [qt[r, at], turn(dkt[r, at], c, sn).astype(BF16), dvt[r, at].astype(BF16)]
        gp[at, :] = jnp.concatenate(pieces, axis=0).T
        out_copy(3, gp, gp_o, i).start()

        @pl.when(i >= 2)
        def _():
            h_copy(i - 2).wait()

        slot = lax.rem(i, 2)

        def grads(c):
            return dot_nt(gu[at, :], wu[c:c + chunk, :]), dot_nn(gp[at, :], wqt[:, c:c + chunk])

        def use(c, made):
            cut = slice(c, c + chunk)
            for q in range(0, BLK, STRIP):
                strip = slice(q, q + STRIP)
                gs, gf = made[0][strip], made[1][strip]
                spare(0, c, strip)[...] = gf
                spare(1, c, strip)[...] = gs
                hst[slot, strip, cut] = (gf * g1[:, cut] + gs * g2[:, cut]).astype(BF16)

        made = grads(0)
        for q in range(0, BLK, STRIP):
            normed, _ = stats_of(xv[pl.ds(pl.multiple_of(i * BLK + q, STRIP), STRIP), :].astype(F32))
            for c in range(0, width, chunk):
                spare(2, c, slice(q, q + STRIP))[...] = normed[:, c:c + chunk]
        for c in range(chunk, width, chunk):
            later = grads(c)
            use(c - chunk, made)
            made = later
        use(width - chunk, made)
        h_copy(i).start()
        at_row = lax.broadcasted_iota(jnp.int32, (STRIP, chunk), 0)

        @pl.loop(doc_of(i * BLK), doc_of(i * BLK + BLK - 1) + 1)
        def _(d):
            low_row, high_row = bounds[d] - i * BLK, bounds[d + 1] - i * BLK
            for c in range(0, width, chunk):
                sums = [jnp.zeros((STRIP, chunk), F32)] * 4
                for q in range(0, BLK, STRIP):
                    strip = slice(q, q + STRIP)
                    inside = (at_row >= low_row - q) & (at_row < high_row - q)
                    gf, gs = (jnp.where(inside, spare(k, c, strip)[...], 0.0) for k in range(2))
                    normed = spare(2, c, strip)[...]
                    sums = [s + v for s, v in zip(sums, (gf * normed, gf, gs * normed, gs))]
                for n in range(4):
                    vec8[n, d, :, c:c + chunk] += sums[n][:8] + sums[n][8:]

    vec_ref[...] = jnp.sum(vec8[...], axis=2)

    pairs_of = ((first, gp, 1.0), (second, gu, 1.0))

    def gram_block(j, first_row, size):
        at, cols = pl.ds(pl.multiple_of(first_row, HALF), size), block(j)

        def gram(m):
            return dot_nt(m[at, :], m[cols, :])

        grams = [(gram(a), plus, gram(b)) for a, b, plus in pairs_of] + [(gram(att) + gram(act), share, gram(dyv))]
        ahead = lax.broadcasted_iota(jnp.int32, (STRIP, BLK), 0) - lax.broadcasted_iota(jnp.int32, (STRIP, BLK), 1)
        reach = end[:, cols] - first_row
        row_off = lax.broadcasted_iota(jnp.int32, (STRIP, BLK), 0)
        total = jnp.zeros((STRIP, BLK), F32)
        for r in range(0, size, STRIP):
            terms = None
            for a, plus, b in grams:
                term = (a[r:r + STRIP] + plus) * b[r:r + STRIP]
                terms = term if terms is None else terms + term
            gap = ahead + (first_row - j * BLK + r)
            weight = jnp.where(gap > 0, 2.0, jnp.where(gap == 0, 1.0, 0.0))
            total = total + jnp.where(row_off + r < reach, terms * weight, 0.0)
        col_ref[:, cols] += total[:8] + total[8:]

    col_ref[...] = jnp.zeros_like(col_ref)

    @pl.loop(0, blocks)
    def _(j):
        total = lax.div(end_of(j) - j * BLK + HALF - 1, HALF)
        pl.loop(0, lax.div(total, 4))(lambda s: gram_block(j, j * BLK + s * 4 * HALF, 4 * HALF))
        for n in range(1, 4):
            pl.when(lax.rem(total, 4) == n)(lambda n=n: gram_block(j, j * BLK + (total - n) * HALF, n * HALF))

    for i in (blocks - 2, blocks - 1):
        h_copy(i).wait()

    @pl.loop(0, blocks)
    def _(i):
        for n, (src, out) in enumerate(outs):
            out_copy(n, src, out, i).wait()


def pre(share, seg, params, x, dy, wqkv, wup, wdown, wout):
    tokens, width = x.shape
    heads3, units, heads = wqkv.shape[1], wup.shape[1], wout.shape[0]
    blocks = tokens // BLK
    hbm, vmem = pl.BlockSpec(memory_space=pl.ANY), pl.BlockSpec(memory_space=pltpu.VMEM)
    V, D = pltpu.VMEM, pltpu.SemaphoreType.DMA
    t_shape, S = (width, tokens), jax.ShapeDtypeStruct
    return pl.pallas_call(
        functools.partial(pre_kernel, share),
        in_specs=[vmem] * 7 + [hbm] * 6,
        out_specs=[hbm] * 8 + [vmem] * 2,
        out_shape=[S(t_shape, BF16)] * 3 + [S((tokens, n), BF16) for n in (heads3, units, units, heads, width)] + [S((8, tokens), F32), S((4, DOCS, width), F32)],
        scratch_shapes=[V((tokens, width), BF16)] * 4 + [V((tokens, units), BF16)] * 2 + [V((tokens, heads3), BF16), V((tokens, heads), BF16)]
        + [V((heads, tokens), BF16)] * 4 + [V((tokens, heads), BF16)] * 2 + [V((heads, tokens), F32)] * 2
        + [V((heads3, width), BF16), V((width, units), BF16), V((units, width), BF16), V((heads, width), BF16), V((2, BLK, width), BF16)]
        + [V((1, tokens), jnp.int32)] * 2 + [V((ROT // 2, tokens), F32)] * 2 + [V((heads3, 8), F32), V((4, DOCS, 8, width), F32)]
        + [V((MOST * BLK, BLK), F32), V((heads // HD, max(MOST, -(-3 * width // BLK // (heads // HD))) * BLK, BLK), F32), V((max(heads // HD, 3), MOST * BLK, BLK), BF16), V((2, MOST * BLK, BLK), F32)]
        + [pltpu.SMEM((DOCS + 1,), jnp.int32)]
        + [D((blocks,)), D((blocks,)), D((4,)), D((3,)), D((2,)), D((4, blocks))],
        compiler_params=pltpu.CompilerParams(vmem_limit_bytes=63 * 1024 * 1024),
        name="pre",
    )(seg, *params, x, dy, wqkv, wup, wdown, wout)


LOAD_AHEAD = 4
LAG = 3


def bit_of(index, bit):
    return lax.rem(lax.div(index, 2**bit), 2)


def across(index, bit):
    return index + (1 - 2 * bit_of(index, bit)) * 2**bit


def log2(n):
    return n.bit_length() - 1


def remote(src, dst, send, recv, axis, index):
    return pltpu.make_async_remote_copy(src_ref=src, dst_ref=dst, send_sem=send, recv_sem=recv, device_id={axis: index}, device_id_type=pl.DeviceIdType.MESH)


def tail_kernel(n, tp, w, vec_ref, col_ref, seg_ref, b1_ref, b2_ref, second_t, first_t, dy_t, gu, gp, act, att, h, x, dy, wdown, wout,
                gup_ref, gq_ref, gdown_ref, gout_ref, bo_ref, gi_ref, small_ref, norm_ref,
                at, b, snd, rcv, keep, oacc, hown, hs, hr, bs, br, wd, xr, dyr, trow, tcol, vsend, vrecv, bsum, smine, sall,
                at_sem, b_sem, w_sem, snd_sem, rcv_sem, hs_sem, hr_sem, bs_sem, br_sem, gs_sem, gr_sem, ss_sem, sr_sem, hown_sem, row_sem, gi_stage, bo_stage, out_sem):
    width, tokens = first_t.shape
    me, m = lax.axis_index("dp"), lax.axis_index("mp")
    nb, mb = log2(n), log2(tp)
    shard, rows_own = width // n, tokens // tp
    nu, nq, na, ne = (r.shape[1] // w for r in (gu, gp, act, att))
    units = nu + nq + na + ne

    barrier = pltpu.get_barrier_semaphore()
    for r in range(1, n):
        pl.semaphore_signal(barrier, inc=1, device_id={"dp": lax.rem(me + r, n)}, device_id_type=pl.DeviceIdType.MESH)
    for r in range(1, tp):
        pl.semaphore_signal(barrier, inc=1, device_id={"mp": lax.rem(m + r, tp)}, device_id_type=pl.DeviceIdType.MESH)
    pl.semaphore_wait(barrier, n - 1 + tp - 1)

    def vec_exchange(k):
        return remote(vsend.at[k], vrecv.at[k], gs_sem.at[k], gr_sem.at[k], "mp", across(m, k))

    hot = seg_ref[...] == lax.broadcasted_iota(jnp.int32, (DOCS, tokens), 0)
    mine = jnp.sum(jnp.where(hot, jnp.sum(col_ref[...], axis=0, keepdims=True), 0.0), axis=1, keepdims=True)
    vsend[0, :4] = vec_ref[...]
    vsend[0, 4] = jnp.broadcast_to(mine, (DOCS, width))
    vec_exchange(0).start()

    for j in range(tp // 2):
        there = 2 * j + 1 - bit_of(m, 0)
        remote(h.at[pl.ds(there * rows_own, rows_own)], hr[0].at[j], hs_sem.at[0, j], hr_sem.at[0, j], "mp", across(m, 0)).start()

    sources = (second_t, first_t, dy_t)

    def place(p):
        return sum(((p >> (nb - 1 - k)) & 1) << k for k in range(nb))

    def load_at(mat):
        for p in range(n):
            pltpu.make_async_copy(sources[mat].at[pl.ds(place(p) * shard, shard)], at.at[mat, pl.ds(p * shard, shard)], at_sem.at[mat]).start()

    def load_b(base, src):
        for i in range(src.shape[1] // w):
            pltpu.make_async_copy(src.at[:, pl.ds(i * w, w)], b.at[base + i], b_sem.at[base + i]).start()

    load_at(0)
    load_b(0, gu)
    load_at(1)
    load_b(nu, gp)
    load_at(2)
    load_b(nu + nq, act)
    load_b(nu + nq + na, att)
    split = act.shape[1]
    wd_copies = (pltpu.make_async_copy(wdown, wd.at[pl.ds(0, split)], w_sem.at[0]), pltpu.make_async_copy(wout, wd.at[pl.ds(split, wd.shape[0] - split)], w_sem.at[1]))
    own_at = pl.ds(m * rows_own, rows_own)
    row_copies = (pltpu.make_async_copy(x.at[own_at], xr, row_sem.at[0]), pltpu.make_async_copy(dy.at[own_at], dyr, row_sem.at[1]))
    hown_copies = [pltpu.make_async_copy(h.at[pl.ds((2 * j + bit_of(m, 0)) * rows_own, rows_own)], hown.at[j], hown_sem.at[j]) for j in range(tp // 2)]
    for c in (*wd_copies, *row_copies, *hown_copies):
        c.start()

    for k in range(mb):
        vec_exchange(k).wait_recv()
        vsend[k + 1] = vsend[k] + vrecv[k]
        if k + 1 < mb:
            vec_exchange(k + 1).start()
    squares = vsend[mb, 4, :, :1]
    for j in range(4):
        squares = squares + jnp.sum(vsend[mb, j] * vsend[mb, j], axis=1, keepdims=True)
    norm = jnp.sqrt(squares + NORM_EPS)
    norm_ref[...] = jnp.broadcast_to(norm, norm_ref.shape)
    clip = jnp.minimum(1.0, jnp.mean(norm, axis=0, keepdims=True) / norm)
    per_token = jnp.sum(jnp.where(hot, clip, 0.0), axis=0, keepdims=True)
    trow[...] = per_token
    tcol[...] = jnp.broadcast_to(per_token, (DOCS, tokens)).T
    smine[...] = jnp.zeros_like(smine)
    for j in range(4):
        smine[3 + j:4 + j, :] = jnp.sum(vsend[mb, j] * clip, axis=0, keepdims=True)

    orders = (tuple(range(nb)), tuple(range(1, nb)) + (0,))

    def z_first(u):
        return (u == 1) | (u == units - 3)

    def by_order(u, body):
        pl.when(jnp.logical_not(z_first(u)))(functools.partial(body, orders[0]))
        pl.when(z_first(u))(functools.partial(body, orders[1]))

    def matrix_of(u):
        return jnp.where(u >= nu, 1, 0) + jnp.where(u >= nu + nq, 1, 0)

    def exchange(order, k, u):
        return remote(snd[k].at[u], rcv[k].at[u], snd_sem.at[k, u], rcv_sem.at[k, u], "dp", across(me, order[k]))

    def pieces(bit, side):
        size = width >> (bit + 1)
        return [pl.ds(pl.multiple_of((2 * g + side) * size, size), size) for g in range(2**bit)], size

    def other_half(mat, clipped, u):
        pltpu.make_async_copy(gu.at[:, pl.ds(0, w)], b.at[u], b_sem.at[u]).wait()
        if clipped:
            scaled = b[u].astype(F32) * tcol[:, :1]
            b[u] = scaled.astype(BF16)
            bsum[u] = jnp.sum(scaled.reshape(tokens // 8, 8, w), axis=0)

        def send(order):
            away, size = pieces(order[0], 1 - bit_of(me, order[0]))
            for g, piece in enumerate(away):
                snd[0][u, g * size:(g + 1) * size, :] = dot_nn(at[mat, piece, :], b[u]).astype(BF16)

            @pl.when(u < LOAD_AHEAD)
            def _():
                exchange(order, 0, u).start()

        by_order(u, send)

    def at_ready(mat):
        pltpu.make_async_copy(sources[mat], at.at[mat], at_sem.at[mat]).wait()

    at_ready(0)
    pl.loop(0, nu)(lambda u: other_half(0, True, u))
    at_ready(1)
    pl.loop(nu, nu + nq)(lambda u: other_half(1, True, u))
    at_ready(2)
    for p in range(n):
        piece = pl.ds(p * shard, shard)
        scaled = at[2, piece, :].astype(F32) * trow[...]
        at[2, piece, :] = scaled.astype(BF16)
        folded = scaled[:, :128]
        for k in range(1, tokens // 128):
            folded = folded + scaled[:, k * 128:(k + 1) * 128]
        smine[2:3, place(p) * shard:(place(p) + 1) * shard] = jnp.sum(folded.T, axis=0, keepdims=True)
    pl.loop(nu + nq, units)(lambda u: other_half(2, False, u))

    for i in range(nq):
        smine[0:1, i * w:(i + 1) * w] = jnp.sum(bsum[nu + i], axis=0, keepdims=True)
    for i in range(nu):
        smine[1:2, i * w:(i + 1) * w] = jnp.sum(bsum[i], axis=0, keepdims=True)
    sall[me] = smine[...]
    for r in range(1, n):
        remote(smine, sall.at[me], ss_sem.at[r - 1], sr_sem.at[me], "dp", lax.rem(me + r, n)).start()

    chunk = min(rows_own, 256)
    def branch(owner, c, chunk=chunk):
        at_rows = pl.ds(pl.multiple_of(owner * rows_own + c * chunk, chunk), chunk)
        left = jnp.concatenate([b[nu + nq + i, at_rows, :] for i in range(na + ne)], axis=1)
        return dot_nn(left, wd[...])

    def chunks(body):
        pl.loop(0, rows_own // chunk)(lambda c: body(c, pl.ds(pl.multiple_of(c * chunk, chunk), chunk)))

    def slot(owner, k):
        return lax.div(owner, 2 ** (k + 1))

    def wait_mp(k, buf, recv_sem, send_sem):
        for j in range(tp >> (k + 1)):
            remote(buf[k].at[j], buf[k].at[j], send_sem.at[k, j], recv_sem.at[k, j], "mp", across(m, k)).wait_recv()

    def owner_of(k, j):
        return (2 * j + 1 - bit_of(m, k)) * 2**k + lax.rem(m, 2**k)

    def h_task(k, j):
        if j == 0:
            if k == 1:
                for c in hown_copies:
                    c.wait()
            wait_mp(k - 1, hr, hr_sem, hs_sem)
        owner = owner_of(k, j)

        def h_send(c, rows_at):
            val = hown[slot(owner, 0), rows_at, :].astype(F32)
            for r in range(k):
                val = val + hr[r][slot(owner, r), rows_at, :].astype(F32)
            hs[k - 1][j, rows_at, :] = val.astype(BF16)

        chunks(h_send)
        remote(hs[k - 1].at[j], hr[k].at[j], hs_sem.at[k, j], hr_sem.at[k, j], "mp", across(m, k)).start()

    def b_task(k, j):
        if k == 0 and j == 0:
            for c in wd_copies:
                c.wait()
        if k > 0 and j == 0:
            wait_mp(k - 1, br, br_sem, bs_sem)
        owner = owner_of(k, j)

        def b_send(c, rows_at):
            val = branch(owner, c)
            for r in range(k):
                val = val + br[r][slot(owner, r), rows_at, :].astype(F32)
            bs[k][j, rows_at, :] = val.astype(BF16)

        chunks(b_send)
        remote(bs[k].at[j], br[k].at[j], bs_sem.at[k, j], br_sem.at[k, j], "mp", across(m, k)).start()

    tasks = [functools.partial(h_task, 1, j) for j in range(tp // 4)] + [functools.partial(b_task, 0, j) for j in range(tp // 2)]
    for k in range(1, mb):
        tasks += [functools.partial(h_task, k, j) for j in range(tp >> (k + 1)) if k > 1]
        tasks += [functools.partial(b_task, k, j) for j in range(tp >> (k + 1))]

    def split(val, pos, bit):
        size = val.shape[0] >> (pos + 1)
        low = [val[2 * g * size:(2 * g + 1) * size] for g in range(2**pos)]
        high = [val[(2 * g + 1) * size:(2 * g + 2) * size] for g in range(2**pos)]
        low, high = (v[0] if len(v) == 1 else jnp.concatenate(v, axis=0) for v in (low, high))
        return jnp.where(bit == 1, low, high), jnp.where(bit == 1, high, low)

    def later(k, u):
        def body(order):
            exchange(order, k, u).wait_recv()
            val = keep[k - 1][lax.rem(u, LAG + 1)] + rcv[k][u].astype(F32)
            if k == nb - 1:
                oacc[u] = val
                return
            pos = 1 if order[0] != 0 and k + 1 < nb - 1 else 0
            away, stay = split(val, pos, bit_of(me, order[k + 1]))
            snd[k + 1][u] = away.astype(BF16)
            keep[k][lax.rem(u, LAG + 1)] = stay
            exchange(order, k + 1, u).start()

        by_order(u, body)

    def first(u):
        mat = matrix_of(u)

        def body(order):
            exchange(order, 0, u).wait_recv()
            near, size = pieces(order[0], bit_of(me, order[0]))
            for g, piece in enumerate(near):
                val = dot_nn(at[mat, piece, :], b[u]) + rcv[0][u, g * size:(g + 1) * size, :].astype(F32)
                away, stay = split(val, 0, bit_of(me, order[1]))
                part = size // 2
                snd[1][u, g * part:(g + 1) * part, :] = away.astype(BF16)
                keep[0][lax.rem(u, LAG + 1), g * part:(g + 1) * part, :] = stay
            exchange(order, 1, u).start()

        by_order(u, body)

        @pl.when(u + LOAD_AHEAD < units)
        def _():
            by_order(u + LOAD_AHEAD, lambda order: exchange(order, 0, u + LOAD_AHEAD).start())

    def step(t):
        for k in range(nb - 1, 0, -1):
            pl.when((t >= k * LAG) & (t < units + k * LAG))(functools.partial(later, k, t - k * LAG))
        pl.when(t < units)(functools.partial(first, t))
        for spot, task in enumerate(tasks):
            pl.when(t == min(spot, units - 1))(task)

    pl.loop(0, units)(step)

    for c in row_copies:
        c.wait()
    wait_mp(mb - 1, hr, hr_sem, hs_sem)
    wait_mp(mb - 1, br, br_sem, bs_sem)

    fine = min(rows_own, 128)
    bias = (b1_ref[...].astype(F32) + b2_ref[...].astype(F32)).reshape(1, width)

    def out_copies(c):
        spot = lax.rem(c, 2)
        to = pl.ds(pl.multiple_of(c * fine, fine), fine)
        return (pltpu.make_async_copy(gi_stage.at[spot], gi_ref.at[to], out_sem.at[0, spot]),
                pltpu.make_async_copy(bo_stage.at[spot], bo_ref.at[to], out_sem.at[1, spot]))

    def finish(c):
        spot = lax.rem(c, 2)
        rows_at = pl.ds(pl.multiple_of(c * fine, fine), fine)

        @pl.when(c >= 2)
        def _():
            for copy in out_copies(c - 2):
                copy.wait()

        val = hown[slot(m, 0), rows_at, :].astype(F32)
        for r in range(mb):
            val = val + hr[r][slot(m, r), rows_at, :].astype(F32)
        xs = xr[rows_at, :].astype(F32)
        normed, inv = stats_of(xs)
        back_x = inv * (val - jnp.mean(val, axis=-1, keepdims=True) - normed * jnp.mean(val * normed, axis=-1, keepdims=True))
        gi_stage[spot] = dyr[rows_at, :].astype(F32) + back_x
        out = branch(m, c, fine) + (xs + bias)
        for r in range(mb):
            out = out + br[r][slot(m, r), rows_at, :].astype(F32)
        bo_stage[spot] = out.astype(BF16)
        for copy in out_copies(c):
            copy.start()

    pl.loop(0, rows_own // fine)(finish)
    pl.loop(units, units + (nb - 1) * LAG)(step)

    for i in range(nu):
        gup_ref[:, i * w:(i + 1) * w] = oacc[i]
    for i in range(nq):
        gq_ref[:, i * w:(i + 1) * w] = oacc[nu + i]
    for i in range(na):
        gdown_ref[i * w:(i + 1) * w, :] = oacc[nu + nq + i].T
    for i in range(ne):
        gout_ref[i * w:(i + 1) * w, :] = oacc[nu + nq + na + i].T
    for r in range(1, n):
        src = lax.rem(me + r, n)
        remote(smine, sall.at[src], ss_sem.at[r - 1], sr_sem.at[src], "dp", src).wait_recv()
    total = sall[0]
    for r in range(1, n):
        total = total + sall[r]
    small_ref[...] = total

    for c in range(max(rows_own // fine - 2, 0), rows_own // fine):
        for copy in out_copies(c):
            copy.wait()

    @pl.loop(0, units)
    def _(u):
        for k in range(nb):
            exchange(orders[0], k, u).wait_send()

    for r in range(1, n):
        remote(smine, sall.at[me], ss_sem.at[r - 1], sr_sem.at[me], "dp", lax.rem(me + r, n)).wait_send()
    for k in range(mb):
        vec_exchange(k).wait_send()
    for k in range(mb):
        for j in range(tp >> (k + 1)):
            src_h = h.at[pl.ds(0, rows_own)] if k == 0 else hs[k - 1].at[j]
            remote(src_h, hr[k].at[j], hs_sem.at[k, j], hr_sem.at[k, j], "mp", across(m, k)).wait_send()
            remote(bs[k].at[j], br[k].at[j], bs_sem.at[k, j], br_sem.at[k, j], "mp", across(m, k)).wait_send()


def tail(n, tp, vec, col, seg, b1, b2, second_t, first_t, dy_t, gu, gp, act, att, h, x, dy, wdown, wout):
    width, tokens = first_t.shape
    widths = [a.shape[1] for a in (gu, gp, act, att)]
    w = BLK if all(v % BLK == 0 for v in widths) else BLK // 2
    units = sum(widths) // w
    nb, mb = log2(n), log2(tp)
    shard, own = width // n, tokens // tp
    hbm = pl.BlockSpec(memory_space=pl.ANY)
    vmem = pl.BlockSpec(memory_space=pltpu.VMEM)
    V, D = pltpu.VMEM, pltpu.SemaphoreType.DMA
    mp_bufs = lambda lo: [V((tp >> (k + 1), own, width), BF16) for k in range(lo, mb)]
    step_bufs = lambda: [V((units, width >> (k + 1), w), BF16) for k in range(nb)]
    return pl.pallas_call(
        functools.partial(tail_kernel, n, tp, w),
        in_specs=[vmem] * 5 + [hbm] * 12,
        out_specs=[vmem] * 4 + [hbm] * 2 + [vmem] * 2,
        out_shape=[jax.ShapeDtypeStruct(s, t) for s, t in (
            ((shard, widths[0]), F32), ((shard, widths[1]), F32), ((widths[2], shard), F32), ((widths[3], shard), F32),
            ((own, width), BF16), ((own, width), F32), ((8, width), F32), ((DOCS, 128), F32))],
        scratch_shapes=[
            V((3, width, tokens), BF16), V((units, tokens, w), BF16), step_bufs(), step_bufs(), [V((LAG + 1, width >> (k + 1), w), F32) for k in range(1, nb)],
            V((units, shard, w), F32), V((tp // 2, own, width), BF16), mp_bufs(1), mp_bufs(0), mp_bufs(0), mp_bufs(0),
            V((wdown.shape[0] + wout.shape[0], width), BF16), V((own, width), BF16), V((own, width), BF16), V((1, tokens), F32), V((tokens, DOCS), F32),
            V((mb + 1, 5, DOCS, width), F32), V((mb, 5, DOCS, width), F32), V((units, 8, w), F32), V((8, width), F32), V((n, 8, width), F32),
            D((3,)), D((units,)), D((2,)), D((nb, units)), D((nb, units)), D((mb, tp // 2)), D((mb, tp // 2)), D((mb, tp // 2)), D((mb, tp // 2)),
            D((mb,)), D((mb,)), D((n - 1,)), D((n,)), D((tp // 2,)), D((2,)), V((2, min(own, 128), width), F32), V((2, min(own, 128), width), BF16), D((2, 2))],
        compiler_params=pltpu.CompilerParams(collective_id=1, has_side_effects=True, vmem_limit_bytes=64 * 1024 * 1024 - 1024 * 1024),
        name="tail",
    )(vec, col, seg, b1, b2, second_t, first_t, dy_t, gu, gp, act, att, h, x, dy, wdown, wout)


def finish_kernel(*refs):
    large, (small_ref, norm_ref) = refs[:6], refs[6:8]
    outs, (bq, bu, bo, bd, *norms), norm_out = refs[8:14], refs[14:22], refs[22]
    for src, dst in zip(large, outs):
        dst[...] = src[...]

    @pl.when(pl.program_id(0) == 0)
    def _():
        bq[...] = small_ref[0, :bq.shape[0]]
        bu[...] = small_ref[1, :bu.shape[0]]
        bo[...] = small_ref[2, :]
        bd[...] = small_ref[2, :]
        for k, ref in enumerate(norms):
            ref[...] = small_ref[3 + k, :]
        at = lax.broadcasted_iota(jnp.int32, (DOCS, 128), 0) == lax.broadcasted_iota(jnp.int32, (DOCS, 128), 1)
        norm_out[...] = jnp.sum(jnp.where(at, norm_ref[...], 0.0), axis=0, keepdims=True)[:, :DOCS]


def finish(steps, large, small, norms, heads3, units):
    width = small.shape[1]
    S = jax.ShapeDtypeStruct
    cut = lambda a: pl.BlockSpec((a.shape[0] // steps, a.shape[1]), lambda i: (i, 0))
    vectors = [heads3, units] + [width] * 6
    return pl.pallas_call(
        finish_kernel,
        grid=(steps,),
        in_specs=[cut(a) for a in large] + [full(small.shape), full(norms.shape)],
        out_specs=[cut(a) for a in large] + [full((v,)) for v in vectors] + [full((1, DOCS))],
        out_shape=[S(a.shape, a.dtype) for a in large] + [S((v,), F32) for v in vectors] + [S((1, DOCS), F32)],
        name="finish",
    )(*large, small, norms)


def shards(block_input, segment_ids, cotangent, weight_qkv, bias_qkv, weight_out, bias_out, weight_up, bias_up, weight_down, bias_down,
           gain_first, shift_first, gain_second, shift_second):
    tp = lax.axis_size("mp")
    x, dy = block_input[0], cotangent[0]
    params = (bias_qkv, bias_up, gain_first, shift_first, gain_second, shift_second)
    first_t, second_t, dy_t, gp, gu, act, att, h, col_sums, vec = pre(2.0 / tp, segment_ids, params, x, dy, weight_qkv, weight_up, weight_down, weight_out)
    g_up, g_qkv, g_down, g_out, block_output, grad_input, small, norms = tail(
        lax.axis_size("dp"), tp, vec, col_sums, segment_ids, bias_out, bias_down, second_t, first_t, dy_t, gu, gp, act, att, h, x, dy, weight_down, weight_out)
    g_up, g_qkv, g_down, g_out, block_output, grad_input, b_qkv, b_up, b_out, b_down, *norm_grads, norm_values = finish(
        4, (g_up, g_qkv, g_down, g_out, block_output, grad_input), small, norms, weight_qkv.shape[1], weight_up.shape[1])
    return (block_output[None], grad_input[None], g_qkv, b_qkv, g_out, b_out, g_up, b_up, g_down, b_down, *norm_grads, norm_values)


def solution(mesh):
    placed = (P("dp", None, None), P("dp", None), P("dp", None, None), P(None, "mp"), P("mp"), P("mp", None), P(), P(None, "mp"), P("mp"), P("mp", None),
              P(), P(), P(), P(), P())
    return jax.shard_map(
        shards,
        mesh=mesh,
        in_specs=placed,
        out_specs=(P("dp", "mp", None), P("dp", "mp", None), P("dp", "mp"), P("mp"), P("mp", "dp"), P(), P("dp", "mp"), P("mp"), P("mp", "dp"), P(), P(),
                   P(), P(), P(), P("dp", None)),
        check_vma=False,
    )
```

```python
import functools
import math

import jax
import jax.numpy as jnp
from jax import lax
from jax.experimental import pallas as pl
from jax.experimental.pallas import tpu as pltpu
from jax.sharding import PartitionSpec as P

HD = 64
ROT = 16
DOCS = 8
BLK = 256
LN_EPS = 1e-05
NORM_EPS = 1e-06
NEG = -1e30
F32 = jnp.float32
BF16 = jnp.bfloat16
VMEM_LIMIT = 60 * 1024 * 1024

TAIL = (0.099163489, 0.109273513, 0.0348237317, 0.263242867, -0.249259412, 0.332377466, -0.089621649)


def dot_nn(a, b):
    return lax.dot_general(a, b, (((1,), (0,)), ((), ())), preferred_element_type=F32)


def dot_nt(a, b):
    return lax.dot_general(a, b, (((1,), (1,)), ((), ())), preferred_element_type=F32)


def stats_of(x):
    mean = jnp.mean(x, axis=-1, keepdims=True)
    centred = x - mean
    var = jnp.mean(centred * centred, axis=-1, keepdims=True)
    inv = lax.rsqrt(var + LN_EPS)
    return centred * inv, inv


def gelu_parts(u):
    e = jnp.exp(u * u * -0.5)
    t = 1.0 / (1.0 + 0.25 * jnp.abs(u))
    r = jnp.full_like(t, TAIL[-1])
    for c in TAIL[-2::-1]:
        r = r * t + c
    tail = r * t * e
    cdf = jnp.where(u >= 0.0, 1.0 - tail, tail)
    return u * cdf, cdf + u * (e * (1.0 / math.sqrt(2.0 * math.pi)))


def full(shape):
    return pl.BlockSpec(shape, lambda *_: (0,) * len(shape))


MOST = 5


STRIP = 16
HALF = BLK // 2


def pre_kernel(share, seg_ref, bqkv_ref, bup_ref, g1_ref, s1_ref, g2_ref, s2_ref, x, dy, wqkv, wup, wdown, wout,
               first_o, second_o, dy_o, gp_o, gu_o, act_o, att_o, h_o, col_ref, vec_ref,
               xv, dyv, first, second, act, gu, gp, att, qt, kt, vt, gat, kf, vf, dkt, dvt, wqt, wu, wd, wo, hst, start, end, cosr, sinr, bq, moments, vec8, bias, ex, low, gprob, bounds,
               x_sem, dy_sem, w_sem, t_sem, h_sem, o_sem):
    tokens, width = xv.shape
    units, heads3 = act.shape[1], gp.shape[1]
    heads = att.shape[1]
    count = heads // HD
    blocks = tokens // BLK

    def block(i, n=1):
        return pl.ds(pl.multiple_of(i * BLK, BLK), n * BLK)

    def x_copy(i):
        return pltpu.make_async_copy(x.at[block(i)], xv.at[block(i)], x_sem.at[i])

    def dy_copy(i):
        return pltpu.make_async_copy(dy.at[block(i)], dyv.at[block(i)], dy_sem.at[i])

    raw = gp.at[pl.ds(0, width)]
    w_copies = [pltpu.make_async_copy(a, b, w_sem.at[n]) for n, (a, b) in enumerate(((wqkv, raw), (wout, wo), (wup, wu), (wdown, wd)))]
    w_copies[0].start()
    x_copy(0).start()
    dy_copy(0).start()
    for c in w_copies[1:]:
        c.start()
    x_copy(1).start()
    dy_copy(1).start()

    seg = seg_ref[...]
    edges = [jnp.sum((seg < d).astype(jnp.int32)) for d in range(1, DOCS)]
    bounds[0] = 0
    bounds[DOCS] = tokens
    begin, finish = jnp.zeros_like(seg), jnp.full_like(seg, tokens)
    for d in range(1, DOCS):
        bounds[d] = edges[d - 1]
        begin = jnp.where(seg >= d, edges[d - 1], begin)
    for d in range(DOCS - 1, 0, -1):
        finish = jnp.where(seg < d, edges[d - 1], finish)
    start[...] = begin
    end[...] = finish
    half = ROT // 2
    at_token = lax.broadcasted_iota(jnp.int32, (half, tokens), 1)
    freq = jnp.exp(lax.broadcasted_iota(jnp.int32, (half, tokens), 0).astype(F32) * (2.0 / ROT) * -math.log(10000.0))
    angle = (at_token - begin).astype(F32) * freq
    cosr[...] = jnp.cos(angle)
    sinr[...] = jnp.sin(angle)
    bqkv, bup, g1, s1, g2, s2 = (r[...].astype(F32).reshape(1, -1) for r in (bqkv_ref, bup_ref, g1_ref, s1_ref, g2_ref, s2_ref))
    bq[...] = jnp.broadcast_to(bqkv, (8, heads3)).T
    w_copies[0].wait()
    wqt[...] = raw[...].T

    def t_copies(i):
        return [pltpu.make_async_copy(low.at[n, pl.ds(0, width)], out.at[:, block(i)], t_sem.at[n]) for n, out in enumerate((first_o, second_o, dy_o))]

    def out_copy(n, src, out, i):
        return pltpu.make_async_copy(src.at[block(i)], out.at[block(i)], o_sem.at[n, i])

    outs = ((act, act_o), (gu, gu_o), (att, att_o), (gp, gp_o))

    def turn(v, c, s):
        a, b = v[:half], v[half:ROT]
        return jnp.concatenate([a * c - b * s, b * c + a * s, v[ROT:]], axis=0)

    def norm_block(i):
        for q in range(0, BLK, STRIP):
            at = pl.ds(pl.multiple_of(i * BLK + q, STRIP), STRIP)
            xs = xv[at, :].astype(F32)
            normed, inv = stats_of(xs)
            moments[at, 0:1] = jnp.mean(xs, axis=-1, keepdims=True)
            moments[at, 1:2] = inv
            first[at, :] = (normed * g1 + s1).astype(BF16)
            second[at, :] = (normed * g2 + s2).astype(BF16)

    x_copy(0).wait()
    norm_block(0)
    for c in w_copies[1:]:
        c.wait()

    @pl.loop(0, blocks)
    def _(i):
        at = block(i)
        after = jnp.minimum(i + 1, blocks - 1)
        dy_copy(i).wait()

        @pl.when(i + 1 < blocks)
        def _():
            x_copy(i + 1).wait()

        @pl.when(i + 2 < blocks)
        def _():
            x_copy(i + 2).start()
            dy_copy(i + 2).start()

        chunk = min(256, units)

        def ups(c):
            return dot_nn(second[at, :], wu[:, c:c + chunk]), dot_nt(dyv[at, :], wd[c:c + chunk, :])

        def gelu(c, made):
            for q in range(0, BLK, STRIP):
                strip = pl.ds(pl.multiple_of(i * BLK + q, STRIP), STRIP)
                value, slope = gelu_parts(made[0][q:q + STRIP] + bup[:, c:c + chunk])
                act[strip, c:c + chunk] = value.astype(BF16)
                gu[strip, c:c + chunk] = (made[1][q:q + STRIP] * slope).astype(BF16)

        pt = dot_nt(wqt[...], first[at, :])
        made = ups(0)
        norm_block(after)
        for c in range(chunk, units, chunk):
            later = ups(c)
            gelu(c - chunk, made)
            made = later
        gat[:, at] = dot_nt(wo[...], dyv[at, :]).astype(BF16)
        gelu(units - chunk, made)

        @pl.when(i >= 1)
        def _():
            for copy in t_copies(i - 1):
                copy.wait()

        for n, rows_in in enumerate((first, second, dyv)):
            low[n, :width] = rows_in[at, :].T
        c, s = cosr[:, at], sinr[:, at]
        ks, vs = [], []
        for h in range(count):
            o = h * 3 * HD
            part = [pt[o + n * HD:o + (n + 1) * HD] + bq[o + n * HD:o + (n + 1) * HD, :1] for n in range(3)]
            qt[h * HD:(h + 1) * HD, at] = (turn(part[0], c, s).astype(BF16).astype(F32) * (1.0 / math.sqrt(HD))).astype(BF16)
            ks.append(turn(part[1], c, s).astype(BF16))
            vs.append(part[2].astype(BF16))
            kt[h * HD:(h + 1) * HD, at] = ks[h]
            vt[h * HD:(h + 1) * HD, at] = vs[h]
        kb, vb = jnp.concatenate(ks, axis=0), jnp.concatenate(vs, axis=0)
        kf[at, :] = kb.T
        vf[at, :] = vb.T
        for copy in (*t_copies(i), out_copy(0, act, act_o, i), out_copy(1, gu, gu_o, i)):
            copy.start()

    for copy in t_copies(blocks - 1):
        copy.wait()

    dkt[...] = jnp.zeros_like(dkt)
    dvt[...] = jnp.zeros_like(dvt)

    def low_block(i):
        lowest = 0
        for d in range(1, DOCS):
            lowest = jnp.maximum(lowest, jnp.where(bounds[d] <= i * BLK, bounds[d], 0))
        return lax.div(lowest, BLK)

    def end_of(j):
        last = j * BLK + BLK - 1
        highest = tokens
        for d in range(1, DOCS):
            highest = jnp.minimum(highest, jnp.where(bounds[d] > last, bounds[d], tokens))
        return highest

    def attend(i, lo, n):
        at, keys, size = block(i), block(lo, n), n * BLK
        strips = [slice(r, r + STRIP) for r in range(0, size, STRIP)]
        k_off = lax.broadcasted_iota(jnp.int32, (STRIP, BLK), 0)
        last = i * BLK - lo * BLK + lax.broadcasted_iota(jnp.int32, (1, BLK), 1)
        lead = start[:, at] - lo * BLK
        for r in strips:
            k_at = k_off + r.start
            bias[r] = jnp.where((k_at <= last) & (k_at >= lead), 0.0, NEG)
        blank = jnp.zeros((HD, BLK), BF16)
        span = min(2 * HD, heads)

        def spread(v, h):
            return jnp.concatenate([v if g == h % (span // HD) else blank for g in range(span // HD)], axis=0)

        def lanes(h):
            return slice(h * HD // span * span, h * HD // span * span + span)

        def rows_of(h):
            return slice(h * HD, (h + 1) * HD)

        atts, dqs, share_of = {}, {}, {}

        def stage_a(h):
            ex[h, :size] = dot_nn(kf[keys, lanes(h)], spread(qt[rows_of(h), at], h))

        def stage_b(h):
            best = jnp.full((STRIP, BLK), NEG, F32)
            for r in strips:
                s = ex[h, r] + bias[r]
                ex[h, r] = s
                best = jnp.maximum(best, s)
            best = jnp.max(best, axis=0, keepdims=True)
            total = jnp.zeros((STRIP, BLK), F32)
            for r in strips:
                e = jnp.exp(ex[h, r] - best)
                ex[h, r] = e
                total = total + e
            share_of[h] = 1.0 / jnp.sum(total, axis=0, keepdims=True)
            for r in strips:
                low[h, r] = (ex[h, r] * share_of[h]).astype(BF16)

        def stage_c(h):
            atts[h] = dot_nn(vt[rows_of(h), keys], low[h, :size])
            gprob[h % 2, :size] = dot_nn(vf[keys, lanes(h)], spread(gat[rows_of(h), at], h))
            dvt[rows_of(h), keys] += dot_nt(gat[rows_of(h), at], low[h, :size])

        def stage_d(h):
            delta = jnp.sum(atts[h] * gat[rows_of(h), at].astype(F32), axis=0, keepdims=True)
            for r in strips:
                low[h, r] = (ex[h, r] * share_of[h] * (gprob[h % 2, r] - delta)).astype(BF16)

        def stage_e(h):
            dqs[h] = dot_nn(kt[rows_of(h), keys], low[h, :size])
            dkt[rows_of(h), keys] += dot_nt(qt[rows_of(h), at], low[h, :size])

        stages = (stage_a, stage_b, stage_c, stage_d, stage_e)
        for t in range(count + len(stages) - 1):
            for k, stage in enumerate(stages):
                if 0 <= t - k < count:
                    stage(t - k)
        att[at, :] = jnp.concatenate([atts[h] for h in range(count)], axis=0).T.astype(BF16)
        c, sn = cosr[:, at], -sinr[:, at]
        qt[:, at] = jnp.concatenate([turn(dqs[h] * (1.0 / math.sqrt(HD)), c, sn) for h in range(count)], axis=0).astype(BF16)

    @pl.loop(0, blocks)
    def _(i):
        lo = low_block(i)
        for n in range(1, MOST + 1):
            pl.when(i - lo + 1 == n)(functools.partial(attend, i, lo, n))
        out_copy(2, att, att_o, i).start()

    vec8[...] = jnp.zeros_like(vec8)
    chunk = min(256, width)

    def spare(what, c, strip):
        k = c // chunk * 3 + what
        return ex.at[k % count, pl.ds(k // count * BLK + strip.start, strip.stop - strip.start)]

    def h_copy(i):
        slot = lax.rem(i, 2)
        return pltpu.make_async_copy(hst.at[slot], h_o.at[block(i)], h_sem.at[slot])

    def doc_of(t):
        return sum(jnp.where(bounds[d] <= t, 1, 0) for d in range(1, DOCS))

    @pl.loop(0, blocks)
    def _(i):
        at = block(i)
        c, sn = cosr[:, at], -sinr[:, at]
        pieces = []
        for h in range(count):
            r = slice(h * HD, (h + 1) * HD)
            pieces += [qt[r, at], turn(dkt[r, at], c, sn).astype(BF16), dvt[r, at].astype(BF16)]
        gp[at, :] = jnp.concatenate(pieces, axis=0).T
        out_copy(3, gp, gp_o, i).start()

        @pl.when(i >= 2)
        def _():
            h_copy(i - 2).wait()

        slot = lax.rem(i, 2)

        def grads(c):
            return dot_nt(gu[at, :], wu[c:c + chunk, :]), dot_nn(gp[at, :], wqt[:, c:c + chunk])

        def use(c, made):
            cut = slice(c, c + chunk)
            for q in range(0, BLK, STRIP):
                strip = slice(q, q + STRIP)
                gs, gf = made[0][strip], made[1][strip]
                spare(0, c, strip)[...] = gf
                spare(1, c, strip)[...] = gs
                hst[slot, strip, cut] = (gf * g1[:, cut] + gs * g2[:, cut]).astype(BF16)

        made = grads(0)
        for q in range(0, BLK, STRIP):
            here = pl.ds(pl.multiple_of(i * BLK + q, STRIP), STRIP)
            normed = (xv[here, :].astype(F32) - moments[here, 0:1]) * moments[here, 1:2]
            for c in range(0, width, chunk):
                spare(2, c, slice(q, q + STRIP))[...] = normed[:, c:c + chunk]
        for c in range(chunk, width, chunk):
            later = grads(c)
            use(c - chunk, made)
            made = later
        use(width - chunk, made)
        h_copy(i).start()
        at_row = lax.broadcasted_iota(jnp.int32, (STRIP, chunk), 0)

        @pl.loop(doc_of(i * BLK), doc_of(i * BLK + BLK - 1) + 1)
        def _(d):
            low_row, high_row = bounds[d] - i * BLK, bounds[d + 1] - i * BLK
            for c in range(0, width, chunk):
                sums = [jnp.zeros((STRIP, chunk), F32)] * 4
                for q in range(0, BLK, STRIP):
                    strip = slice(q, q + STRIP)
                    inside = (at_row >= low_row - q) & (at_row < high_row - q)
                    gf, gs = (jnp.where(inside, spare(k, c, strip)[...], 0.0) for k in range(2))
                    normed = spare(2, c, strip)[...]
                    sums = [s + v for s, v in zip(sums, (gf * normed, gf, gs * normed, gs))]
                for n in range(4):
                    vec8[n, d, :, c:c + chunk] += sums[n][:8] + sums[n][8:]

    vec_ref[...] = jnp.sum(vec8[...], axis=2)

    pairs_of = ((first, gp, 1.0), (second, gu, 1.0))

    def gram_block(j, first_row, size):
        at, cols = pl.ds(pl.multiple_of(first_row, HALF), size), block(j)

        def gram(m):
            return dot_nt(m[at, :], m[cols, :])

        grams = [(gram(a), plus, gram(b)) for a, b, plus in pairs_of] + [(gram(att) + gram(act), share, gram(dyv))]
        ahead = lax.broadcasted_iota(jnp.int32, (STRIP, BLK), 0) - lax.broadcasted_iota(jnp.int32, (STRIP, BLK), 1)
        reach = end[:, cols] - first_row
        row_off = lax.broadcasted_iota(jnp.int32, (STRIP, BLK), 0)
        total = jnp.zeros((STRIP, BLK), F32)
        for r in range(0, size, STRIP):
            terms = None
            for a, plus, b in grams:
                term = (a[r:r + STRIP] + plus) * b[r:r + STRIP]
                terms = term if terms is None else terms + term
            gap = ahead + (first_row - j * BLK + r)
            weight = jnp.where(gap > 0, 2.0, jnp.where(gap == 0, 1.0, 0.0))
            total = total + jnp.where(row_off + r < reach, terms * weight, 0.0)
        col_ref[:, cols] += total[:8] + total[8:]

    col_ref[...] = jnp.zeros_like(col_ref)

    @pl.loop(0, blocks)
    def _(j):
        total = lax.div(end_of(j) - j * BLK + HALF - 1, HALF)
        pl.loop(0, lax.div(total, 4))(lambda s: gram_block(j, j * BLK + s * 4 * HALF, 4 * HALF))
        for n in range(1, 4):
            pl.when(lax.rem(total, 4) == n)(lambda n=n: gram_block(j, j * BLK + (total - n) * HALF, n * HALF))

    for i in (blocks - 2, blocks - 1):
        h_copy(i).wait()

    @pl.loop(0, blocks)
    def _(i):
        for n, (src, out) in enumerate(outs):
            out_copy(n, src, out, i).wait()


def pre(share, seg, params, x, dy, wqkv, wup, wdown, wout):
    tokens, width = x.shape
    heads3, units, heads = wqkv.shape[1], wup.shape[1], wout.shape[0]
    blocks = tokens // BLK
    hbm, vmem = pl.BlockSpec(memory_space=pl.ANY), pl.BlockSpec(memory_space=pltpu.VMEM)
    V, D = pltpu.VMEM, pltpu.SemaphoreType.DMA
    t_shape, S = (width, tokens), jax.ShapeDtypeStruct
    return pl.pallas_call(
        functools.partial(pre_kernel, share),
        in_specs=[vmem] * 7 + [hbm] * 6,
        out_specs=[hbm] * 8 + [vmem] * 2,
        out_shape=[S(t_shape, BF16)] * 3 + [S((tokens, n), BF16) for n in (heads3, units, units, heads, width)] + [S((8, tokens), F32), S((4, DOCS, width), F32)],
        scratch_shapes=[V((tokens, width), BF16)] * 4 + [V((tokens, units), BF16)] * 2 + [V((tokens, heads3), BF16), V((tokens, heads), BF16)]
        + [V((heads, tokens), BF16)] * 4 + [V((tokens, heads), BF16)] * 2 + [V((heads, tokens), F32)] * 2
        + [V((heads3, width), BF16), V((width, units), BF16), V((units, width), BF16), V((heads, width), BF16), V((2, BLK, width), BF16)]
        + [V((1, tokens), jnp.int32)] * 2 + [V((ROT // 2, tokens), F32)] * 2 + [V((heads3, 8), F32), V((tokens, 2), F32), V((4, DOCS, 8, width), F32)]
        + [V((MOST * BLK, BLK), F32), V((heads // HD, max(MOST, -(-3 * width // BLK // (heads // HD))) * BLK, BLK), F32), V((max(heads // HD, 3), MOST * BLK, BLK), BF16), V((2, MOST * BLK, BLK), F32)]
        + [pltpu.SMEM((DOCS + 1,), jnp.int32)]
        + [D((blocks,)), D((blocks,)), D((4,)), D((3,)), D((2,)), D((4, blocks))],
        compiler_params=pltpu.CompilerParams(vmem_limit_bytes=63 * 1024 * 1024),
        name="pre",
    )(seg, *params, x, dy, wqkv, wup, wdown, wout)


LOAD_AHEAD = 4
LAG = 3


def bit_of(index, bit):
    return lax.rem(lax.div(index, 2**bit), 2)


def across(index, bit):
    return index + (1 - 2 * bit_of(index, bit)) * 2**bit


def log2(n):
    return n.bit_length() - 1


def remote(src, dst, send, recv, axis, index):
    return pltpu.make_async_remote_copy(src_ref=src, dst_ref=dst, send_sem=send, recv_sem=recv, device_id={axis: index}, device_id_type=pl.DeviceIdType.MESH)


def tail_kernel(n, tp, w, vec_ref, col_ref, seg_ref, b1_ref, b2_ref, second_t, first_t, dy_t, gu, gp, act, att, h, x, dy, wdown, wout,
                gup_ref, gq_ref, gdown_ref, gout_ref, bo_ref, gi_ref, small_ref, norm_ref,
                at, b, snd, rcv, keep, oacc, hown, hs, hr, bs, br, wd, xr, dyr, trow, tcol, vsend, vrecv, bsum, smine, sall,
                at_sem, b_sem, w_sem, snd_sem, rcv_sem, hs_sem, hr_sem, bs_sem, br_sem, gs_sem, gr_sem, ss_sem, sr_sem, hown_sem, row_sem, gi_stage, bo_stage, out_sem):
    width, tokens = first_t.shape
    me, m = lax.axis_index("dp"), lax.axis_index("mp")
    nb, mb = log2(n), log2(tp)
    shard, rows_own = width // n, tokens // tp
    nu, nq, na, ne = (r.shape[1] // w for r in (gu, gp, act, att))
    units = nu + nq + na + ne

    barrier = pltpu.get_barrier_semaphore()
    for r in range(1, n):
        pl.semaphore_signal(barrier, inc=1, device_id={"dp": lax.rem(me + r, n)}, device_id_type=pl.DeviceIdType.MESH)
    for r in range(1, tp):
        pl.semaphore_signal(barrier, inc=1, device_id={"mp": lax.rem(m + r, tp)}, device_id_type=pl.DeviceIdType.MESH)
    pl.semaphore_wait(barrier, n - 1 + tp - 1)

    def vec_exchange(k):
        return remote(vsend.at[k], vrecv.at[k], gs_sem.at[k], gr_sem.at[k], "mp", across(m, k))

    hot = seg_ref[...] == lax.broadcasted_iota(jnp.int32, (DOCS, tokens), 0)
    mine = jnp.sum(jnp.where(hot, jnp.sum(col_ref[...], axis=0, keepdims=True), 0.0), axis=1, keepdims=True)
    vsend[0, :4] = vec_ref[...]
    vsend[0, 4] = jnp.broadcast_to(mine, (DOCS, width))
    vec_exchange(0).start()

    for j in range(tp // 2):
        there = 2 * j + 1 - bit_of(m, 0)
        remote(h.at[pl.ds(there * rows_own, rows_own)], hr[0].at[j], hs_sem.at[0, j], hr_sem.at[0, j], "mp", across(m, 0)).start()

    sources = (second_t, first_t, dy_t)

    def place(p):
        return sum(((p >> (nb - 1 - k)) & 1) << k for k in range(nb))

    def load_at(mat):
        for p in range(n):
            pltpu.make_async_copy(sources[mat].at[pl.ds(place(p) * shard, shard)], at.at[mat, pl.ds(p * shard, shard)], at_sem.at[mat]).start()

    def load_b(base, src):
        for i in range(src.shape[1] // w):
            pltpu.make_async_copy(src.at[:, pl.ds(i * w, w)], b.at[base + i], b_sem.at[base + i]).start()

    load_at(0)
    load_b(0, gu)
    load_at(1)
    load_b(nu, gp)
    load_at(2)
    load_b(nu + nq, act)
    load_b(nu + nq + na, att)
    split = act.shape[1]
    wd_copies = (pltpu.make_async_copy(wdown, wd.at[pl.ds(0, split)], w_sem.at[0]), pltpu.make_async_copy(wout, wd.at[pl.ds(split, wd.shape[0] - split)], w_sem.at[1]))
    own_at = pl.ds(m * rows_own, rows_own)
    row_copies = (pltpu.make_async_copy(x.at[own_at], xr, row_sem.at[0]), pltpu.make_async_copy(dy.at[own_at], dyr, row_sem.at[1]))
    hown_copies = [pltpu.make_async_copy(h.at[pl.ds((2 * j + bit_of(m, 0)) * rows_own, rows_own)], hown.at[j], hown_sem.at[j]) for j in range(tp // 2)]
    for c in (*wd_copies, *row_copies, *hown_copies):
        c.start()

    for k in range(mb):
        vec_exchange(k).wait_recv()
        vsend[k + 1] = vsend[k] + vrecv[k]
        if k + 1 < mb:
            vec_exchange(k + 1).start()
    squares = vsend[mb, 4, :, :1]
    for j in range(4):
        squares = squares + jnp.sum(vsend[mb, j] * vsend[mb, j], axis=1, keepdims=True)
    norm = jnp.sqrt(squares + NORM_EPS)
    norm_ref[...] = jnp.broadcast_to(norm, norm_ref.shape)
    clip = jnp.minimum(1.0, jnp.mean(norm, axis=0, keepdims=True) / norm)
    per_token = jnp.sum(jnp.where(hot, clip, 0.0), axis=0, keepdims=True)
    trow[...] = per_token
    tcol[...] = jnp.broadcast_to(per_token, (DOCS, tokens)).T
    smine[...] = jnp.zeros_like(smine)
    for j in range(4):
        smine[3 + j:4 + j, :] = jnp.sum(vsend[mb, j] * clip, axis=0, keepdims=True)

    orders = (tuple(range(nb)), tuple(range(1, nb)) + (0,))

    def z_first(u):
        return (u == 1) | (u == units - 3)

    def by_order(u, body):
        pl.when(jnp.logical_not(z_first(u)))(functools.partial(body, orders[0]))
        pl.when(z_first(u))(functools.partial(body, orders[1]))

    def matrix_of(u):
        return jnp.where(u >= nu, 1, 0) + jnp.where(u >= nu + nq, 1, 0)

    def exchange(order, k, u):
        return remote(snd[k].at[u], rcv[k].at[u], snd_sem.at[k, u], rcv_sem.at[k, u], "dp", across(me, order[k]))

    def pieces(bit, side):
        size = width >> (bit + 1)
        return [pl.ds(pl.multiple_of((2 * g + side) * size, size), size) for g in range(2**bit)], size

    def other_half(mat, clipped, u):
        pltpu.make_async_copy(gu.at[:, pl.ds(0, w)], b.at[u], b_sem.at[u]).wait()
        if clipped:
            scaled = b[u].astype(F32) * tcol[:, :1]
            b[u] = scaled.astype(BF16)
            bsum[u] = jnp.sum(scaled.reshape(tokens // 8, 8, w), axis=0)

        def send(order):
            away, size = pieces(order[0], 1 - bit_of(me, order[0]))
            for g, piece in enumerate(away):
                snd[0][u, g * size:(g + 1) * size, :] = dot_nn(at[mat, piece, :], b[u]).astype(BF16)

            @pl.when(u < LOAD_AHEAD)
            def _():
                exchange(order, 0, u).start()

        by_order(u, send)

    def at_ready(mat):
        pltpu.make_async_copy(sources[mat], at.at[mat], at_sem.at[mat]).wait()

    at_ready(0)
    pl.loop(0, nu)(lambda u: other_half(0, True, u))
    at_ready(1)
    pl.loop(nu, nu + nq)(lambda u: other_half(1, True, u))
    at_ready(2)
    for p in range(n):
        piece = pl.ds(p * shard, shard)
        scaled = at[2, piece, :].astype(F32) * trow[...]
        at[2, piece, :] = scaled.astype(BF16)
        folded = scaled[:, :128]
        for k in range(1, tokens // 128):
            folded = folded + scaled[:, k * 128:(k + 1) * 128]
        smine[2:3, place(p) * shard:(place(p) + 1) * shard] = jnp.sum(folded.T, axis=0, keepdims=True)
    pl.loop(nu + nq, units)(lambda u: other_half(2, False, u))

    for i in range(nq):
        smine[0:1, i * w:(i + 1) * w] = jnp.sum(bsum[nu + i], axis=0, keepdims=True)
    for i in range(nu):
        smine[1:2, i * w:(i + 1) * w] = jnp.sum(bsum[i], axis=0, keepdims=True)
    sall[me] = smine[...]
    for r in range(1, n):
        remote(smine, sall.at[me], ss_sem.at[r - 1], sr_sem.at[me], "dp", lax.rem(me + r, n)).start()

    chunk = min(rows_own, 256)
    def branch(owner, c, chunk=chunk):
        at_rows = pl.ds(pl.multiple_of(owner * rows_own + c * chunk, chunk), chunk)
        left = jnp.concatenate([b[nu + nq + i, at_rows, :] for i in range(na + ne)], axis=1)
        return dot_nn(left, wd[...])

    def chunks(body):
        pl.loop(0, rows_own // chunk)(lambda c: body(c, pl.ds(pl.multiple_of(c * chunk, chunk), chunk)))

    def slot(owner, k):
        return lax.div(owner, 2 ** (k + 1))

    def wait_mp(k, buf, recv_sem, send_sem):
        for j in range(tp >> (k + 1)):
            remote(buf[k].at[j], buf[k].at[j], send_sem.at[k, j], recv_sem.at[k, j], "mp", across(m, k)).wait_recv()

    def owner_of(k, j):
        return (2 * j + 1 - bit_of(m, k)) * 2**k + lax.rem(m, 2**k)

    def h_task(k, j):
        if j == 0:
            if k == 1:
                for c in hown_copies:
                    c.wait()
            wait_mp(k - 1, hr, hr_sem, hs_sem)
        owner = owner_of(k, j)

        def h_send(c, rows_at):
            val = hown[slot(owner, 0), rows_at, :].astype(F32)
            for r in range(k):
                val = val + hr[r][slot(owner, r), rows_at, :].astype(F32)
            hs[k - 1][j, rows_at, :] = val.astype(BF16)

        chunks(h_send)
        remote(hs[k - 1].at[j], hr[k].at[j], hs_sem.at[k, j], hr_sem.at[k, j], "mp", across(m, k)).start()

    def b_task(k, j):
        if k == 0 and j == 0:
            for c in wd_copies:
                c.wait()
        if k > 0 and j == 0:
            wait_mp(k - 1, br, br_sem, bs_sem)
        owner = owner_of(k, j)

        def b_send(c, rows_at):
            val = branch(owner, c)
            for r in range(k):
                val = val + br[r][slot(owner, r), rows_at, :].astype(F32)
            bs[k][j, rows_at, :] = val.astype(BF16)

        chunks(b_send)
        remote(bs[k].at[j], br[k].at[j], bs_sem.at[k, j], br_sem.at[k, j], "mp", across(m, k)).start()

    tasks = [functools.partial(h_task, 1, j) for j in range(tp // 4)] + [functools.partial(b_task, 0, j) for j in range(tp // 2)]
    for k in range(1, mb):
        tasks += [functools.partial(h_task, k, j) for j in range(tp >> (k + 1)) if k > 1]
        tasks += [functools.partial(b_task, k, j) for j in range(tp >> (k + 1))]

    def split(val, pos, bit):
        size = val.shape[0] >> (pos + 1)
        low = [val[2 * g * size:(2 * g + 1) * size] for g in range(2**pos)]
        high = [val[(2 * g + 1) * size:(2 * g + 2) * size] for g in range(2**pos)]
        low, high = (v[0] if len(v) == 1 else jnp.concatenate(v, axis=0) for v in (low, high))
        return jnp.where(bit == 1, low, high), jnp.where(bit == 1, high, low)

    def later(k, u):
        def body(order):
            exchange(order, k, u).wait_recv()
            val = keep[k - 1][lax.rem(u, LAG + 1)] + rcv[k][u].astype(F32)
            if k == nb - 1:
                oacc[u] = val
                return
            pos = 1 if order[0] != 0 and k + 1 < nb - 1 else 0
            away, stay = split(val, pos, bit_of(me, order[k + 1]))
            snd[k + 1][u] = away.astype(BF16)
            keep[k][lax.rem(u, LAG + 1)] = stay
            exchange(order, k + 1, u).start()

        by_order(u, body)

    def first(u):
        mat = matrix_of(u)

        def body(order):
            exchange(order, 0, u).wait_recv()
            near, size = pieces(order[0], bit_of(me, order[0]))
            for g, piece in enumerate(near):
                val = dot_nn(at[mat, piece, :], b[u]) + rcv[0][u, g * size:(g + 1) * size, :].astype(F32)
                away, stay = split(val, 0, bit_of(me, order[1]))
                part = size // 2
                snd[1][u, g * part:(g + 1) * part, :] = away.astype(BF16)
                keep[0][lax.rem(u, LAG + 1), g * part:(g + 1) * part, :] = stay
            exchange(order, 1, u).start()

        by_order(u, body)

        @pl.when(u + LOAD_AHEAD < units)
        def _():
            by_order(u + LOAD_AHEAD, lambda order: exchange(order, 0, u + LOAD_AHEAD).start())

    def step(t):
        for k in range(nb - 1, 0, -1):
            pl.when((t >= k * LAG) & (t < units + k * LAG))(functools.partial(later, k, t - k * LAG))
        pl.when(t < units)(functools.partial(first, t))
        for spot, task in enumerate(tasks):
            pl.when(t == min(spot, units - 1))(task)

    pl.loop(0, units)(step)

    for c in row_copies:
        c.wait()
    wait_mp(mb - 1, hr, hr_sem, hs_sem)
    wait_mp(mb - 1, br, br_sem, bs_sem)

    fine = min(rows_own, 128)
    bias = (b1_ref[...].astype(F32) + b2_ref[...].astype(F32)).reshape(1, width)

    def out_copies(c):
        spot = lax.rem(c, 2)
        to = pl.ds(pl.multiple_of(c * fine, fine), fine)
        return (pltpu.make_async_copy(gi_stage.at[spot], gi_ref.at[to], out_sem.at[0, spot]),
                pltpu.make_async_copy(bo_stage.at[spot], bo_ref.at[to], out_sem.at[1, spot]))

    def finish(c):
        spot = lax.rem(c, 2)
        rows_at = pl.ds(pl.multiple_of(c * fine, fine), fine)

        @pl.when(c >= 2)
        def _():
            for copy in out_copies(c - 2):
                copy.wait()

        val = hown[slot(m, 0), rows_at, :].astype(F32)
        for r in range(mb):
            val = val + hr[r][slot(m, r), rows_at, :].astype(F32)
        xs = xr[rows_at, :].astype(F32)
        normed, inv = stats_of(xs)
        back_x = inv * (val - jnp.mean(val, axis=-1, keepdims=True) - normed * jnp.mean(val * normed, axis=-1, keepdims=True))
        gi_stage[spot] = dyr[rows_at, :].astype(F32) + back_x
        out = branch(m, c, fine) + (xs + bias)
        for r in range(mb):
            out = out + br[r][slot(m, r), rows_at, :].astype(F32)
        bo_stage[spot] = out.astype(BF16)
        for copy in out_copies(c):
            copy.start()

    pl.loop(0, rows_own // fine)(finish)
    pl.loop(units, units + (nb - 1) * LAG)(step)

    for i in range(nu):
        gup_ref[:, i * w:(i + 1) * w] = oacc[i]
    for i in range(nq):
        gq_ref[:, i * w:(i + 1) * w] = oacc[nu + i]
    for i in range(na):
        gdown_ref[i * w:(i + 1) * w, :] = oacc[nu + nq + i].T
    for i in range(ne):
        gout_ref[i * w:(i + 1) * w, :] = oacc[nu + nq + na + i].T
    for r in range(1, n):
        src = lax.rem(me + r, n)
        remote(smine, sall.at[src], ss_sem.at[r - 1], sr_sem.at[src], "dp", src).wait_recv()
    total = sall[0]
    for r in range(1, n):
        total = total + sall[r]
    small_ref[...] = total

    for c in range(max(rows_own // fine - 2, 0), rows_own // fine):
        for copy in out_copies(c):
            copy.wait()

    @pl.loop(0, units)
    def _(u):
        for k in range(nb):
            exchange(orders[0], k, u).wait_send()

    for r in range(1, n):
        remote(smine, sall.at[me], ss_sem.at[r - 1], sr_sem.at[me], "dp", lax.rem(me + r, n)).wait_send()
    for k in range(mb):
        vec_exchange(k).wait_send()
    for k in range(mb):
        for j in range(tp >> (k + 1)):
            src_h = h.at[pl.ds(0, rows_own)] if k == 0 else hs[k - 1].at[j]
            remote(src_h, hr[k].at[j], hs_sem.at[k, j], hr_sem.at[k, j], "mp", across(m, k)).wait_send()
            remote(bs[k].at[j], br[k].at[j], bs_sem.at[k, j], br_sem.at[k, j], "mp", across(m, k)).wait_send()


def tail(n, tp, vec, col, seg, b1, b2, second_t, first_t, dy_t, gu, gp, act, att, h, x, dy, wdown, wout):
    width, tokens = first_t.shape
    widths = [a.shape[1] for a in (gu, gp, act, att)]
    w = BLK if all(v % BLK == 0 for v in widths) else BLK // 2
    units = sum(widths) // w
    nb, mb = log2(n), log2(tp)
    shard, own = width // n, tokens // tp
    hbm = pl.BlockSpec(memory_space=pl.ANY)
    vmem = pl.BlockSpec(memory_space=pltpu.VMEM)
    V, D = pltpu.VMEM, pltpu.SemaphoreType.DMA
    mp_bufs = lambda lo: [V((tp >> (k + 1), own, width), BF16) for k in range(lo, mb)]
    step_bufs = lambda: [V((units, width >> (k + 1), w), BF16) for k in range(nb)]
    return pl.pallas_call(
        functools.partial(tail_kernel, n, tp, w),
        in_specs=[vmem] * 5 + [hbm] * 12,
        out_specs=[vmem] * 4 + [hbm] * 2 + [vmem] * 2,
        out_shape=[jax.ShapeDtypeStruct(s, t) for s, t in (
            ((shard, widths[0]), F32), ((shard, widths[1]), F32), ((widths[2], shard), F32), ((widths[3], shard), F32),
            ((own, width), BF16), ((own, width), F32), ((8, width), F32), ((DOCS, 128), F32))],
        scratch_shapes=[
            V((3, width, tokens), BF16), V((units, tokens, w), BF16), step_bufs(), step_bufs(), [V((LAG + 1, width >> (k + 1), w), F32) for k in range(1, nb)],
            V((units, shard, w), F32), V((tp // 2, own, width), BF16), mp_bufs(1), mp_bufs(0), mp_bufs(0), mp_bufs(0),
            V((wdown.shape[0] + wout.shape[0], width), BF16), V((own, width), BF16), V((own, width), BF16), V((1, tokens), F32), V((tokens, DOCS), F32),
            V((mb + 1, 5, DOCS, width), F32), V((mb, 5, DOCS, width), F32), V((units, 8, w), F32), V((8, width), F32), V((n, 8, width), F32),
            D((3,)), D((units,)), D((2,)), D((nb, units)), D((nb, units)), D((mb, tp // 2)), D((mb, tp // 2)), D((mb, tp // 2)), D((mb, tp // 2)),
            D((mb,)), D((mb,)), D((n - 1,)), D((n,)), D((tp // 2,)), D((2,)), V((2, min(own, 128), width), F32), V((2, min(own, 128), width), BF16), D((2, 2))],
        compiler_params=pltpu.CompilerParams(collective_id=1, has_side_effects=True, vmem_limit_bytes=64 * 1024 * 1024 - 1024 * 1024),
        name="tail",
    )(vec, col, seg, b1, b2, second_t, first_t, dy_t, gu, gp, act, att, h, x, dy, wdown, wout)


def finish_kernel(*refs):
    large, (small_ref, norm_ref) = refs[:6], refs[6:8]
    outs, (bq, bu, bo, bd, *norms), norm_out = refs[8:14], refs[14:22], refs[22]
    for src, dst in zip(large, outs):
        dst[...] = src[...]

    @pl.when(pl.program_id(0) == 0)
    def _():
        bq[...] = small_ref[0, :bq.shape[0]]
        bu[...] = small_ref[1, :bu.shape[0]]
        bo[...] = small_ref[2, :]
        bd[...] = small_ref[2, :]
        for k, ref in enumerate(norms):
            ref[...] = small_ref[3 + k, :]
        at = lax.broadcasted_iota(jnp.int32, (DOCS, 128), 0) == lax.broadcasted_iota(jnp.int32, (DOCS, 128), 1)
        norm_out[...] = jnp.sum(jnp.where(at, norm_ref[...], 0.0), axis=0, keepdims=True)[:, :DOCS]


def finish(steps, large, small, norms, heads3, units):
    width = small.shape[1]
    S = jax.ShapeDtypeStruct
    cut = lambda a: pl.BlockSpec((a.shape[0] // steps, a.shape[1]), lambda i: (i, 0))
    vectors = [heads3, units] + [width] * 6
    return pl.pallas_call(
        finish_kernel,
        grid=(steps,),
        in_specs=[cut(a) for a in large] + [full(small.shape), full(norms.shape)],
        out_specs=[cut(a) for a in large] + [full((v,)) for v in vectors] + [full((1, DOCS))],
        out_shape=[S(a.shape, a.dtype) for a in large] + [S((v,), F32) for v in vectors] + [S((1, DOCS), F32)],
        name="finish",
    )(*large, small, norms)


def shards(block_input, segment_ids, cotangent, weight_qkv, bias_qkv, weight_out, bias_out, weight_up, bias_up, weight_down, bias_down,
           gain_first, shift_first, gain_second, shift_second):
    tp = lax.axis_size("mp")
    x, dy = block_input[0], cotangent[0]
    params = (bias_qkv, bias_up, gain_first, shift_first, gain_second, shift_second)
    first_t, second_t, dy_t, gp, gu, act, att, h, col_sums, vec = pre(2.0 / tp, segment_ids, params, x, dy, weight_qkv, weight_up, weight_down, weight_out)
    g_up, g_qkv, g_down, g_out, block_output, grad_input, small, norms = tail(
        lax.axis_size("dp"), tp, vec, col_sums, segment_ids, bias_out, bias_down, second_t, first_t, dy_t, gu, gp, act, att, h, x, dy, weight_down, weight_out)
    g_up, g_qkv, g_down, g_out, block_output, grad_input, b_qkv, b_up, b_out, b_down, *norm_grads, norm_values = finish(
        4, (g_up, g_qkv, g_down, g_out, block_output, grad_input), small, norms, weight_qkv.shape[1], weight_up.shape[1])
    return (block_output[None], grad_input[None], g_qkv, b_qkv, g_out, b_out, g_up, b_up, g_down, b_down, *norm_grads, norm_values)


def solution(mesh):
    placed = (P("dp", None, None), P("dp", None), P("dp", None, None), P(None, "mp"), P("mp"), P("mp", None), P(), P(None, "mp"), P("mp"), P("mp", None),
              P(), P(), P(), P(), P())
    return jax.shard_map(
        shards,
        mesh=mesh,
        in_specs=placed,
        out_specs=(P("dp", "mp", None), P("dp", "mp", None), P("dp", "mp"), P("mp"), P("mp", "dp"), P(), P("dp", "mp"), P("mp"), P("mp", "dp"), P(), P(),
                   P(), P(), P(), P("dp", None)),
        check_vma=False,
    )
```

```python
import functools
import math

import jax
import jax.numpy as jnp
from jax import lax
from jax.experimental import pallas as pl
from jax.experimental.pallas import tpu as pltpu
from jax.sharding import PartitionSpec as P

HD = 64
ROT = 16
DOCS = 8
BLK = 256
LN_EPS = 1e-05
NORM_EPS = 1e-06
NEG = -1e30
F32 = jnp.float32
BF16 = jnp.bfloat16
VMEM_LIMIT = 60 * 1024 * 1024

TAIL = (0.099163489, 0.109273513, 0.0348237317, 0.263242867, -0.249259412, 0.332377466, -0.089621649)


def dot_nn(a, b):
    return lax.dot_general(a, b, (((1,), (0,)), ((), ())), preferred_element_type=F32)


def dot_nt(a, b):
    return lax.dot_general(a, b, (((1,), (1,)), ((), ())), preferred_element_type=F32)


def stats_of(x):
    mean = jnp.mean(x, axis=-1, keepdims=True)
    centred = x - mean
    var = jnp.mean(centred * centred, axis=-1, keepdims=True)
    inv = lax.rsqrt(var + LN_EPS)
    return centred * inv, inv


def gelu_parts(u):
    e = jnp.exp(u * u * -0.5)
    t = 1.0 / (1.0 + 0.25 * jnp.abs(u))
    r = jnp.full_like(t, TAIL[-1])
    for c in TAIL[-2::-1]:
        r = r * t + c
    tail = r * t * e
    cdf = jnp.where(u >= 0.0, 1.0 - tail, tail)
    return u * cdf, cdf + u * (e * (1.0 / math.sqrt(2.0 * math.pi)))


def full(shape):
    return pl.BlockSpec(shape, lambda *_: (0,) * len(shape))


MOST = 5


STRIP = 16
HALF = BLK // 2


def pre_kernel(share, seg_ref, bqkv_ref, bup_ref, g1_ref, s1_ref, g2_ref, s2_ref, x, dy, wqkv, wup, wdown, wout,
               first_o, second_o, dy_o, gp_o, gu_o, act_o, att_o, h_o, col_ref, vec_ref,
               xv, dyv, first, second, act, gu, gp, att, qt, kt, vt, gat, kf, vf, dkt, dvt, wqt, wu, wd, wo, hst, start, end, cosr, sinr, bq, moments, vec8, bias, ex, low, gprob, bounds,
               x_sem, dy_sem, w_sem, t_sem, h_sem, o_sem):
    tokens, width = xv.shape
    units, heads3 = act.shape[1], gp.shape[1]
    heads = att.shape[1]
    count = heads // HD
    blocks = tokens // BLK

    def block(i, n=1):
        return pl.ds(pl.multiple_of(i * BLK, BLK), n * BLK)

    def x_copy(i):
        return pltpu.make_async_copy(x.at[block(i)], xv.at[block(i)], x_sem.at[i])

    def dy_copy(i):
        return pltpu.make_async_copy(dy.at[block(i)], dyv.at[block(i)], dy_sem.at[i])

    raw = gp.at[pl.ds(0, width)]
    w_copies = [pltpu.make_async_copy(a, b, w_sem.at[n]) for n, (a, b) in enumerate(((wqkv, raw), (wout, wo), (wup, wu), (wdown, wd)))]
    w_copies[0].start()
    x_copy(0).start()
    dy_copy(0).start()
    for c in w_copies[1:]:
        c.start()
    x_copy(1).start()
    dy_copy(1).start()

    seg = seg_ref[...]
    edges = [jnp.sum((seg < d).astype(jnp.int32)) for d in range(1, DOCS)]
    bounds[0] = 0
    bounds[DOCS] = tokens
    begin, finish = jnp.zeros_like(seg), jnp.full_like(seg, tokens)
    for d in range(1, DOCS):
        bounds[d] = edges[d - 1]
        begin = jnp.where(seg >= d, edges[d - 1], begin)
    for d in range(DOCS - 1, 0, -1):
        finish = jnp.where(seg < d, edges[d - 1], finish)
    start[...] = begin
    end[...] = finish
    half = ROT // 2
    at_token = lax.broadcasted_iota(jnp.int32, (half, tokens), 1)
    freq = jnp.exp(lax.broadcasted_iota(jnp.int32, (half, tokens), 0).astype(F32) * (2.0 / ROT) * -math.log(10000.0))
    angle = (at_token - begin).astype(F32) * freq
    cosr[...] = jnp.cos(angle)
    sinr[...] = jnp.sin(angle)
    bqkv, bup, g1, s1, g2, s2 = (r[...].astype(F32).reshape(1, -1) for r in (bqkv_ref, bup_ref, g1_ref, s1_ref, g2_ref, s2_ref))
    bq[...] = jnp.broadcast_to(bqkv, (8, heads3)).T
    w_copies[0].wait()
    wqt[...] = raw[...].T

    def t_copies(i):
        return [pltpu.make_async_copy(low.at[n, pl.ds(0, width)], out.at[:, block(i)], t_sem.at[n]) for n, out in enumerate((first_o, second_o, dy_o))]

    def out_copy(n, src, out, i):
        return pltpu.make_async_copy(src.at[block(i)], out.at[block(i)], o_sem.at[n, i])

    outs = ((act, act_o), (gu, gu_o), (att, att_o), (gp, gp_o))

    def turn(v, c, s):
        a, b = v[:half], v[half:ROT]
        return jnp.concatenate([a * c - b * s, b * c + a * s, v[ROT:]], axis=0)

    def norm_block(i):
        for q in range(0, BLK, STRIP):
            at = pl.ds(pl.multiple_of(i * BLK + q, STRIP), STRIP)
            xs = xv[at, :].astype(F32)
            normed, inv = stats_of(xs)
            moments[at, 0:1] = jnp.mean(xs, axis=-1, keepdims=True)
            moments[at, 1:2] = inv
            first[at, :] = (normed * g1 + s1).astype(BF16)
            second[at, :] = (normed * g2 + s2).astype(BF16)

    x_copy(0).wait()
    norm_block(0)
    for c in w_copies[1:]:
        c.wait()

    @pl.loop(0, blocks)
    def _(i):
        at = block(i)
        dy_copy(i).wait()

        @pl.when(i + 1 < blocks)
        def _():
            x_copy(i + 1).wait()

        @pl.when(i + 2 < blocks)
        def _():
            x_copy(i + 2).start()
            dy_copy(i + 2).start()

        chunk = min(256, units)

        def ups(c):
            return dot_nn(second[at, :], wu[:, c:c + chunk]), dot_nt(dyv[at, :], wd[c:c + chunk, :])

        def gelu(c, made):
            for q in range(0, BLK, STRIP):
                strip = pl.ds(pl.multiple_of(i * BLK + q, STRIP), STRIP)
                value, slope = gelu_parts(made[0][q:q + STRIP] + bup[:, c:c + chunk])
                act[strip, c:c + chunk] = value.astype(BF16)
                gu[strip, c:c + chunk] = (made[1][q:q + STRIP] * slope).astype(BF16)

        pt = dot_nt(wqt[...], first[at, :])
        made = ups(0)
        for c in range(chunk, units, chunk):
            later = ups(c)
            gelu(c - chunk, made)
            made = later
        gat[:, at] = dot_nt(wo[...], dyv[at, :]).astype(BF16)
        gelu(units - chunk, made)

        @pl.when(i >= 1)
        def _():
            for copy in t_copies(i - 1):
                copy.wait()

        for n, rows_in in enumerate((first, second, dyv)):
            low[n, :width] = rows_in[at, :].T
        c, s = cosr[:, at], sinr[:, at]
        ks, vs = [], []
        for h in range(count):
            o = h * 3 * HD
            part = [pt[o + n * HD:o + (n + 1) * HD] + bq[o + n * HD:o + (n + 1) * HD, :1] for n in range(3)]
            qt[h * HD:(h + 1) * HD, at] = (turn(part[0], c, s).astype(BF16).astype(F32) * (1.0 / math.sqrt(HD))).astype(BF16)
            ks.append(turn(part[1], c, s).astype(BF16))
            vs.append(part[2].astype(BF16))
            kt[h * HD:(h + 1) * HD, at] = ks[h]
            vt[h * HD:(h + 1) * HD, at] = vs[h]
        kb, vb = jnp.concatenate(ks, axis=0), jnp.concatenate(vs, axis=0)
        kf[at, :] = kb.T
        vf[at, :] = vb.T
        for copy in (*t_copies(i), out_copy(0, act, act_o, i), out_copy(1, gu, gu_o, i)):
            copy.start()
        pl.when(i + 1 < blocks)(lambda: norm_block(i + 1))

    for copy in t_copies(blocks - 1):
        copy.wait()

    dkt[...] = jnp.zeros_like(dkt)
    dvt[...] = jnp.zeros_like(dvt)

    def low_block(i):
        lowest = 0
        for d in range(1, DOCS):
            lowest = jnp.maximum(lowest, jnp.where(bounds[d] <= i * BLK, bounds[d], 0))
        return lax.div(lowest, BLK)

    def end_of(j):
        last = j * BLK + BLK - 1
        highest = tokens
        for d in range(1, DOCS):
            highest = jnp.minimum(highest, jnp.where(bounds[d] > last, bounds[d], tokens))
        return highest

    def attend(i, lo, n):
        at, keys, size = block(i), block(lo, n), n * BLK
        strips = [slice(r, r + STRIP) for r in range(0, size, STRIP)]
        k_off = lax.broadcasted_iota(jnp.int32, (STRIP, BLK), 0)
        last = i * BLK - lo * BLK + lax.broadcasted_iota(jnp.int32, (1, BLK), 1)
        lead = start[:, at] - lo * BLK
        for r in strips:
            k_at = k_off + r.start
            bias[r] = jnp.where((k_at <= last) & (k_at >= lead), 0.0, NEG)
        blank = jnp.zeros((HD, BLK), BF16)
        span = min(2 * HD, heads)

        def spread(v, h):
            return jnp.concatenate([v if g == h % (span // HD) else blank for g in range(span // HD)], axis=0)

        def lanes(h):
            return slice(h * HD // span * span, h * HD // span * span + span)

        def rows_of(h):
            return slice(h * HD, (h + 1) * HD)

        atts, dqs, share_of = {}, {}, {}

        def stage_a(h):
            ex[h, :size] = dot_nn(kf[keys, lanes(h)], spread(qt[rows_of(h), at], h))

        def stage_b(h):
            best = jnp.full((STRIP, BLK), NEG, F32)
            for r in strips:
                s = ex[h, r] + bias[r]
                ex[h, r] = s
                best = jnp.maximum(best, s)
            best = jnp.max(best, axis=0, keepdims=True)
            total = jnp.zeros((STRIP, BLK), F32)
            for r in strips:
                e = jnp.exp(ex[h, r] - best)
                ex[h, r] = e
                total = total + e
            share_of[h] = 1.0 / jnp.sum(total, axis=0, keepdims=True)
            for r in strips:
                low[h, r] = (ex[h, r] * share_of[h]).astype(BF16)

        def stage_c(h):
            atts[h] = dot_nn(vt[rows_of(h), keys], low[h, :size])
            gprob[h % 2, :size] = dot_nn(vf[keys, lanes(h)], spread(gat[rows_of(h), at], h))
            dvt[rows_of(h), keys] += dot_nt(gat[rows_of(h), at], low[h, :size])

        def stage_d(h):
            delta = jnp.sum(atts[h] * gat[rows_of(h), at].astype(F32), axis=0, keepdims=True)
            for r in strips:
                low[h, r] = (ex[h, r] * share_of[h] * (gprob[h % 2, r] - delta)).astype(BF16)

        def stage_e(h):
            dqs[h] = dot_nn(kt[rows_of(h), keys], low[h, :size])
            dkt[rows_of(h), keys] += dot_nt(qt[rows_of(h), at], low[h, :size])

        stages = (stage_a, stage_b, stage_c, stage_d, stage_e)
        for t in range(count + len(stages) - 1):
            for k, stage in enumerate(stages):
                if 0 <= t - k < count:
                    stage(t - k)
        att[at, :] = jnp.concatenate([atts[h] for h in range(count)], axis=0).T.astype(BF16)
        c, sn = cosr[:, at], -sinr[:, at]
        qt[:, at] = jnp.concatenate([turn(dqs[h] * (1.0 / math.sqrt(HD)), c, sn) for h in range(count)], axis=0).astype(BF16)

    @pl.loop(0, blocks)
    def _(i):
        lo = low_block(i)
        for n in range(1, MOST + 1):
            pl.when(i - lo + 1 == n)(functools.partial(attend, i, lo, n))
        out_copy(2, att, att_o, i).start()

    vec8[...] = jnp.zeros_like(vec8)
    chunk = min(256, width)

    def spare(what, c, strip):
        k = c // chunk * 3 + what
        return ex.at[k % count, pl.ds(k // count * BLK + strip.start, strip.stop - strip.start)]

    def h_copy(i):
        slot = lax.rem(i, 2)
        return pltpu.make_async_copy(hst.at[slot], h_o.at[block(i)], h_sem.at[slot])

    def doc_of(t):
        return sum(jnp.where(bounds[d] <= t, 1, 0) for d in range(1, DOCS))

    @pl.loop(0, blocks)
    def _(i):
        at = block(i)
        c, sn = cosr[:, at], -sinr[:, at]
        pieces = []
        for h in range(count):
            r = slice(h * HD, (h + 1) * HD)
            pieces += [qt[r, at], turn(dkt[r, at], c, sn).astype(BF16), dvt[r, at].astype(BF16)]
        gp[at, :] = jnp.concatenate(pieces, axis=0).T
        out_copy(3, gp, gp_o, i).start()

        @pl.when(i >= 2)
        def _():
            h_copy(i - 2).wait()

        slot = lax.rem(i, 2)

        def grads(c):
            return dot_nt(gu[at, :], wu[c:c + chunk, :]), dot_nn(gp[at, :], wqt[:, c:c + chunk])

        def use(c, made):
            cut = slice(c, c + chunk)
            for q in range(0, BLK, STRIP):
                strip = slice(q, q + STRIP)
                gs, gf = made[0][strip], made[1][strip]
                spare(0, c, strip)[...] = gf
                spare(1, c, strip)[...] = gs
                hst[slot, strip, cut] = (gf * g1[:, cut] + gs * g2[:, cut]).astype(BF16)

        made = grads(0)
        for q in range(0, BLK, STRIP):
            here = pl.ds(pl.multiple_of(i * BLK + q, STRIP), STRIP)
            normed = (xv[here, :].astype(F32) - moments[here, 0:1]) * moments[here, 1:2]
            for c in range(0, width, chunk):
                spare(2, c, slice(q, q + STRIP))[...] = normed[:, c:c + chunk]
        for c in range(chunk, width, chunk):
            later = grads(c)
            use(c - chunk, made)
            made = later
        use(width - chunk, made)
        h_copy(i).start()
        at_row = lax.broadcasted_iota(jnp.int32, (STRIP, chunk), 0)

        @pl.loop(doc_of(i * BLK), doc_of(i * BLK + BLK - 1) + 1)
        def _(d):
            low_row, high_row = bounds[d] - i * BLK, bounds[d + 1] - i * BLK
            for c in range(0, width, chunk):
                sums = [jnp.zeros((STRIP, chunk), F32)] * 4
                for q in range(0, BLK, STRIP):
                    strip = slice(q, q + STRIP)
                    inside = (at_row >= low_row - q) & (at_row < high_row - q)
                    gf, gs = (jnp.where(inside, spare(k, c, strip)[...], 0.0) for k in range(2))
                    normed = spare(2, c, strip)[...]
                    sums = [s + v for s, v in zip(sums, (gf * normed, gf, gs * normed, gs))]
                for n in range(4):
                    vec8[n, d, :, c:c + chunk] += sums[n][:8] + sums[n][8:]

    vec_ref[...] = jnp.sum(vec8[...], axis=2)

    pairs_of = ((first, gp, 1.0), (second, gu, 1.0))

    def gram_block(j, first_row, size):
        at, cols = pl.ds(pl.multiple_of(first_row, HALF), size), block(j)

        def gram(m):
            return dot_nt(m[at, :], m[cols, :])

        grams = [(gram(a), plus, gram(b)) for a, b, plus in pairs_of] + [(gram(att) + gram(act), share, gram(dyv))]
        ahead = lax.broadcasted_iota(jnp.int32, (STRIP, BLK), 0) - lax.broadcasted_iota(jnp.int32, (STRIP, BLK), 1)
        reach = end[:, cols] - first_row
        row_off = lax.broadcasted_iota(jnp.int32, (STRIP, BLK), 0)
        total = jnp.zeros((STRIP, BLK), F32)
        for r in range(0, size, STRIP):
            terms = None
            for a, plus, b in grams:
                term = (a[r:r + STRIP] + plus) * b[r:r + STRIP]
                terms = term if terms is None else terms + term
            gap = ahead + (first_row - j * BLK + r)
            weight = jnp.where(gap > 0, 2.0, jnp.where(gap == 0, 1.0, 0.0))
            total = total + jnp.where(row_off + r < reach, terms * weight, 0.0)
        col_ref[:, cols] += total[:8] + total[8:]

    col_ref[...] = jnp.zeros_like(col_ref)

    @pl.loop(0, blocks)
    def _(j):
        total = lax.div(end_of(j) - j * BLK + HALF - 1, HALF)
        pl.loop(0, lax.div(total, 4))(lambda s: gram_block(j, j * BLK + s * 4 * HALF, 4 * HALF))
        for n in range(1, 4):
            pl.when(lax.rem(total, 4) == n)(lambda n=n: gram_block(j, j * BLK + (total - n) * HALF, n * HALF))

    for i in (blocks - 2, blocks - 1):
        h_copy(i).wait()

    @pl.loop(0, blocks)
    def _(i):
        for n, (src, out) in enumerate(outs):
            out_copy(n, src, out, i).wait()


def pre(share, seg, params, x, dy, wqkv, wup, wdown, wout):
    tokens, width = x.shape
    heads3, units, heads = wqkv.shape[1], wup.shape[1], wout.shape[0]
    blocks = tokens // BLK
    hbm, vmem = pl.BlockSpec(memory_space=pl.ANY), pl.BlockSpec(memory_space=pltpu.VMEM)
    V, D = pltpu.VMEM, pltpu.SemaphoreType.DMA
    t_shape, S = (width, tokens), jax.ShapeDtypeStruct
    return pl.pallas_call(
        functools.partial(pre_kernel, share),
        in_specs=[vmem] * 7 + [hbm] * 6,
        out_specs=[hbm] * 8 + [vmem] * 2,
        out_shape=[S(t_shape, BF16)] * 3 + [S((tokens, n), BF16) for n in (heads3, units, units, heads, width)] + [S((8, tokens), F32), S((4, DOCS, width), F32)],
        scratch_shapes=[V((tokens, width), BF16)] * 4 + [V((tokens, units), BF16)] * 2 + [V((tokens, heads3), BF16), V((tokens, heads), BF16)]
        + [V((heads, tokens), BF16)] * 4 + [V((tokens, heads), BF16)] * 2 + [V((heads, tokens), F32)] * 2
        + [V((heads3, width), BF16), V((width, units), BF16), V((units, width), BF16), V((heads, width), BF16), V((2, BLK, width), BF16)]
        + [V((1, tokens), jnp.int32)] * 2 + [V((ROT // 2, tokens), F32)] * 2 + [V((heads3, 8), F32), V((tokens, 2), F32), V((4, DOCS, 8, width), F32)]
        + [V((MOST * BLK, BLK), F32), V((heads // HD, max(MOST, -(-3 * width // BLK // (heads // HD))) * BLK, BLK), F32), V((max(heads // HD, 3), MOST * BLK, BLK), BF16), V((2, MOST * BLK, BLK), F32)]
        + [pltpu.SMEM((DOCS + 1,), jnp.int32)]
        + [D((blocks,)), D((blocks,)), D((4,)), D((3,)), D((2,)), D((4, blocks))],
        compiler_params=pltpu.CompilerParams(vmem_limit_bytes=63 * 1024 * 1024),
        name="pre",
    )(seg, *params, x, dy, wqkv, wup, wdown, wout)


LOAD_AHEAD = 4
LAG = 3


def bit_of(index, bit):
    return lax.rem(lax.div(index, 2**bit), 2)


def across(index, bit):
    return index + (1 - 2 * bit_of(index, bit)) * 2**bit


def log2(n):
    return n.bit_length() - 1


def remote(src, dst, send, recv, axis, index):
    return pltpu.make_async_remote_copy(src_ref=src, dst_ref=dst, send_sem=send, recv_sem=recv, device_id={axis: index}, device_id_type=pl.DeviceIdType.MESH)


def tail_kernel(n, tp, w, vec_ref, col_ref, seg_ref, b1_ref, b2_ref, second_t, first_t, dy_t, gu, gp, act, att, h, x, dy, wdown, wout,
                gup_ref, gq_ref, gdown_ref, gout_ref, bo_ref, gi_ref, small_ref, norm_ref,
                at, b, snd, rcv, keep, oacc, hown, hs, hr, bs, br, wd, xr, dyr, trow, tcol, vsend, vrecv, bsum, smine, sall,
                at_sem, b_sem, w_sem, snd_sem, rcv_sem, hs_sem, hr_sem, bs_sem, br_sem, gs_sem, gr_sem, ss_sem, sr_sem, hown_sem, row_sem, gi_stage, bo_stage, out_sem):
    width, tokens = first_t.shape
    me, m = lax.axis_index("dp"), lax.axis_index("mp")
    nb, mb = log2(n), log2(tp)
    shard, rows_own = width // n, tokens // tp
    nu, nq, na, ne = (r.shape[1] // w for r in (gu, gp, act, att))
    units = nu + nq + na + ne

    sources = (second_t, first_t, dy_t)

    def place(p):
        return sum(((p >> (nb - 1 - k)) & 1) << k for k in range(nb))

    def load_at(mat):
        for p in range(n):
            pltpu.make_async_copy(sources[mat].at[pl.ds(place(p) * shard, shard)], at.at[mat, pl.ds(p * shard, shard)], at_sem.at[mat]).start()

    def load_b(base, src):
        for i in range(src.shape[1] // w):
            pltpu.make_async_copy(src.at[:, pl.ds(i * w, w)], b.at[base + i], b_sem.at[base + i]).start()

    load_at(0)
    load_b(0, gu)
    def vec_exchange(k):
        return remote(vsend.at[k], vrecv.at[k], gs_sem.at[k], gr_sem.at[k], "mp", across(m, k))

    hot = seg_ref[...] == lax.broadcasted_iota(jnp.int32, (DOCS, tokens), 0)
    mine = jnp.sum(jnp.where(hot, jnp.sum(col_ref[...], axis=0, keepdims=True), 0.0), axis=1, keepdims=True)
    vsend[0, :4] = vec_ref[...]
    vsend[0, 4] = jnp.broadcast_to(mine, (DOCS, width))

    barrier = pltpu.get_barrier_semaphore()
    for r in range(1, n):
        pl.semaphore_signal(barrier, inc=1, device_id={"dp": lax.rem(me + r, n)}, device_id_type=pl.DeviceIdType.MESH)
    for r in range(1, tp):
        pl.semaphore_signal(barrier, inc=1, device_id={"mp": lax.rem(m + r, tp)}, device_id_type=pl.DeviceIdType.MESH)
    pl.semaphore_wait(barrier, n - 1 + tp - 1)

    vec_exchange(0).start()

    split = act.shape[1]
    wd_copies = (pltpu.make_async_copy(wdown, wd.at[pl.ds(0, split)], w_sem.at[0]), pltpu.make_async_copy(wout, wd.at[pl.ds(split, wd.shape[0] - split)], w_sem.at[1]))
    own_at = pl.ds(m * rows_own, rows_own)
    row_copies = (pltpu.make_async_copy(x.at[own_at], xr, row_sem.at[0]), pltpu.make_async_copy(dy.at[own_at], dyr, row_sem.at[1]))
    hown_copies = [pltpu.make_async_copy(h.at[pl.ds((2 * j + bit_of(m, 0)) * rows_own, rows_own)], hown.at[j], hown_sem.at[j]) for j in range(tp // 2)]

    for k in range(mb):
        vec_exchange(k).wait_recv()
        vsend[k + 1] = vsend[k] + vrecv[k]
        if k + 1 < mb:
            vec_exchange(k + 1).start()
        if k == 0:
            load_at(1)
            load_b(nu, gp)
    load_at(2)
    load_b(nu + nq, act)
    load_b(nu + nq + na, att)
    for c in (*wd_copies, *row_copies, *hown_copies):
        c.start()

    for j in range(tp // 2):
        there = 2 * j + 1 - bit_of(m, 0)
        remote(h.at[pl.ds(there * rows_own, rows_own)], hr[0].at[j], hs_sem.at[0, j], hr_sem.at[0, j], "mp", across(m, 0)).start()

    squares = vsend[mb, 4, :, :1]
    for j in range(4):
        squares = squares + jnp.sum(vsend[mb, j] * vsend[mb, j], axis=1, keepdims=True)
    norm = jnp.sqrt(squares + NORM_EPS)
    norm_ref[...] = jnp.broadcast_to(norm, norm_ref.shape)
    clip = jnp.minimum(1.0, jnp.mean(norm, axis=0, keepdims=True) / norm)
    per_token = jnp.sum(jnp.where(hot, clip, 0.0), axis=0, keepdims=True)
    trow[...] = per_token
    tcol[...] = jnp.broadcast_to(per_token, (DOCS, tokens)).T
    smine[...] = jnp.zeros_like(smine)
    for j in range(4):
        smine[3 + j:4 + j, :] = jnp.sum(vsend[mb, j] * clip, axis=0, keepdims=True)

    orders = (tuple(range(nb)), tuple(range(1, nb)) + (0,))

    def z_first(u):
        return (u == 1) | (u == units - 3)

    def by_order(u, body):
        pl.when(jnp.logical_not(z_first(u)))(functools.partial(body, orders[0]))
        pl.when(z_first(u))(functools.partial(body, orders[1]))

    def matrix_of(u):
        return jnp.where(u >= nu, 1, 0) + jnp.where(u >= nu + nq, 1, 0)

    def exchange(order, k, u):
        return remote(snd[k].at[u], rcv[k].at[u], snd_sem.at[k, u], rcv_sem.at[k, u], "dp", across(me, order[k]))

    def pieces(bit, side):
        size = width >> (bit + 1)
        return [pl.ds(pl.multiple_of((2 * g + side) * size, size), size) for g in range(2**bit)], size

    def other_half(mat, clipped, u):
        pltpu.make_async_copy(gu.at[:, pl.ds(0, w)], b.at[u], b_sem.at[u]).wait()
        if clipped:
            scaled = b[u].astype(F32) * tcol[:, :1]
            b[u] = scaled.astype(BF16)
            bsum[u] = jnp.sum(scaled.reshape(tokens // 8, 8, w), axis=0)

        def send(order):
            away, size = pieces(order[0], 1 - bit_of(me, order[0]))
            for g, piece in enumerate(away):
                snd[0][u, g * size:(g + 1) * size, :] = dot_nn(at[mat, piece, :], b[u]).astype(BF16)

            @pl.when(u < LOAD_AHEAD)
            def _():
                exchange(order, 0, u).start()

        by_order(u, send)

    def at_ready(mat):
        pltpu.make_async_copy(sources[mat], at.at[mat], at_sem.at[mat]).wait()

    at_ready(0)
    pl.loop(0, nu)(lambda u: other_half(0, True, u))
    at_ready(1)
    pl.loop(nu, nu + nq)(lambda u: other_half(1, True, u))
    at_ready(2)
    for p in range(n):
        piece = pl.ds(p * shard, shard)
        scaled = at[2, piece, :].astype(F32) * trow[...]
        at[2, piece, :] = scaled.astype(BF16)
        folded = scaled[:, :128]
        for k in range(1, tokens // 128):
            folded = folded + scaled[:, k * 128:(k + 1) * 128]
        smine[2:3, place(p) * shard:(place(p) + 1) * shard] = jnp.sum(folded.T, axis=0, keepdims=True)
    pl.loop(nu + nq, units)(lambda u: other_half(2, False, u))

    for i in range(nq):
        smine[0:1, i * w:(i + 1) * w] = jnp.sum(bsum[nu + i], axis=0, keepdims=True)
    for i in range(nu):
        smine[1:2, i * w:(i + 1) * w] = jnp.sum(bsum[i], axis=0, keepdims=True)
    sall[me] = smine[...]
    for r in range(1, n):
        remote(smine, sall.at[me], ss_sem.at[r - 1], sr_sem.at[me], "dp", lax.rem(me + r, n)).start()

    chunk = min(rows_own, 256)
    def branch(owner, c, chunk=chunk):
        at_rows = pl.ds(pl.multiple_of(owner * rows_own + c * chunk, chunk), chunk)
        left = jnp.concatenate([b[nu + nq + i, at_rows, :] for i in range(na + ne)], axis=1)
        return dot_nn(left, wd[...])

    def chunks(body):
        pl.loop(0, rows_own // chunk)(lambda c: body(c, pl.ds(pl.multiple_of(c * chunk, chunk), chunk)))

    def slot(owner, k):
        return lax.div(owner, 2 ** (k + 1))

    def wait_mp(k, buf, recv_sem, send_sem):
        for j in range(tp >> (k + 1)):
            remote(buf[k].at[j], buf[k].at[j], send_sem.at[k, j], recv_sem.at[k, j], "mp", across(m, k)).wait_recv()

    def owner_of(k, j):
        return (2 * j + 1 - bit_of(m, k)) * 2**k + lax.rem(m, 2**k)

    def h_task(k, j):
        if j == 0:
            if k == 1:
                for c in hown_copies:
                    c.wait()
            wait_mp(k - 1, hr, hr_sem, hs_sem)
        owner = owner_of(k, j)

        def h_send(c, rows_at):
            val = hown[slot(owner, 0), rows_at, :].astype(F32)
            for r in range(k):
                val = val + hr[r][slot(owner, r), rows_at, :].astype(F32)
            hs[k - 1][j, rows_at, :] = val.astype(BF16)

        chunks(h_send)
        remote(hs[k - 1].at[j], hr[k].at[j], hs_sem.at[k, j], hr_sem.at[k, j], "mp", across(m, k)).start()

    def b_task(k, j):
        if k == 0 and j == 0:
            for c in wd_copies:
                c.wait()
        if k > 0 and j == 0:
            wait_mp(k - 1, br, br_sem, bs_sem)
        owner = owner_of(k, j)

        def b_send(c, rows_at):
            val = branch(owner, c)
            for r in range(k):
                val = val + br[r][slot(owner, r), rows_at, :].astype(F32)
            bs[k][j, rows_at, :] = val.astype(BF16)

        chunks(b_send)
        remote(bs[k].at[j], br[k].at[j], bs_sem.at[k, j], br_sem.at[k, j], "mp", across(m, k)).start()

    tasks = [functools.partial(h_task, 1, j) for j in range(tp // 4)] + [functools.partial(b_task, 0, j) for j in range(tp // 2)]
    for k in range(1, mb):
        tasks += [functools.partial(h_task, k, j) for j in range(tp >> (k + 1)) if k > 1]
        tasks += [functools.partial(b_task, k, j) for j in range(tp >> (k + 1))]

    def split(val, pos, bit):
        size = val.shape[0] >> (pos + 1)
        low = [val[2 * g * size:(2 * g + 1) * size] for g in range(2**pos)]
        high = [val[(2 * g + 1) * size:(2 * g + 2) * size] for g in range(2**pos)]
        low, high = (v[0] if len(v) == 1 else jnp.concatenate(v, axis=0) for v in (low, high))
        return jnp.where(bit == 1, low, high), jnp.where(bit == 1, high, low)

    def later(k, u):
        def body(order):
            exchange(order, k, u).wait_recv()
            val = keep[k - 1][lax.rem(u, LAG + 1)] + rcv[k][u].astype(F32)
            if k == nb - 1:
                oacc[u] = val
                return
            pos = 1 if order[0] != 0 and k + 1 < nb - 1 else 0
            away, stay = split(val, pos, bit_of(me, order[k + 1]))
            snd[k + 1][u] = away.astype(BF16)
            keep[k][lax.rem(u, LAG + 1)] = stay
            exchange(order, k + 1, u).start()

        by_order(u, body)

    def first(u):
        mat = matrix_of(u)

        def body(order):
            exchange(order, 0, u).wait_recv()
            near, size = pieces(order[0], bit_of(me, order[0]))
            for g, piece in enumerate(near):
                val = dot_nn(at[mat, piece, :], b[u]) + rcv[0][u, g * size:(g + 1) * size, :].astype(F32)
                away, stay = split(val, 0, bit_of(me, order[1]))
                part = size // 2
                snd[1][u, g * part:(g + 1) * part, :] = away.astype(BF16)
                keep[0][lax.rem(u, LAG + 1), g * part:(g + 1) * part, :] = stay
            exchange(order, 1, u).start()

        by_order(u, body)

        @pl.when(u + LOAD_AHEAD < units)
        def _():
            by_order(u + LOAD_AHEAD, lambda order: exchange(order, 0, u + LOAD_AHEAD).start())

    def step(t):
        for k in range(nb - 1, 0, -1):
            pl.when((t >= k * LAG) & (t < units + k * LAG))(functools.partial(later, k, t - k * LAG))
        pl.when(t < units)(functools.partial(first, t))
        for spot, task in enumerate(tasks):
            pl.when(t == min(spot, units - 1))(task)

    pl.loop(0, units)(step)

    for c in row_copies:
        c.wait()
    wait_mp(mb - 1, hr, hr_sem, hs_sem)
    wait_mp(mb - 1, br, br_sem, bs_sem)

    fine = min(rows_own, 128)
    bias = (b1_ref[...].astype(F32) + b2_ref[...].astype(F32)).reshape(1, width)

    def out_copies(c):
        spot = lax.rem(c, 2)
        to = pl.ds(pl.multiple_of(c * fine, fine), fine)
        return (pltpu.make_async_copy(gi_stage.at[spot], gi_ref.at[to], out_sem.at[0, spot]),
                pltpu.make_async_copy(bo_stage.at[spot], bo_ref.at[to], out_sem.at[1, spot]))

    def finish(c):
        spot = lax.rem(c, 2)
        rows_at = pl.ds(pl.multiple_of(c * fine, fine), fine)

        @pl.when(c >= 2)
        def _():
            for copy in out_copies(c - 2):
                copy.wait()

        val = hown[slot(m, 0), rows_at, :].astype(F32)
        for r in range(mb):
            val = val + hr[r][slot(m, r), rows_at, :].astype(F32)
        xs = xr[rows_at, :].astype(F32)
        normed, inv = stats_of(xs)
        back_x = inv * (val - jnp.mean(val, axis=-1, keepdims=True) - normed * jnp.mean(val * normed, axis=-1, keepdims=True))
        gi_stage[spot] = dyr[rows_at, :].astype(F32) + back_x
        out = branch(m, c, fine) + (xs + bias)
        for r in range(mb):
            out = out + br[r][slot(m, r), rows_at, :].astype(F32)
        bo_stage[spot] = out.astype(BF16)
        for copy in out_copies(c):
            copy.start()

    pl.loop(0, rows_own // fine)(finish)
    pl.loop(units, units + (nb - 1) * LAG)(step)

    for i in range(nu):
        gup_ref[:, i * w:(i + 1) * w] = oacc[i]
    for i in range(nq):
        gq_ref[:, i * w:(i + 1) * w] = oacc[nu + i]
    for i in range(na):
        gdown_ref[i * w:(i + 1) * w, :] = oacc[nu + nq + i].T
    for i in range(ne):
        gout_ref[i * w:(i + 1) * w, :] = oacc[nu + nq + na + i].T
    for r in range(1, n):
        src = lax.rem(me + r, n)
        remote(smine, sall.at[src], ss_sem.at[r - 1], sr_sem.at[src], "dp", src).wait_recv()
    total = sall[0]
    for r in range(1, n):
        total = total + sall[r]
    small_ref[...] = total

    for c in range(max(rows_own // fine - 2, 0), rows_own // fine):
        for copy in out_copies(c):
            copy.wait()

    @pl.loop(0, units)
    def _(u):
        for k in range(nb):
            exchange(orders[0], k, u).wait_send()

    for r in range(1, n):
        remote(smine, sall.at[me], ss_sem.at[r - 1], sr_sem.at[me], "dp", lax.rem(me + r, n)).wait_send()
    for k in range(mb):
        vec_exchange(k).wait_send()
    for k in range(mb):
        for j in range(tp >> (k + 1)):
            src_h = h.at[pl.ds(0, rows_own)] if k == 0 else hs[k - 1].at[j]
            remote(src_h, hr[k].at[j], hs_sem.at[k, j], hr_sem.at[k, j], "mp", across(m, k)).wait_send()
            remote(bs[k].at[j], br[k].at[j], bs_sem.at[k, j], br_sem.at[k, j], "mp", across(m, k)).wait_send()


def tail(n, tp, vec, col, seg, b1, b2, second_t, first_t, dy_t, gu, gp, act, att, h, x, dy, wdown, wout):
    width, tokens = first_t.shape
    widths = [a.shape[1] for a in (gu, gp, act, att)]
    w = BLK if all(v % BLK == 0 for v in widths) else BLK // 2
    units = sum(widths) // w
    nb, mb = log2(n), log2(tp)
    shard, own = width // n, tokens // tp
    hbm = pl.BlockSpec(memory_space=pl.ANY)
    vmem = pl.BlockSpec(memory_space=pltpu.VMEM)
    V, D = pltpu.VMEM, pltpu.SemaphoreType.DMA
    mp_bufs = lambda lo: [V((tp >> (k + 1), own, width), BF16) for k in range(lo, mb)]
    step_bufs = lambda: [V((units, width >> (k + 1), w), BF16) for k in range(nb)]
    return pl.pallas_call(
        functools.partial(tail_kernel, n, tp, w),
        in_specs=[vmem] * 5 + [hbm] * 12,
        out_specs=[vmem] * 4 + [hbm] * 2 + [vmem] * 2,
        out_shape=[jax.ShapeDtypeStruct(s, t) for s, t in (
            ((shard, widths[0]), F32), ((shard, widths[1]), F32), ((widths[2], shard), F32), ((widths[3], shard), F32),
            ((own, width), BF16), ((own, width), F32), ((8, width), F32), ((DOCS, 128), F32))],
        scratch_shapes=[
            V((3, width, tokens), BF16), V((units, tokens, w), BF16), step_bufs(), step_bufs(), [V((LAG + 1, width >> (k + 1), w), F32) for k in range(1, nb)],
            V((units, shard, w), F32), V((tp // 2, own, width), BF16), mp_bufs(1), mp_bufs(0), mp_bufs(0), mp_bufs(0),
            V((wdown.shape[0] + wout.shape[0], width), BF16), V((own, width), BF16), V((own, width), BF16), V((1, tokens), F32), V((tokens, DOCS), F32),
            V((mb + 1, 5, DOCS, width), F32), V((mb, 5, DOCS, width), F32), V((units, 8, w), F32), V((8, width), F32), V((n, 8, width), F32),
            D((3,)), D((units,)), D((2,)), D((nb, units)), D((nb, units)), D((mb, tp // 2)), D((mb, tp // 2)), D((mb, tp // 2)), D((mb, tp // 2)),
            D((mb,)), D((mb,)), D((n - 1,)), D((n,)), D((tp // 2,)), D((2,)), V((2, min(own, 128), width), F32), V((2, min(own, 128), width), BF16), D((2, 2))],
        compiler_params=pltpu.CompilerParams(collective_id=1, has_side_effects=True, vmem_limit_bytes=64 * 1024 * 1024 - 1024 * 1024),
        name="tail",
    )(vec, col, seg, b1, b2, second_t, first_t, dy_t, gu, gp, act, att, h, x, dy, wdown, wout)


def finish_kernel(*refs):
    large, (small_ref, norm_ref) = refs[:6], refs[6:8]
    outs, (bq, bu, bo, bd, *norms), norm_out = refs[8:14], refs[14:22], refs[22]
    for src, dst in zip(large, outs):
        dst[...] = src[...]

    @pl.when(pl.program_id(0) == 0)
    def _():
        bq[...] = small_ref[0, :bq.shape[0]]
        bu[...] = small_ref[1, :bu.shape[0]]
        bo[...] = small_ref[2, :]
        bd[...] = small_ref[2, :]
        for k, ref in enumerate(norms):
            ref[...] = small_ref[3 + k, :]
        at = lax.broadcasted_iota(jnp.int32, (DOCS, 128), 0) == lax.broadcasted_iota(jnp.int32, (DOCS, 128), 1)
        norm_out[...] = jnp.sum(jnp.where(at, norm_ref[...], 0.0), axis=0, keepdims=True)[:, :DOCS]


def finish(steps, large, small, norms, heads3, units):
    width = small.shape[1]
    S = jax.ShapeDtypeStruct
    cut = lambda a: pl.BlockSpec((a.shape[0] // steps, a.shape[1]), lambda i: (i, 0))
    vectors = [heads3, units] + [width] * 6
    return pl.pallas_call(
        finish_kernel,
        grid=(steps,),
        in_specs=[cut(a) for a in large] + [full(small.shape), full(norms.shape)],
        out_specs=[cut(a) for a in large] + [full((v,)) for v in vectors] + [full((1, DOCS))],
        out_shape=[S(a.shape, a.dtype) for a in large] + [S((v,), F32) for v in vectors] + [S((1, DOCS), F32)],
        name="finish",
    )(*large, small, norms)


def shards(block_input, segment_ids, cotangent, weight_qkv, bias_qkv, weight_out, bias_out, weight_up, bias_up, weight_down, bias_down,
           gain_first, shift_first, gain_second, shift_second):
    tp = lax.axis_size("mp")
    x, dy = block_input[0], cotangent[0]
    params = (bias_qkv, bias_up, gain_first, shift_first, gain_second, shift_second)
    first_t, second_t, dy_t, gp, gu, act, att, h, col_sums, vec = pre(2.0 / tp, segment_ids, params, x, dy, weight_qkv, weight_up, weight_down, weight_out)
    g_up, g_qkv, g_down, g_out, block_output, grad_input, small, norms = tail(
        lax.axis_size("dp"), tp, vec, col_sums, segment_ids, bias_out, bias_down, second_t, first_t, dy_t, gu, gp, act, att, h, x, dy, weight_down, weight_out)
    g_up, g_qkv, g_down, g_out, block_output, grad_input, b_qkv, b_up, b_out, b_down, *norm_grads, norm_values = finish(
        4, (g_up, g_qkv, g_down, g_out, block_output, grad_input), small, norms, weight_qkv.shape[1], weight_up.shape[1])
    return (block_output[None], grad_input[None], g_qkv, b_qkv, g_out, b_out, g_up, b_up, g_down, b_down, *norm_grads, norm_values)


def solution(mesh):
    placed = (P("dp", None, None), P("dp", None), P("dp", None, None), P(None, "mp"), P("mp"), P("mp", None), P(), P(None, "mp"), P("mp"), P("mp", None),
              P(), P(), P(), P(), P())
    return jax.shard_map(
        shards,
        mesh=mesh,
        in_specs=placed,
        out_specs=(P("dp", "mp", None), P("dp", "mp", None), P("dp", "mp"), P("mp"), P("mp", "dp"), P(), P("dp", "mp"), P("mp"), P("mp", "dp"), P(), P(),
                   P(), P(), P(), P("dp", None)),
        check_vma=False,
    )
```

```python
import functools
import math

import jax
import jax.numpy as jnp
from jax import lax
from jax.experimental import pallas as pl
from jax.experimental.pallas import tpu as pltpu
from jax.sharding import PartitionSpec as P

HD = 64
ROT = 16
DOCS = 8
BLK = 256
LN_EPS = 1e-05
NORM_EPS = 1e-06
NEG = -1e30
F32 = jnp.float32
BF16 = jnp.bfloat16
VMEM_LIMIT = 60 * 1024 * 1024

TAIL = (0.099163489, 0.109273513, 0.0348237317, 0.263242867, -0.249259412, 0.332377466, -0.089621649)


def dot_nn(a, b):
    return lax.dot_general(a, b, (((1,), (0,)), ((), ())), preferred_element_type=F32)


def dot_nt(a, b):
    return lax.dot_general(a, b, (((1,), (1,)), ((), ())), preferred_element_type=F32)


def stats_of(x):
    mean = jnp.mean(x, axis=-1, keepdims=True)
    centred = x - mean
    var = jnp.mean(centred * centred, axis=-1, keepdims=True)
    inv = lax.rsqrt(var + LN_EPS)
    return centred * inv, inv


def gelu_parts(u):
    e = jnp.exp(u * u * -0.5)
    t = 1.0 / (1.0 + 0.25 * jnp.abs(u))
    r = jnp.full_like(t, TAIL[-1])
    for c in TAIL[-2::-1]:
        r = r * t + c
    tail = r * t * e
    cdf = jnp.where(u >= 0.0, 1.0 - tail, tail)
    return u * cdf, cdf + u * (e * (1.0 / math.sqrt(2.0 * math.pi)))


def full(shape):
    return pl.BlockSpec(shape, lambda *_: (0,) * len(shape))


MOST = 5


STRIP = 16
HALF = BLK // 2


def pre_kernel(share, seg_ref, bqkv_ref, bup_ref, g1_ref, s1_ref, g2_ref, s2_ref, x, dy, wqkv, wup, wdown, wout,
               first_o, second_o, dy_o, gp_o, gu_o, act_o, att_o, h_o, col_ref, vec_ref,
               xv, dyv, first, second, act, gu, gp, att, qt, kt, vt, gat, kf, vf, dkt, dvt, wqt, wu, wd, wo, hst, start, end, cosr, sinr, bq, moments, vec8, bias, ex, low, gprob, bounds,
               x_sem, dy_sem, w_sem, t_sem, h_sem, o_sem):
    tokens, width = xv.shape
    units, heads3 = act.shape[1], gp.shape[1]
    heads = att.shape[1]
    count = heads // HD
    blocks = tokens // BLK

    def block(i, n=1):
        return pl.ds(pl.multiple_of(i * BLK, BLK), n * BLK)

    def x_copy(i):
        return pltpu.make_async_copy(x.at[block(i)], xv.at[block(i)], x_sem.at[i])

    def dy_copy(i):
        return pltpu.make_async_copy(dy.at[block(i)], dyv.at[block(i)], dy_sem.at[i])

    raw = gp.at[pl.ds(0, width)]
    w_copies = [pltpu.make_async_copy(a, b, w_sem.at[n]) for n, (a, b) in enumerate(((wqkv, raw), (wout, wo), (wup, wu), (wdown, wd)))]
    w_copies[0].start()
    x_copy(0).start()
    dy_copy(0).start()
    for c in w_copies[1:]:
        c.start()
    x_copy(1).start()
    dy_copy(1).start()

    seg = seg_ref[...]
    edges = [jnp.sum((seg < d).astype(jnp.int32)) for d in range(1, DOCS)]
    bounds[0] = 0
    bounds[DOCS] = tokens
    begin, finish = jnp.zeros_like(seg), jnp.full_like(seg, tokens)
    for d in range(1, DOCS):
        bounds[d] = edges[d - 1]
        begin = jnp.where(seg >= d, edges[d - 1], begin)
    for d in range(DOCS - 1, 0, -1):
        finish = jnp.where(seg < d, edges[d - 1], finish)
    start[...] = begin
    end[...] = finish
    half = ROT // 2
    at_token = lax.broadcasted_iota(jnp.int32, (half, tokens), 1)
    freq = jnp.exp(lax.broadcasted_iota(jnp.int32, (half, tokens), 0).astype(F32) * (2.0 / ROT) * -math.log(10000.0))
    angle = (at_token - begin).astype(F32) * freq
    cosr[...] = jnp.cos(angle)
    sinr[...] = jnp.sin(angle)
    bqkv, bup, g1, s1, g2, s2 = (r[...].astype(F32).reshape(1, -1) for r in (bqkv_ref, bup_ref, g1_ref, s1_ref, g2_ref, s2_ref))
    bq[...] = jnp.broadcast_to(bqkv, (8, heads3)).T
    w_copies[0].wait()
    wqt[...] = raw[...].T

    def t_copies(i):
        return [pltpu.make_async_copy(low.at[n, pl.ds(0, width)], out.at[:, block(i)], t_sem.at[n]) for n, out in enumerate((first_o, second_o, dy_o))]

    def out_copy(n, src, out, i):
        return pltpu.make_async_copy(src.at[block(i)], out.at[block(i)], o_sem.at[n, i])

    outs = ((act, act_o), (gu, gu_o), (att, att_o), (gp, gp_o))

    def turn(v, c, s):
        a, b = v[:half], v[half:ROT]
        return jnp.concatenate([a * c - b * s, b * c + a * s, v[ROT:]], axis=0)

    def norm_block(i):
        for q in range(0, BLK, STRIP):
            at = pl.ds(pl.multiple_of(i * BLK + q, STRIP), STRIP)
            xs = xv[at, :].astype(F32)
            normed, inv = stats_of(xs)
            moments[at, 0:1] = jnp.mean(xs, axis=-1, keepdims=True)
            moments[at, 1:2] = inv
            first[at, :] = (normed * g1 + s1).astype(BF16)
            second[at, :] = (normed * g2 + s2).astype(BF16)

    x_copy(0).wait()
    norm_block(0)
    for c in w_copies[1:]:
        c.wait()

    @pl.loop(0, blocks)
    def _(i):
        at = block(i)
        dy_copy(i).wait()

        @pl.when(i + 1 < blocks)
        def _():
            x_copy(i + 1).wait()

        @pl.when(i + 2 < blocks)
        def _():
            x_copy(i + 2).start()
            dy_copy(i + 2).start()

        chunk = min(256, units)

        def ups(c):
            return dot_nn(second[at, :], wu[:, c:c + chunk]), dot_nt(dyv[at, :], wd[c:c + chunk, :])

        def gelu(c, made):
            for q in range(0, BLK, STRIP):
                strip = pl.ds(pl.multiple_of(i * BLK + q, STRIP), STRIP)
                value, slope = gelu_parts(made[0][q:q + STRIP] + bup[:, c:c + chunk])
                act[strip, c:c + chunk] = value.astype(BF16)
                gu[strip, c:c + chunk] = (made[1][q:q + STRIP] * slope).astype(BF16)

        pt = dot_nt(wqt[...], first[at, :])
        made = ups(0)
        for c in range(chunk, units, chunk):
            later = ups(c)
            gelu(c - chunk, made)
            made = later
        gat[:, at] = dot_nt(wo[...], dyv[at, :]).astype(BF16)
        gelu(units - chunk, made)

        @pl.when(i >= 1)
        def _():
            for copy in t_copies(i - 1):
                copy.wait()

        for n, rows_in in enumerate((first, second, dyv)):
            low[n, :width] = rows_in[at, :].T
        c, s = cosr[:, at], sinr[:, at]
        ks, vs = [], []
        for h in range(count):
            o = h * 3 * HD
            part = [pt[o + n * HD:o + (n + 1) * HD] + bq[o + n * HD:o + (n + 1) * HD, :1] for n in range(3)]
            qt[h * HD:(h + 1) * HD, at] = (turn(part[0], c, s).astype(BF16).astype(F32) * (1.0 / math.sqrt(HD))).astype(BF16)
            ks.append(turn(part[1], c, s).astype(BF16))
            vs.append(part[2].astype(BF16))
            kt[h * HD:(h + 1) * HD, at] = ks[h]
            vt[h * HD:(h + 1) * HD, at] = vs[h]
        kb, vb = jnp.concatenate(ks, axis=0), jnp.concatenate(vs, axis=0)
        kf[at, :] = kb.T
        vf[at, :] = vb.T
        for copy in (*t_copies(i), out_copy(0, act, act_o, i), out_copy(1, gu, gu_o, i)):
            copy.start()
        pl.when(i + 1 < blocks)(lambda: norm_block(i + 1))

    for copy in t_copies(blocks - 1):
        copy.wait()

    dkt[...] = jnp.zeros_like(dkt)
    dvt[...] = jnp.zeros_like(dvt)

    def low_block(i):
        lowest = 0
        for d in range(1, DOCS):
            lowest = jnp.maximum(lowest, jnp.where(bounds[d] <= i * BLK, bounds[d], 0))
        return lax.div(lowest, BLK)

    def end_of(j):
        last = j * BLK + BLK - 1
        highest = tokens
        for d in range(1, DOCS):
            highest = jnp.minimum(highest, jnp.where(bounds[d] > last, bounds[d], tokens))
        return highest

    def attend(i, lo, n):
        at, keys, size = block(i), block(lo, n), n * BLK
        strips = [slice(r, r + STRIP) for r in range(0, size, STRIP)]
        k_off = lax.broadcasted_iota(jnp.int32, (STRIP, BLK), 0)
        last = i * BLK - lo * BLK + lax.broadcasted_iota(jnp.int32, (1, BLK), 1)
        lead = start[:, at] - lo * BLK
        for r in strips:
            k_at = k_off + r.start
            bias[r] = jnp.where((k_at <= last) & (k_at >= lead), 0.0, NEG)
        blank = jnp.zeros((HD, BLK), BF16)
        span = min(2 * HD, heads)

        def spread(v, h):
            return jnp.concatenate([v if g == h % (span // HD) else blank for g in range(span // HD)], axis=0)

        def lanes(h):
            return slice(h * HD // span * span, h * HD // span * span + span)

        def rows_of(h):
            return slice(h * HD, (h + 1) * HD)

        atts, dqs, share_of = {}, {}, {}

        def stage_a(h):
            ex[h, :size] = dot_nn(kf[keys, lanes(h)], spread(qt[rows_of(h), at], h))

        def stage_b(h):
            best = jnp.full((STRIP, BLK), NEG, F32)
            for r in strips:
                s = ex[h, r] + bias[r]
                ex[h, r] = s
                best = jnp.maximum(best, s)
            best = jnp.max(best, axis=0, keepdims=True)
            total = jnp.zeros((STRIP, BLK), F32)
            for r in strips:
                e = jnp.exp(ex[h, r] - best)
                ex[h, r] = e
                total = total + e
            share_of[h] = 1.0 / jnp.sum(total, axis=0, keepdims=True)
            for r in strips:
                low[h, r] = (ex[h, r] * share_of[h]).astype(BF16)

        def stage_c(h):
            atts[h] = dot_nn(vt[rows_of(h), keys], low[h, :size])
            gprob[h % 2, :size] = dot_nn(vf[keys, lanes(h)], spread(gat[rows_of(h), at], h))
            dvt[rows_of(h), keys] += dot_nt(gat[rows_of(h), at], low[h, :size])

        def stage_d(h):
            delta = jnp.sum(atts[h] * gat[rows_of(h), at].astype(F32), axis=0, keepdims=True)
            for r in strips:
                low[h, r] = (ex[h, r] * share_of[h] * (gprob[h % 2, r] - delta)).astype(BF16)

        def stage_e(h):
            dqs[h] = dot_nn(kt[rows_of(h), keys], low[h, :size])
            dkt[rows_of(h), keys] += dot_nt(qt[rows_of(h), at], low[h, :size])

        stages = (stage_a, stage_b, stage_c, stage_d, stage_e)
        for t in range(count + len(stages) - 1):
            for k, stage in enumerate(stages):
                if 0 <= t - k < count:
                    stage(t - k)
        att[at, :] = jnp.concatenate([atts[h] for h in range(count)], axis=0).T.astype(BF16)
        c, sn = cosr[:, at], -sinr[:, at]
        qt[:, at] = jnp.concatenate([turn(dqs[h] * (1.0 / math.sqrt(HD)), c, sn) for h in range(count)], axis=0).astype(BF16)

    @pl.loop(0, blocks)
    def _(i):
        lo = low_block(i)
        for n in range(1, MOST + 1):
            pl.when(i - lo + 1 == n)(functools.partial(attend, i, lo, n))
        out_copy(2, att, att_o, i).start()

    vec8[...] = jnp.zeros_like(vec8)
    chunk = min(256, width)

    def spare(what, c, strip):
        k = c // chunk * 3 + what
        return ex.at[k % count, pl.ds(k // count * BLK + strip.start, strip.stop - strip.start)]

    def h_copy(i):
        slot = lax.rem(i, 2)
        return pltpu.make_async_copy(hst.at[slot], h_o.at[block(i)], h_sem.at[slot])

    def doc_of(t):
        return sum(jnp.where(bounds[d] <= t, 1, 0) for d in range(1, DOCS))

    @pl.loop(0, blocks)
    def _(i):
        at = block(i)
        c, sn = cosr[:, at], -sinr[:, at]
        pieces = []
        for h in range(count):
            r = slice(h * HD, (h + 1) * HD)
            pieces += [qt[r, at], turn(dkt[r, at], c, sn).astype(BF16), dvt[r, at].astype(BF16)]
        gp[at, :] = jnp.concatenate(pieces, axis=0).T
        out_copy(3, gp, gp_o, i).start()

        @pl.when(i >= 2)
        def _():
            h_copy(i - 2).wait()

        slot = lax.rem(i, 2)

        def grads(c):
            return dot_nt(gu[at, :], wu[c:c + chunk, :]), dot_nn(gp[at, :], wqt[:, c:c + chunk])

        def use(c, made):
            cut = slice(c, c + chunk)
            for q in range(0, BLK, STRIP):
                strip = slice(q, q + STRIP)
                gs, gf = made[0][strip], made[1][strip]
                spare(0, c, strip)[...] = gf
                spare(1, c, strip)[...] = gs
                hst[slot, strip, cut] = (gf * g1[:, cut] + gs * g2[:, cut]).astype(BF16)

        made = grads(0)
        for q in range(0, BLK, STRIP):
            here = pl.ds(pl.multiple_of(i * BLK + q, STRIP), STRIP)
            normed = (xv[here, :].astype(F32) - moments[here, 0:1]) * moments[here, 1:2]
            for c in range(0, width, chunk):
                spare(2, c, slice(q, q + STRIP))[...] = normed[:, c:c + chunk]
        for c in range(chunk, width, chunk):
            later = grads(c)
            use(c - chunk, made)
            made = later
        use(width - chunk, made)
        h_copy(i).start()
        at_row = lax.broadcasted_iota(jnp.int32, (STRIP, chunk), 0)

        @pl.loop(doc_of(i * BLK), doc_of(i * BLK + BLK - 1) + 1)
        def _(d):
            low_row, high_row = bounds[d] - i * BLK, bounds[d + 1] - i * BLK
            for c in range(0, width, chunk):
                sums = [jnp.zeros((STRIP, chunk), F32)] * 4
                for q in range(0, BLK, STRIP):
                    strip = slice(q, q + STRIP)
                    inside = (at_row >= low_row - q) & (at_row < high_row - q)
                    gf, gs = (jnp.where(inside, spare(k, c, strip)[...], 0.0) for k in range(2))
                    normed = spare(2, c, strip)[...]
                    sums = [s + v for s, v in zip(sums, (gf * normed, gf, gs * normed, gs))]
                for n in range(4):
                    vec8[n, d, :, c:c + chunk] += sums[n][:8] + sums[n][8:]

    vec_ref[...] = jnp.sum(vec8[...], axis=2)

    pairs_of = ((first, gp, 1.0), (second, gu, 1.0))

    def gram_block(j, first_row, size):
        at, cols = pl.ds(pl.multiple_of(first_row, HALF), size), block(j)

        def gram(m):
            return dot_nt(m[at, :], m[cols, :])

        grams = [(gram(a), plus, gram(b)) for a, b, plus in pairs_of] + [(gram(att) + gram(act), share, gram(dyv))]
        ahead = lax.broadcasted_iota(jnp.int32, (STRIP, BLK), 0) - lax.broadcasted_iota(jnp.int32, (STRIP, BLK), 1)
        reach = end[:, cols] - first_row
        row_off = lax.broadcasted_iota(jnp.int32, (STRIP, BLK), 0)
        total = jnp.zeros((STRIP, BLK), F32)
        for r in range(0, size, STRIP):
            terms = None
            for a, plus, b in grams:
                term = (a[r:r + STRIP] + plus) * b[r:r + STRIP]
                terms = term if terms is None else terms + term
            gap = ahead + (first_row - j * BLK + r)
            weight = jnp.where(gap > 0, 2.0, jnp.where(gap == 0, 1.0, 0.0))
            total = total + jnp.where(row_off + r < reach, terms * weight, 0.0)
        col_ref[:, cols] += total[:8] + total[8:]

    col_ref[...] = jnp.zeros_like(col_ref)

    @pl.loop(0, blocks)
    def _(j):
        total = lax.div(end_of(j) - j * BLK + HALF - 1, HALF)
        pl.loop(0, lax.div(total, 4))(lambda s: gram_block(j, j * BLK + s * 4 * HALF, 4 * HALF))
        for n in range(1, 4):
            pl.when(lax.rem(total, 4) == n)(lambda n=n: gram_block(j, j * BLK + (total - n) * HALF, n * HALF))

    for i in (blocks - 2, blocks - 1):
        h_copy(i).wait()

    @pl.loop(0, blocks)
    def _(i):
        for n, (src, out) in enumerate(outs):
            out_copy(n, src, out, i).wait()


def pre(share, seg, params, x, dy, wqkv, wup, wdown, wout):
    tokens, width = x.shape
    heads3, units, heads = wqkv.shape[1], wup.shape[1], wout.shape[0]
    blocks = tokens // BLK
    hbm, vmem = pl.BlockSpec(memory_space=pl.ANY), pl.BlockSpec(memory_space=pltpu.VMEM)
    V, D = pltpu.VMEM, pltpu.SemaphoreType.DMA
    t_shape, S = (width, tokens), jax.ShapeDtypeStruct
    return pl.pallas_call(
        functools.partial(pre_kernel, share),
        in_specs=[vmem] * 7 + [hbm] * 6,
        out_specs=[hbm] * 8 + [vmem] * 2,
        out_shape=[S(t_shape, BF16)] * 3 + [S((tokens, n), BF16) for n in (heads3, units, units, heads, width)] + [S((8, tokens), F32), S((4, DOCS, width), F32)],
        scratch_shapes=[V((tokens, width), BF16)] * 4 + [V((tokens, units), BF16)] * 2 + [V((tokens, heads3), BF16), V((tokens, heads), BF16)]
        + [V((heads, tokens), BF16)] * 4 + [V((tokens, heads), BF16)] * 2 + [V((heads, tokens), F32)] * 2
        + [V((heads3, width), BF16), V((width, units), BF16), V((units, width), BF16), V((heads, width), BF16), V((2, BLK, width), BF16)]
        + [V((1, tokens), jnp.int32)] * 2 + [V((ROT // 2, tokens), F32)] * 2 + [V((heads3, 8), F32), V((tokens, 2), F32), V((4, DOCS, 8, width), F32)]
        + [V((MOST * BLK, BLK), F32), V((heads // HD, max(MOST, -(-3 * width // BLK // (heads // HD))) * BLK, BLK), F32), V((max(heads // HD, 3), MOST * BLK, BLK), BF16), V((2, MOST * BLK, BLK), F32)]
        + [pltpu.SMEM((DOCS + 1,), jnp.int32)]
        + [D((blocks,)), D((blocks,)), D((4,)), D((3,)), D((2,)), D((4, blocks))],
        compiler_params=pltpu.CompilerParams(vmem_limit_bytes=63 * 1024 * 1024),
        name="pre",
    )(seg, *params, x, dy, wqkv, wup, wdown, wout)


LOAD_AHEAD = 4
LAG = 3


def bit_of(index, bit):
    return lax.rem(lax.div(index, 2**bit), 2)


def across(index, bit):
    return index + (1 - 2 * bit_of(index, bit)) * 2**bit


def log2(n):
    return n.bit_length() - 1


def remote(src, dst, send, recv, axis, index):
    return pltpu.make_async_remote_copy(src_ref=src, dst_ref=dst, send_sem=send, recv_sem=recv, device_id={axis: index}, device_id_type=pl.DeviceIdType.MESH)


def tail_kernel(n, tp, w, vec_ref, col_ref, seg_ref, b1_ref, b2_ref, second_t, first_t, dy_t, gu, gp, act, att, h, x, dy, wdown, wout,
                gup_ref, gq_ref, gdown_ref, gout_ref, bo_ref, gi_ref, small_ref, norm_ref,
                at, b, snd, rcv, keep, oacc, hown, hs, hr, bs, br, wd, xr, dyr, trow, tcol, vsend, vrecv, bsum, smine, sall,
                at_sem, b_sem, w_sem, snd_sem, rcv_sem, hs_sem, hr_sem, bs_sem, br_sem, gs_sem, gr_sem, ss_sem, sr_sem, hown_sem, row_sem, gi_stage, bo_stage, out_sem):
    width, tokens = first_t.shape
    me, m = lax.axis_index("dp"), lax.axis_index("mp")
    nb, mb = log2(n), log2(tp)
    shard, rows_own = width // n, tokens // tp
    nu, nq, na, ne = (r.shape[1] // w for r in (gu, gp, act, att))
    units = nu + nq + na + ne

    sources = (second_t, first_t, dy_t)

    def place(p):
        return sum(((p >> (nb - 1 - k)) & 1) << k for k in range(nb))

    def load_at(mat):
        for p in range(n):
            pltpu.make_async_copy(sources[mat].at[pl.ds(place(p) * shard, shard)], at.at[mat, pl.ds(p * shard, shard)], at_sem.at[mat]).start()

    def load_b(base, src):
        for i in range(src.shape[1] // w):
            pltpu.make_async_copy(src.at[:, pl.ds(i * w, w)], b.at[base + i], b_sem.at[base + i]).start()

    load_at(0)
    load_b(0, gu)
    def vec_exchange(k):
        return remote(vsend.at[k], vrecv.at[k], gs_sem.at[k], gr_sem.at[k], "mp", across(m, k))

    hot = seg_ref[...] == lax.broadcasted_iota(jnp.int32, (DOCS, tokens), 0)
    mine = jnp.sum(jnp.where(hot, jnp.sum(col_ref[...], axis=0, keepdims=True), 0.0), axis=1, keepdims=True)
    vsend[0, :4] = vec_ref[...]
    vsend[0, 4] = jnp.broadcast_to(mine, (DOCS, width))

    barrier = pltpu.get_barrier_semaphore()
    for r in range(1, n):
        pl.semaphore_signal(barrier, inc=1, device_id={"dp": lax.rem(me + r, n)}, device_id_type=pl.DeviceIdType.MESH)
    for r in range(1, tp):
        pl.semaphore_signal(barrier, inc=1, device_id={"mp": lax.rem(m + r, tp)}, device_id_type=pl.DeviceIdType.MESH)
    pl.semaphore_wait(barrier, n - 1 + tp - 1)

    vec_exchange(0).start()

    split = act.shape[1]
    wd_copies = (pltpu.make_async_copy(wdown, wd.at[pl.ds(0, split)], w_sem.at[0]), pltpu.make_async_copy(wout, wd.at[pl.ds(split, wd.shape[0] - split)], w_sem.at[1]))
    own_at = pl.ds(m * rows_own, rows_own)
    row_copies = (pltpu.make_async_copy(x.at[own_at], xr, row_sem.at[0]), pltpu.make_async_copy(dy.at[own_at], dyr, row_sem.at[1]))
    hown_copies = [pltpu.make_async_copy(h.at[pl.ds((2 * j + bit_of(m, 0)) * rows_own, rows_own)], hown.at[j], hown_sem.at[j]) for j in range(tp // 2)]

    for k in range(mb):
        vec_exchange(k).wait_recv()
        vsend[k + 1] = vsend[k] + vrecv[k]
        if k + 1 < mb:
            vec_exchange(k + 1).start()
        if k == 0:
            load_at(1)
            load_b(nu, gp)
    load_at(2)
    load_b(nu + nq, act)
    load_b(nu + nq + na, att)
    for c in (*wd_copies, *row_copies, *hown_copies):
        c.start()

    for j in range(tp // 2):
        there = 2 * j + 1 - bit_of(m, 0)
        remote(h.at[pl.ds(there * rows_own, rows_own)], hr[0].at[j], hs_sem.at[0, j], hr_sem.at[0, j], "mp", across(m, 0)).start()

    squares = vsend[mb, 4, :, :1]
    for j in range(4):
        squares = squares + jnp.sum(vsend[mb, j] * vsend[mb, j], axis=1, keepdims=True)
    norm = jnp.sqrt(squares + NORM_EPS)
    norm_ref[...] = jnp.broadcast_to(norm, norm_ref.shape)
    clip = jnp.minimum(1.0, jnp.mean(norm, axis=0, keepdims=True) / norm)
    per_token = jnp.sum(jnp.where(hot, clip, 0.0), axis=0, keepdims=True)
    trow[...] = per_token
    tcol[...] = jnp.broadcast_to(per_token, (DOCS, tokens)).T
    smine[...] = jnp.zeros_like(smine)
    for j in range(4):
        smine[3 + j:4 + j, :] = jnp.sum(vsend[mb, j] * clip, axis=0, keepdims=True)

    orders = (tuple(range(nb)), tuple(range(1, nb)) + (0,))

    def z_first(u):
        return (u == 1) | (u == units - 3)

    def by_order(u, body):
        pl.when(jnp.logical_not(z_first(u)))(functools.partial(body, orders[0]))
        pl.when(z_first(u))(functools.partial(body, orders[1]))

    def matrix_of(u):
        return jnp.where(u >= nu, 1, 0) + jnp.where(u >= nu + nq, 1, 0)

    def exchange(order, k, u):
        return remote(snd[k].at[u], rcv[k].at[u], snd_sem.at[k, u], rcv_sem.at[k, u], "dp", across(me, order[k]))

    def pieces(bit, side):
        size = width >> (bit + 1)
        return [pl.ds(pl.multiple_of((2 * g + side) * size, size), size) for g in range(2**bit)], size

    def other_half(mat, clipped, u):
        pltpu.make_async_copy(gu.at[:, pl.ds(0, w)], b.at[u], b_sem.at[u]).wait()
        if clipped:
            scaled = b[u].astype(F32) * tcol[:, :1]
            b[u] = scaled.astype(BF16)
            bsum[u] = jnp.sum(scaled.reshape(tokens // 8, 8, w), axis=0)

        def send(order):
            away, size = pieces(order[0], 1 - bit_of(me, order[0]))
            for g, piece in enumerate(away):
                snd[0][u, g * size:(g + 1) * size, :] = dot_nn(at[mat, piece, :], b[u]).astype(BF16)

            @pl.when(u < LOAD_AHEAD)
            def _():
                exchange(order, 0, u).start()

        by_order(u, send)

    def at_ready(mat):
        pltpu.make_async_copy(sources[mat], at.at[mat], at_sem.at[mat]).wait()

    at_ready(0)
    pl.loop(0, nu)(lambda u: other_half(0, True, u))
    at_ready(1)
    pl.loop(nu, nu + nq)(lambda u: other_half(1, True, u))
    at_ready(2)
    for p in range(n):
        piece = pl.ds(p * shard, shard)
        scaled = at[2, piece, :].astype(F32) * trow[...]
        at[2, piece, :] = scaled.astype(BF16)
        folded = scaled[:, :128]
        for k in range(1, tokens // 128):
            folded = folded + scaled[:, k * 128:(k + 1) * 128]
        smine[2:3, place(p) * shard:(place(p) + 1) * shard] = jnp.sum(folded.T, axis=0, keepdims=True)
    pl.loop(nu + nq, units)(lambda u: other_half(2, False, u))

    for i in range(nq):
        smine[0:1, i * w:(i + 1) * w] = jnp.sum(bsum[nu + i], axis=0, keepdims=True)
    for i in range(nu):
        smine[1:2, i * w:(i + 1) * w] = jnp.sum(bsum[i], axis=0, keepdims=True)
    sall[me] = smine[...]
    for r in range(1, n):
        remote(smine, sall.at[me], ss_sem.at[r - 1], sr_sem.at[me], "dp", lax.rem(me + r, n)).start()

    chunk = min(rows_own, 256)
    def branch(owner, c, chunk=chunk):
        at_rows = pl.ds(pl.multiple_of(owner * rows_own + c * chunk, chunk), chunk)
        left = jnp.concatenate([b[nu + nq + i, at_rows, :] for i in range(na + ne)], axis=1)
        return dot_nn(left, wd[...])

    def chunks(body):
        pl.loop(0, rows_own // chunk)(lambda c: body(c, pl.ds(pl.multiple_of(c * chunk, chunk), chunk)))

    def slot(owner, k):
        return lax.div(owner, 2 ** (k + 1))

    def wait_mp(k, buf, recv_sem, send_sem):
        for j in range(tp >> (k + 1)):
            remote(buf[k].at[j], buf[k].at[j], send_sem.at[k, j], recv_sem.at[k, j], "mp", across(m, k)).wait_recv()

    def owner_of(k, j):
        return (2 * j + 1 - bit_of(m, k)) * 2**k + lax.rem(m, 2**k)

    def h_task(k, j):
        if j == 0:
            if k == 1:
                for c in hown_copies:
                    c.wait()
            wait_mp(k - 1, hr, hr_sem, hs_sem)
        owner = owner_of(k, j)

        def h_send(c, rows_at):
            val = hown[slot(owner, 0), rows_at, :].astype(F32)
            for r in range(k):
                val = val + hr[r][slot(owner, r), rows_at, :].astype(F32)
            hs[k - 1][j, rows_at, :] = val.astype(BF16)

        chunks(h_send)
        remote(hs[k - 1].at[j], hr[k].at[j], hs_sem.at[k, j], hr_sem.at[k, j], "mp", across(m, k)).start()

    def b_task(k, j):
        if k == 0 and j == 0:
            for c in wd_copies:
                c.wait()
        if k > 0 and j == 0:
            wait_mp(k - 1, br, br_sem, bs_sem)
        owner = owner_of(k, j)

        def b_send(c, rows_at):
            val = branch(owner, c)
            for r in range(k):
                val = val + br[r][slot(owner, r), rows_at, :].astype(F32)
            bs[k][j, rows_at, :] = val.astype(BF16)

        chunks(b_send)
        remote(bs[k].at[j], br[k].at[j], bs_sem.at[k, j], br_sem.at[k, j], "mp", across(m, k)).start()

    tasks = [functools.partial(h_task, 1, j) for j in range(tp // 4)] + [functools.partial(b_task, 0, j) for j in range(tp // 2)]
    for k in range(1, mb):
        tasks += [functools.partial(h_task, k, j) for j in range(tp >> (k + 1)) if k > 1]
        tasks += [functools.partial(b_task, k, j) for j in range(tp >> (k + 1))]

    def split(val, pos, bit):
        size = val.shape[0] >> (pos + 1)
        low = [val[2 * g * size:(2 * g + 1) * size] for g in range(2**pos)]
        high = [val[(2 * g + 1) * size:(2 * g + 2) * size] for g in range(2**pos)]
        low, high = (v[0] if len(v) == 1 else jnp.concatenate(v, axis=0) for v in (low, high))
        return jnp.where(bit == 1, low, high), jnp.where(bit == 1, high, low)

    def later(k, u):
        def body(order):
            exchange(order, k, u).wait_recv()
            val = keep[k - 1][lax.rem(u, LAG + 1)] + rcv[k][u].astype(F32)
            if k == nb - 1:
                oacc[u] = val
                return
            pos = 1 if order[0] != 0 and k + 1 < nb - 1 else 0
            away, stay = split(val, pos, bit_of(me, order[k + 1]))
            snd[k + 1][u] = away.astype(BF16)
            keep[k][lax.rem(u, LAG + 1)] = stay
            exchange(order, k + 1, u).start()

        by_order(u, body)

    def first(u):
        mat = matrix_of(u)

        def body(order):
            exchange(order, 0, u).wait_recv()
            near, size = pieces(order[0], bit_of(me, order[0]))
            for g, piece in enumerate(near):
                val = dot_nn(at[mat, piece, :], b[u]) + rcv[0][u, g * size:(g + 1) * size, :].astype(F32)
                away, stay = split(val, 0, bit_of(me, order[1]))
                part = size // 2
                snd[1][u, g * part:(g + 1) * part, :] = away.astype(BF16)
                keep[0][lax.rem(u, LAG + 1), g * part:(g + 1) * part, :] = stay
            exchange(order, 1, u).start()

        by_order(u, body)

        @pl.when(u + LOAD_AHEAD < units)
        def _():
            by_order(u + LOAD_AHEAD, lambda order: exchange(order, 0, u + LOAD_AHEAD).start())

    def step(t):
        for k in range(nb - 1, 0, -1):
            pl.when((t >= k * LAG) & (t < units + k * LAG))(functools.partial(later, k, t - k * LAG))
        pl.when(t < units)(functools.partial(first, t))
        for spot, task in enumerate(tasks):
            pl.when(t == min(spot, units - 1))(task)

    pl.loop(0, units)(step)

    for c in row_copies:
        c.wait()
    wait_mp(mb - 1, hr, hr_sem, hs_sem)
    wait_mp(mb - 1, br, br_sem, bs_sem)

    fine = min(rows_own, 128)
    bias = (b1_ref[...].astype(F32) + b2_ref[...].astype(F32)).reshape(1, width)

    def out_copies(c):
        spot = lax.rem(c, 2)
        to = pl.ds(pl.multiple_of(c * fine, fine), fine)
        return (pltpu.make_async_copy(gi_stage.at[spot], gi_ref.at[to], out_sem.at[0, spot]),
                pltpu.make_async_copy(bo_stage.at[spot], bo_ref.at[to], out_sem.at[1, spot]))

    def finish(c):
        spot = lax.rem(c, 2)
        rows_at = pl.ds(pl.multiple_of(c * fine, fine), fine)

        @pl.when(c >= 2)
        def _():
            for copy in out_copies(c - 2):
                copy.wait()

        val = hown[slot(m, 0), rows_at, :].astype(F32)
        for r in range(mb):
            val = val + hr[r][slot(m, r), rows_at, :].astype(F32)
        xs = xr[rows_at, :].astype(F32)
        normed, inv = stats_of(xs)
        back_x = inv * (val - jnp.mean(val, axis=-1, keepdims=True) - normed * jnp.mean(val * normed, axis=-1, keepdims=True))
        gi_stage[spot] = dyr[rows_at, :].astype(F32) + back_x
        out = branch(m, c, fine) + (xs + bias)
        for r in range(mb):
            out = out + br[r][slot(m, r), rows_at, :].astype(F32)
        bo_stage[spot] = out.astype(BF16)
        for copy in out_copies(c):
            copy.start()

    pl.loop(0, rows_own // fine)(finish)
    pl.loop(units, units + (nb - 1) * LAG)(step)

    for i in range(nu):
        gup_ref[:, i * w:(i + 1) * w] = oacc[i]
    for i in range(nq):
        gq_ref[:, i * w:(i + 1) * w] = oacc[nu + i]
    for i in range(na):
        gdown_ref[i * w:(i + 1) * w, :] = oacc[nu + nq + i].T
    for i in range(ne):
        gout_ref[i * w:(i + 1) * w, :] = oacc[nu + nq + na + i].T
    for r in range(1, n):
        src = lax.rem(me + r, n)
        remote(smine, sall.at[src], ss_sem.at[r - 1], sr_sem.at[src], "dp", src).wait_recv()
    total = sall[0]
    for r in range(1, n):
        total = total + sall[r]
    small_ref[...] = total

    for c in range(max(rows_own // fine - 2, 0), rows_own // fine):
        for copy in out_copies(c):
            copy.wait()

    @pl.loop(0, units)
    def _(u):
        for k in range(nb):
            exchange(orders[0], k, u).wait_send()

    for r in range(1, n):
        remote(smine, sall.at[me], ss_sem.at[r - 1], sr_sem.at[me], "dp", lax.rem(me + r, n)).wait_send()
    for k in range(mb):
        vec_exchange(k).wait_send()
    for k in range(mb):
        for j in range(tp >> (k + 1)):
            src_h = h.at[pl.ds(0, rows_own)] if k == 0 else hs[k - 1].at[j]
            remote(src_h, hr[k].at[j], hs_sem.at[k, j], hr_sem.at[k, j], "mp", across(m, k)).wait_send()
            remote(bs[k].at[j], br[k].at[j], bs_sem.at[k, j], br_sem.at[k, j], "mp", across(m, k)).wait_send()


def tail(n, tp, vec, col, seg, b1, b2, second_t, first_t, dy_t, gu, gp, act, att, h, x, dy, wdown, wout):
    width, tokens = first_t.shape
    widths = [a.shape[1] for a in (gu, gp, act, att)]
    w = BLK if all(v % BLK == 0 for v in widths) else BLK // 2
    units = sum(widths) // w
    nb, mb = log2(n), log2(tp)
    shard, own = width // n, tokens // tp
    hbm = pl.BlockSpec(memory_space=pl.ANY)
    vmem = pl.BlockSpec(memory_space=pltpu.VMEM)
    V, D = pltpu.VMEM, pltpu.SemaphoreType.DMA
    mp_bufs = lambda lo: [V((tp >> (k + 1), own, width), BF16) for k in range(lo, mb)]
    step_bufs = lambda: [V((units, width >> (k + 1), w), BF16) for k in range(nb)]
    return pl.pallas_call(
        functools.partial(tail_kernel, n, tp, w),
        in_specs=[vmem] * 5 + [hbm] * 12,
        out_specs=[vmem] * 4 + [hbm] * 2 + [vmem] * 2,
        out_shape=[jax.ShapeDtypeStruct(s, t) for s, t in (
            ((shard, widths[0]), F32), ((shard, widths[1]), F32), ((widths[2], shard), F32), ((widths[3], shard), F32),
            ((own, width), BF16), ((own, width), F32), ((8, width), F32), ((DOCS, 128), F32))],
        scratch_shapes=[
            V((3, width, tokens), BF16), V((units, tokens, w), BF16), step_bufs(), step_bufs(), [V((LAG + 1, width >> (k + 1), w), F32) for k in range(1, nb)],
            V((units, shard, w), F32), V((tp // 2, own, width), BF16), mp_bufs(1), mp_bufs(0), mp_bufs(0), mp_bufs(0),
            V((wdown.shape[0] + wout.shape[0], width), BF16), V((own, width), BF16), V((own, width), BF16), V((1, tokens), F32), V((tokens, DOCS), F32),
            V((mb + 1, 5, DOCS, width), F32), V((mb, 5, DOCS, width), F32), V((units, 8, w), F32), V((8, width), F32), V((n, 8, width), F32),
            D((3,)), D((units,)), D((2,)), D((nb, units)), D((nb, units)), D((mb, tp // 2)), D((mb, tp // 2)), D((mb, tp // 2)), D((mb, tp // 2)),
            D((mb,)), D((mb,)), D((n - 1,)), D((n,)), D((tp // 2,)), D((2,)), V((2, min(own, 128), width), F32), V((2, min(own, 128), width), BF16), D((2, 2))],
        compiler_params=pltpu.CompilerParams(collective_id=1, has_side_effects=True, vmem_limit_bytes=64 * 1024 * 1024 - 1024 * 1024),
        name="tail",
    )(vec, col, seg, b1, b2, second_t, first_t, dy_t, gu, gp, act, att, h, x, dy, wdown, wout)


def finish_kernel(*refs):
    large, (small_ref, norm_ref) = refs[:6], refs[6:8]
    outs, (bq, bu, bo, bd, *norms), norm_out = refs[8:14], refs[14:22], refs[22]
    for src, dst in zip(large, outs):
        dst[...] = src[...]

    @pl.when(pl.program_id(0) == 0)
    def _():
        bq[...] = small_ref[0, :bq.shape[0]]
        bu[...] = small_ref[1, :bu.shape[0]]
        bo[...] = small_ref[2, :]
        bd[...] = small_ref[2, :]
        for k, ref in enumerate(norms):
            ref[...] = small_ref[3 + k, :]
        at = lax.broadcasted_iota(jnp.int32, (DOCS, 128), 0) == lax.broadcasted_iota(jnp.int32, (DOCS, 128), 1)
        norm_out[...] = jnp.sum(jnp.where(at, norm_ref[...], 0.0), axis=0, keepdims=True)[:, :DOCS]


def finish(steps, large, small, norms, heads3, units):
    width = small.shape[1]
    S = jax.ShapeDtypeStruct
    cut = lambda a: pl.BlockSpec((a.shape[0] // steps, a.shape[1]), lambda i: (i, 0))
    vectors = [heads3, units] + [width] * 6
    return pl.pallas_call(
        finish_kernel,
        grid=(steps,),
        in_specs=[cut(a) for a in large] + [full(small.shape), full(norms.shape)],
        out_specs=[cut(a) for a in large] + [full((v,)) for v in vectors] + [full((1, DOCS))],
        out_shape=[S(a.shape, a.dtype) for a in large] + [S((v,), F32) for v in vectors] + [S((1, DOCS), F32)],
        name="finish",
    )(*large, small, norms)


def shards(block_input, segment_ids, cotangent, weight_qkv, bias_qkv, weight_out, bias_out, weight_up, bias_up, weight_down, bias_down,
           gain_first, shift_first, gain_second, shift_second):
    tp = lax.axis_size("mp")
    x, dy = block_input[0], cotangent[0]
    params = (bias_qkv, bias_up, gain_first, shift_first, gain_second, shift_second)
    first_t, second_t, dy_t, gp, gu, act, att, h, col_sums, vec = pre(2.0 / tp, segment_ids, params, x, dy, weight_qkv, weight_up, weight_down, weight_out)
    g_up, g_qkv, g_down, g_out, block_output, grad_input, small, norms = tail(
        lax.axis_size("dp"), tp, vec, col_sums, segment_ids, bias_out, bias_down, second_t, first_t, dy_t, gu, gp, act, att, h, x, dy, weight_down, weight_out)
    g_up, g_qkv, g_down, g_out, block_output, grad_input, b_qkv, b_up, b_out, b_down, *norm_grads, norm_values = finish(
        2, (g_up, g_qkv, g_down, g_out, block_output, grad_input), small, norms, weight_qkv.shape[1], weight_up.shape[1])
    return (block_output[None], grad_input[None], g_qkv, b_qkv, g_out, b_out, g_up, b_up, g_down, b_down, *norm_grads, norm_values)


def solution(mesh):
    placed = (P("dp", None, None), P("dp", None), P("dp", None, None), P(None, "mp"), P("mp"), P("mp", None), P(), P(None, "mp"), P("mp"), P("mp", None),
              P(), P(), P(), P(), P())
    return jax.shard_map(
        shards,
        mesh=mesh,
        in_specs=placed,
        out_specs=(P("dp", "mp", None), P("dp", "mp", None), P("dp", "mp"), P("mp"), P("mp", "dp"), P(), P("dp", "mp"), P("mp"), P("mp", "dp"), P(), P(),
                   P(), P(), P(), P("dp", None)),
        check_vma=False,
    )
```
